32 devices in a mesh: dp: 16 (over z, x, core), head: 2 (over y).
Axes of the slice: x: 2, y: 2, z: 4, core: 2. Of those that a mesh axis runs over, the one named last changes fastest.
Arguments:
- hidden_in: bfloat16 [8192, 768], P('dp'), may hold values from -6 to 6
- lengths: int32 [16], P('dp'), may hold values from 256 to 512
- cotangent: bfloat16 [8192, 768], P('dp'), may hold values from -6 to 6
- w_query: bfloat16 [768, 768], P(None, 'head'), may hold values from -0.21875 to 0.21875
- b_query: bfloat16 [768], P('head'), may hold values from -2 to 2
- w_key: bfloat16 [768, 768], P(None, 'head'), may hold values from -0.21875 to 0.21875
- b_key: bfloat16 [768], P('head'), may hold values from -2 to 2
- w_value: bfloat16 [768, 768], P(None, 'head'), may hold values from -0.21875 to 0.21875
- b_value: bfloat16 [768], P('head'), may hold values from -2 to 2
- w_out: bfloat16 [768, 768], P('head'), may hold values from -2.5 to 2.5
- b_out: bfloat16 [768], replicated, may hold values from -2 to 2
- ln1_gain: bfloat16 [768], replicated, may hold values from 0.5 to 1.5
- ln1_bias: bfloat16 [768], replicated, may hold values from -2 to 2
- w_in: bfloat16 [768, 3072], P(None, 'head'), may hold values from -0.21875 to 0.21875
- b_in: bfloat16 [3072], P('head'), may hold values from -2 to 2
- w_down: bfloat16 [3072, 768], P('head'), may hold values from -0.109375 to 0.109375
- b_down: bfloat16 [768], replicated, may hold values from -2 to 2
- ln2_gain: bfloat16 [768], replicated, may hold values from 0.5 to 1.5
- ln2_bias: bfloat16 [768], replicated, may hold values from -2 to 2
- rel_table: bfloat16 [512, 768], replicated, may hold values from -6 to 6
Outputs:
- output: bfloat16 [8192, 768], P('dp')
- grad_input: bfloat16 [8192, 768], P('dp')
- grad_w_query: float32 [768, 768], P('dp', 'head')
- grad_b_query: float32 [768], P('head')
- grad_w_key: float32 [768, 768], P('dp', 'head')
- grad_b_key: float32 [768], P('head')
- grad_w_value: float32 [768, 768], P('dp', 'head')
- grad_b_value: float32 [768], P('head')
- grad_w_out: float32 [768, 768], P('head', 'dp')
- grad_b_out: float32 [768], replicated
- grad_ln1_gain: float32 [768], replicated
- grad_ln1_bias: float32 [768], replicated
- grad_w_in: float32 [768, 3072], P('dp', 'head')
- grad_b_in: float32 [3072], P('head')
- grad_w_down: float32 [3072, 768], P('head', 'dp')
- grad_b_down: float32 [768], replicated
- grad_ln2_gain: float32 [768], replicated
- grad_ln2_bias: float32 [768], replicated
- grad_rel_table: float32 [512, 768], replicated
The draws below stay inside these ranges and needn't reach their ends.
Inputs may be any that keep to these rules, and one draw needn't show every extreme that they name: The first lengths tokens of a row are real, the rest is padding.
All inputs are finite; a program needn't handle non-finite values.
Results may differ from the reference program's by a relative error of at most 0.024.
Values sent between devices are 32-bit elements; how exact they have to be, the bound alone decides.
No kernel may reach another device: no remote copies, remote signals or barrier semaphores. Data moves between devices by JAX's collectives and lax.ppermute only.
A program may use at most 192 MiB of HBM per device.

```python
import math
import jax
import jax.numpy as jnp
import numpy as np
from jax import lax

D = 768
HEADS = 12
HEAD_DIM = 64
FF = 3072
SPAN = 256
MAXPOS = 512
SEQ = 512
ROWS = 16
TOKENS = 8192


def with_ends(array, rng, low, largest):
    shape = array.shape
    spot = [jax.random.randint(jax.random.fold_in(rng, axis), (), 0, shape[axis]) for axis in range(len(shape))]
    array = array.at[tuple(spot)].set(low)
    longest = shape.index(max(shape))
    spot[longest] = (spot[longest] + 1) % shape[longest]
    return array.at[tuple(spot)].set(largest)


def block_scale(stream_key, extent, shards, low, top_value):
    def one(axis_at, shards_of):
        heights = jax.random.uniform(jax.random.fold_in(jax.random.fold_in(stream_key, 6), axis_at), (shards_of,), jnp.float32, low / len(shards), top_value / len(shards))
        return jnp.repeat(jnp.exp(heights), extent[axis_at] // shards_of).reshape((-1,) + (1,) * (len(extent) - axis_at - 1))

    loudness = one(*shards[0])
    for cut in shards[1:]:
        loudness = loudness * one(*cut)
    return loudness


def bell_draw(own_key, shape, deviation, limit, pieces=(), kind=jnp.bfloat16):
    array = jax.random.normal(own_key, shape, jnp.float32) * deviation
    if len(pieces) > 0:
        array = block_scale(own_key, shape, pieces, -0.22, 0.18) * array
    return jnp.clip(array, min=-limit, max=limit).astype(kind)


def setup_inputs(seed: int = 0) -> dict:
    seeds = jax.random.split(jax.random.key(seed), 21)
    hidden_in = bell_draw(seeds[0], (TOKENS, D), 1.0, 6.0, ((0, 16),))
    lengths = with_ends(jax.random.randint(seeds[1], (ROWS,), SEQ // 2, SEQ + 1), jax.random.fold_in(seeds[1], 1), SEQ // 2, SEQ).astype(jnp.int32)
    cotangent = bell_draw(seeds[2], (TOKENS, D), 1.0, 6.0, ((0, 16),))
    w_query = bell_draw(seeds[3], (D, D), D ** -0.5, 0.21875, ((1, 2),))
    b_query = bell_draw(seeds[4], (D,), 0.3, 2.0, ((0, 2),))
    w_key = bell_draw(seeds[5], (D, D), D ** -0.5, 0.21875, ((1, 2),))
    b_key = bell_draw(seeds[6], (D,), 0.3, 2.0, ((0, 2),))
    w_value = bell_draw(seeds[7], (D, D), D ** -0.5, 0.21875, ((1, 2),))
    b_value = bell_draw(seeds[8], (D,), 0.3, 2.0, ((0, 2),))
    w_out = bell_draw(seeds[9], (D, D), (max(1, 4 * D // SEQ)) ** -0.5, 2.5, ((0, 2),))
    b_out = bell_draw(seeds[10], (D,), 0.3, 2.0)
    ln1_gain = jnp.clip(1.0 + 0.1 * jax.random.normal(seeds[11], (D,), jnp.float32), 0.5, 1.5).astype(jnp.bfloat16)
    ln1_bias = bell_draw(seeds[12], (D,), 0.3, 2.0)
    w_in = bell_draw(seeds[13], (D, FF), D ** -0.5, 0.21875, ((1, 2),))
    b_in = bell_draw(seeds[14], (FF,), 0.3, 2.0, ((0, 2),))
    w_down = bell_draw(seeds[15], (FF, D), FF ** -0.5, 0.109375, ((0, 2),))
    b_down = bell_draw(seeds[16], (D,), 0.3, 2.0)
    ln2_gain = jnp.clip(1.0 + 0.1 * jax.random.normal(seeds[17], (D,), jnp.float32), 0.5, 1.5).astype(jnp.bfloat16)
    ln2_bias = bell_draw(seeds[18], (D,), 0.3, 2.0)
    rel_table = bell_draw(seeds[19], (2 * SPAN, D), 1.0, 6.0)
    return {"hidden_in": hidden_in, "lengths": lengths, "cotangent": cotangent, "w_query": w_query, "b_query": b_query, "w_key": w_key, "b_key": b_key, "w_value": w_value, "b_value": b_value, "w_out": w_out, "b_out": b_out, "ln1_gain": ln1_gain, "ln1_bias": ln1_bias, "w_in": w_in, "b_in": b_in, "w_down": w_down, "b_down": b_down, "ln2_gain": ln2_gain, "ln2_bias": ln2_bias, "rel_table": rel_table}


EPSILON = 1e-07
MASKED = -1000000000.0

@jax.custom_vjp
def low(v):
    return lax.optimization_barrier(v.astype(jnp.bfloat16)).astype(jnp.float32)

@jax.custom_vjp
def low_back(v):
    return v

def low_keep(v):
    return (low(v), None)

def low_pass(kept, grad):
    return (grad,)

def back_keep(v):
    return (v, None)

def back_low(kept, grad):
    return (low(grad),)
low.defvjp(low_keep, low_pass)
low_back.defvjp(back_keep, back_low)

def round_both(values):
    return low_back(low(values))

def bucket_table(length, bucket_span, max_distance):
    offsets = np.arange(length)[:, None] - np.arange(length)[None, :]
    middle = bucket_span // 2
    direction = np.sign(offsets)
    absolute = np.where((offsets < middle) & (offsets > -middle), middle - 1, np.abs(offsets))
    log_part = np.ceil(np.log(absolute / middle) / np.log((max_distance - 1) / middle) * (middle - 1)) + middle
    bucket = np.where(absolute <= middle, offsets, log_part * direction).astype(np.int64)
    return np.clip(bucket + bucket_span, 0, 2 * bucket_span - 1).astype(np.int32)

def layer_norm(values, norm_gain, norm_shift):
    center = values - lax.optimization_barrier(jnp.mean(values, axis=-1, keepdims=True))
    spread = lax.optimization_barrier(jnp.mean(center * center, axis=-1, keepdims=True))
    return center * lax.rsqrt(spread + EPSILON) * norm_gain + norm_shift

def reference(hidden_in, lengths, cotangent, w_query, b_query, w_key, b_key, w_value, b_value, w_out, b_out, ln1_gain, ln1_bias, w_in, b_in, w_down, b_down, ln2_gain, ln2_bias, rel_table):
    highest = lax.Precision.HIGHEST
    bucket_index = jnp.asarray(bucket_table(SEQ, SPAN, MAXPOS))
    pick_index = jnp.broadcast_to(bucket_index, (HEADS, SEQ, SEQ))
    score_scale = 1.0 / math.sqrt(3 * HEAD_DIM)
    params = tuple((member.astype(jnp.float32) for member in (w_query, b_query, w_key, b_key, w_value, b_value, w_out, b_out, ln1_gain, ln1_bias, w_in, b_in, w_down, b_down, ln2_gain, ln2_bias, rel_table)))

    def layer_forward(weights, hidden_rows):
        weight_query, bias_query, weight_key, bias_key, weight_value, bias_value, weight_out, bias_out, gain_one, shift_one, weight_in, bias_in, weight_down, bias_down, gain_two, shift_two, table_rows = weights
        rel_query = low(jnp.dot(table_rows, weight_query, precision=highest) + bias_query)
        rel_key = low(jnp.dot(table_rows, weight_key, precision=highest) + bias_key)
        relq_heads = rel_query.reshape(2 * SPAN, HEADS, HEAD_DIM)
        relk_heads = rel_key.reshape(2 * SPAN, HEADS, HEAD_DIM)

        def row_layer(carry_in, row_pair):
            row_in, row_length = row_pair
            query_rows = round_both(jnp.dot(row_in, weight_query, precision=highest) + bias_query).reshape(SEQ, HEADS, HEAD_DIM)
            key_rows = round_both(jnp.dot(row_in, weight_key, precision=highest) + bias_key).reshape(SEQ, HEADS, HEAD_DIM)
            value_rows = round_both(jnp.dot(row_in, weight_value, precision=highest) + bias_value).reshape(SEQ, HEADS, HEAD_DIM)
            content = jnp.einsum('ihd,jhd->hij', query_rows, key_rows, precision=highest)
            to_pos = low_back(jnp.einsum('ihd,rhd->hir', query_rows, relk_heads, precision=highest))
            from_pos = low_back(jnp.einsum('jhd,rhd->hjr', key_rows, relq_heads, precision=highest))
            picked = jnp.take_along_axis(to_pos, pick_index, axis=2)
            flipped = jnp.swapaxes(jnp.take_along_axis(from_pos, pick_index, axis=2), 1, 2)
            scores = low_back(score_scale * (content + picked + flipped))
            positions = jnp.arange(SEQ)
            key_valid = positions < row_length
            scores = jnp.where(key_valid[None, None, :], scores, MASKED)
            attend = low(jax.nn.softmax(scores, axis=-1) * key_valid.astype(jnp.float32)[None, :, None])
            context = round_both(jnp.einsum('hij,jhd->ihd', attend, value_rows, precision=highest)).reshape(SEQ, D)
            attn_mixed = low_back(jnp.dot(context, weight_out, precision=highest))
            normed_one = layer_norm(attn_mixed + bias_out + row_in, gain_one, shift_one)
            inner_pre = low_back(jnp.dot(low(normed_one), weight_in, precision=highest) + bias_in)
            activated = low(jax.nn.gelu(inner_pre, approximate=False))
            lowered = low_back(jnp.dot(activated, weight_down, precision=highest))
            output_row = layer_norm(lowered + bias_down + normed_one, gain_two, shift_two)
            return (carry_in, output_row)
        start = jnp.zeros((), jnp.float32)
        carry_out, rows_out = lax.scan(jax.checkpoint(row_layer), start, (hidden_rows.reshape(ROWS, SEQ, D), lengths))
        return rows_out.reshape(ROWS * SEQ, D)
    output, pullback = jax.vjp(layer_forward, params, hidden_in.astype(jnp.float32))
    grad_params, grad_hidden = pullback(cotangent.astype(jnp.float32))
    return (output.astype(jnp.bfloat16), grad_hidden.astype(jnp.bfloat16), grad_params[0], grad_params[1], grad_params[2], grad_params[3], grad_params[4], grad_params[5], grad_params[6], grad_params[7], grad_params[8], grad_params[9], grad_params[10], grad_params[11], grad_params[12], grad_params[13], grad_params[14], grad_params[15], grad_params[16])
```

```python
import functools
import math

import jax
import jax.numpy as jnp
import numpy as np
from jax import lax
from jax.experimental import pallas as pl
from jax.experimental.pallas import tpu as pltpu
from jax.sharding import PartitionSpec as P

HEAD_DIM = 64
SPAN = 256
MAXPOS = 512
EPSILON = 1e-07
MASKED = -1000000000.0
LANES = 128
STREAMS = 2
VMEM_LIMIT = 56 * 1024 * 1024

BF16 = jnp.bfloat16
F32 = jnp.float32


def bucket_of(offsets, bucket_span, max_distance):
    middle = bucket_span // 2
    direction = np.sign(offsets)
    absolute = np.where((offsets < middle) & (offsets > -middle), middle - 1, np.abs(offsets))
    log_part = (
        np.ceil(np.log(absolute / middle) / np.log((max_distance - 1) / middle) * (middle - 1))
        + middle
    )
    bucket = np.where(absolute <= middle, offsets, log_part * direction).astype(np.int64)
    return np.clip(bucket + bucket_span, 0, 2 * bucket_span - 1).astype(np.int32)


def distance_buckets(seq_len):
    offsets = np.maximum(seq_len - 1 - np.arange(2 * seq_len), 1 - seq_len)
    return bucket_of(offsets, SPAN, MAXPOS)


def dot_nn(a, b):
    return lax.dot_general(a, b, (((1,), (0,)), ((), ())), preferred_element_type=F32)


def dot_nt(a, b):
    return lax.dot_general(a, b, (((1,), (1,)), ((), ())), preferred_element_type=F32)


def dot_tn(a, b):
    return lax.dot_general(a, b, (((0,), (0,)), ((), ())), preferred_element_type=F32)


def params():
    return pltpu.CompilerParams(vmem_limit_bytes=VMEM_LIMIT)


def cost(flops, nbytes, transcendentals=0):
    return pl.CostEstimate(flops=flops, bytes_accessed=nbytes, transcendentals=transcendentals)


def full(array):
    rank = len(array.shape)
    return pl.BlockSpec(array.shape, lambda i: (0,) * rank)


def rows_of(array, height, at):
    rest = array.shape[1:]
    return pl.BlockSpec((height, *rest), lambda i: (at,) + (0,) * len(rest))


def smem():
    return pl.BlockSpec(memory_space=pltpu.SMEM)


def sds(shape, dtype):
    return jax.ShapeDtypeStruct(shape, dtype)


def project_kernel(
    bucket_ref, hidden_ref, table_ref, wq_ref, bq_ref, wk_ref, bk_ref, wv_ref, bv_ref,
    q_ref, k_ref, v_ref, eq_ref, ek_ref, onehot_ref,
):
    hidden = hidden_ref[...]
    table = table_ref[...]
    buckets = bucket_ref[...]
    span = table.shape[0]
    hot = buckets == lax.broadcasted_iota(jnp.int32, (buckets.shape[0], span), 1)
    onehot = jnp.where(hot, 1.0, 0.0).astype(BF16)
    onehot_ref[...] = onehot
    q_ref[...] = (dot_nn(hidden, wq_ref[...]) + bq_ref[...].astype(F32)).astype(BF16)
    k_ref[...] = (dot_nn(hidden, wk_ref[...]) + bk_ref[...].astype(F32)).astype(BF16)
    v_ref[...] = (dot_nn(hidden, wv_ref[...]) + bv_ref[...].astype(F32)).astype(BF16)
    rel_q = (dot_nn(table, wq_ref[...]) + bq_ref[...].astype(F32)).astype(BF16)
    rel_k = (dot_nn(table, wk_ref[...]) + bk_ref[...].astype(F32)).astype(BF16)
    eq_ref[...] = dot_nn(onehot, rel_q).astype(BF16)
    ek_ref[...] = dot_nn(onehot, rel_k).astype(BF16)


def project(hidden, table, wq, bq, wk, bk, wv, bv):
    seq_len = hidden.shape[0]
    cols = wq.shape[1]
    buckets = jnp.asarray(distance_buckets(seq_len)[:, None])
    outs = [sds((seq_len, cols), BF16)] * 3 + [sds((2 * seq_len, cols), BF16)] * 2
    outs = outs + [sds((2 * seq_len, table.shape[0]), BF16)]
    return pl.pallas_call(
        project_kernel,
        out_shape=outs,
        compiler_params=params(),
        cost_estimate=cost(3 << 30, 8 << 20),
        name="project",
    )(buckets, hidden, table, wq, bq, wk, bk, wv, bv)


def assemble_kernel(side_ref, odd_ref, own_ref, fetched_ref, paired_ref, out_ref):
    side, odd = side_ref[0], odd_ref[0]
    out_ref[side] = own_ref[...]
    half = fetched_ref.shape[0]
    out_ref[1 - side, pl.ds(pl.multiple_of(odd * half, half), half), :] = fetched_ref[...].astype(BF16)
    out_ref[1 - side, pl.ds(pl.multiple_of((1 - odd) * half, half), half), :] = paired_ref[...].astype(BF16)


def assemble(side, odd, own, fetched, paired):
    rows, width = own.shape
    out = sds((2, rows, width), BF16)
    return pl.pallas_call(
        assemble_kernel,
        grid=(1,),
        in_specs=[smem(), smem(), full(own), full(fetched), full(paired)],
        out_specs=full(out),
        out_shape=out,
        compiler_params=params(),
        cost_estimate=cost(0, 4 << 20),
        name="assemble",
    )(side, odd, own, fetched, paired).reshape(2 * rows, width)


def half_masks():
    lane = lax.broadcasted_iota(jnp.int32, (1, LANES), 1)
    return [lane // HEAD_DIM == side for side in range(LANES // HEAD_DIM)]


def attend_kernel(at, len_ref, q_ref, k_ref, v_ref, eq_ref, ek_ref, ctx_ref, att_ref):
    height = q_ref.shape[0]
    seq_len = k_ref.shape[0]
    length = len_ref[0]
    scale = 1.0 / math.sqrt(3 * HEAD_DIM)
    masks = half_masks()
    key_valid = lax.broadcasted_iota(jnp.int32, (1, seq_len), 1) < length
    rows = at * height + lax.broadcasted_iota(jnp.int32, (height, 1), 0)
    query_valid = rows < length
    row_start = seq_len - height - height * at
    for pair in range(q_ref.shape[1] // LANES):
        cols = slice(pair * LANES, (pair + 1) * LANES)
        q_pair = q_ref[:, cols]
        k_pair = k_ref[:, cols]
        v_pair = v_ref[:, cols]
        rel_window = ek_ref[row_start : row_start + seq_len + height, cols]
        outs = []
        for side, mask in enumerate(masks):
            q_one = jnp.where(mask, q_pair, jnp.zeros_like(q_pair))
            k_one = jnp.where(mask, k_pair, jnp.zeros_like(k_pair))
            content = dot_nt(q_one, k_pair)
            wide = dot_nt(q_one, rel_window)
            picked = pltpu.roll(wide, seq_len + 1, 1, stride=1, stride_axis=0)[:, :seq_len]
            blocks = []
            for block in range(seq_len // LANES):
                start = seq_len - LANES - LANES * block + height * at
                window = eq_ref[start : start + LANES + height, cols]
                tall = dot_nt(k_one[block * LANES : (block + 1) * LANES], window)
                tall = pltpu.roll(tall, height + 1, 1, stride=1, stride_axis=0)[:, :height]
                blocks.append(tall.T)
            flipped = jnp.concatenate(blocks, axis=1)
            scores = jnp.where(key_valid, scale * (content + picked + flipped), MASKED)
            peak = jnp.max(scores, axis=-1, keepdims=True)
            weight = jnp.exp(scores - peak)
            total = jnp.sum(weight, axis=-1, keepdims=True)
            keep = jnp.where(query_valid, 1.0 / total, 0.0)
            attend = (weight * keep).astype(BF16)
            att_ref[pair * len(masks) + side] = attend
            outs.append(dot_nn(attend, v_pair))
        ctx = jnp.where(masks[0], outs[0], outs[1])
        ctx_ref[:, cols] = ctx.astype(BF16).astype(F32)


def attend(at, height, lengths, q, k, v, eq, ek):
    seq_len, cols = q.shape
    heads = cols // HEAD_DIM
    return pl.pallas_call(
        functools.partial(attend_kernel, at),
        grid=(1,),
        in_specs=[smem(), rows_of(q, height, at)] + [full(a) for a in (k, v, eq, ek)],
        out_specs=[
            pl.BlockSpec((height, cols), lambda i: (0, 0)),
            pl.BlockSpec((heads, height, seq_len), lambda i: (0, 0, 0)),
        ],
        out_shape=[sds((height, cols), F32), sds((heads, height, seq_len), BF16)],
        compiler_params=params(),
        cost_estimate=cost(4 << 30, 8 << 20),
        name=f"attend_{at}",
    )(lengths, q, k, v, eq, ek)


def attend_back_kernel(
    at, first,
    dn_own_ref, dn_other_ref, d_two_ref, xhat_ref, rstd_ref, gain_ref, wout_ref,
    q_ref, k_ref, v_ref, eq_ref, ek_ref, att_ref,
    dk_in, dv_in, deq_in, dek_in,
    d_one_ref, d_mixed_ref, dq_ref, vec_ref, dk_ref, dv_ref, deq_ref, dek_ref,
):
    height = q_ref.shape[0]
    seq_len = k_ref.shape[0]
    scale = 1.0 / math.sqrt(3 * HEAD_DIM)
    masks = half_masks()
    d_normed = (dn_own_ref[...] + dn_other_ref[...]) + d_two_ref[...]
    xhat = xhat_ref[...]
    vec_ref[0:1, :] = jnp.sum(d_normed * xhat, axis=0, keepdims=True)
    vec_ref[1:2, :] = jnp.sum(d_normed, axis=0, keepdims=True)
    scaled = d_normed * gain_ref[...].astype(F32)
    mean_a = jnp.mean(scaled, axis=-1, keepdims=True)
    mean_b = jnp.mean(scaled * xhat, axis=-1, keepdims=True)
    d_one = rstd_ref[...] * (scaled - mean_a - xhat * mean_b)
    d_one_ref[...] = d_one
    vec_ref[2:3, :] = jnp.sum(d_one, axis=0, keepdims=True)
    d_mixed = d_one.astype(BF16)
    d_mixed_ref[...] = d_mixed
    d_ctx = dot_nt(d_mixed, wout_ref[...]).astype(BF16)

    def anti(size):
        row = lax.broadcasted_iota(jnp.int32, (size, size), 0)
        col = lax.broadcasted_iota(jnp.int32, (size, size), 1)
        return jnp.where(row + col == size - 1, 1.0, 0.0).astype(BF16)

    anti_rows = anti(height)
    anti_keys = anti(LANES)
    row_start = seq_len - height - height * at
    if first:
        dk_ref[...] = jnp.zeros_like(dk_ref)
        dv_ref[...] = jnp.zeros_like(dv_ref)
        deq_ref[...] = jnp.zeros_like(deq_ref)
        dek_ref[...] = jnp.zeros_like(dek_ref)
    else:
        dk_ref[...] = dk_in[...]
        dv_ref[...] = dv_in[...]
        deq_ref[...] = deq_in[...]
        dek_ref[...] = dek_in[...]
    for pair in range(q_ref.shape[1] // LANES):
        cols = slice(pair * LANES, (pair + 1) * LANES)
        q_pair = q_ref[:, cols]
        k_pair = k_ref[:, cols]
        v_pair = v_ref[:, cols]
        ctx_pair = d_ctx[:, cols]
        q_turned = dot_nn(anti_rows, q_pair).astype(BF16)
        k_turned = [
            dot_nn(anti_keys, k_pair[b * LANES : (b + 1) * LANES]).astype(BF16)
            for b in range(seq_len // LANES)
        ]
        rel_window = ek_ref[row_start : row_start + seq_len + height, cols]
        d_q, d_q_turned, d_k, d_v, d_rel_k, d_rel_q, d_k_turned = [], [], [], [], [], [], []
        for side, mask in enumerate(masks):
            weight = att_ref[pair * len(masks) + side]
            ctx_one = jnp.where(mask, ctx_pair, jnp.zeros_like(ctx_pair))
            d_att = dot_nt(ctx_one, v_pair)
            soft = weight.astype(F32)
            inner = jnp.sum(d_att * soft, axis=-1, keepdims=True)
            d_scores = (soft * (d_att - inner)).astype(BF16)
            d_v.append(dot_tn(weight, ctx_pair))
            d_q.append(dot_nn(d_scores, k_pair))
            d_scores_t = d_scores.T
            d_k.append(dot_nn(d_scores_t, q_pair))
            turned = dot_nn(anti_rows, d_scores)
            turned = jnp.concatenate([turned, jnp.zeros((height, height), F32)], axis=1)
            turned = pltpu.roll(turned, 0, 1, stride=1, stride_axis=0).astype(BF16)
            d_q_turned.append(dot_nn(turned, rel_window))
            d_rel_k.append(dot_tn(turned, q_turned))
            d_rel_q.append([])
            d_k_turned.append([])
            for block in range(seq_len // LANES):
                start = seq_len - LANES - LANES * block + height * at
                window = eq_ref[start : start + LANES + height, cols]
                tall = dot_nn(anti_keys, d_scores_t[block * LANES : (block + 1) * LANES])
                tall = jnp.concatenate([tall, jnp.zeros((LANES, LANES), F32)], axis=1)
                tall = pltpu.roll(tall, 0, 1, stride=1, stride_axis=0).astype(BF16)
                d_k_turned[-1].append(dot_nn(tall, window))
                d_rel_q[-1].append(dot_tn(tall, k_turned[block]))

        def join(two):
            return jnp.where(masks[0], two[0], two[1])

        def turn_back(matrix, value):
            high = value.astype(BF16)
            rest = (value - high.astype(F32)).astype(BF16)
            return dot_nn(matrix, high) + dot_nn(matrix, rest)

        dq_ref[:, cols] = (scale * (join(d_q) + turn_back(anti_rows, join(d_q_turned)))).astype(BF16)
        dv_ref[:, cols] += join(d_v)
        dk_ref[:, cols] += scale * join(d_k)
        dek_ref[row_start : row_start + seq_len + height, cols] += scale * join(d_rel_k)
        for block in range(seq_len // LANES):
            start = seq_len - LANES - LANES * block + height * at
            back = turn_back(anti_keys, join([d_k_turned[0][block], d_k_turned[1][block]]))
            dk_ref[block * LANES : (block + 1) * LANES, cols] += scale * back
            deq_ref[start : start + LANES + height, cols] += scale * join(
                [d_rel_q[0][block], d_rel_q[1][block]]
            )


def attend_back(
    at, height, dn_own, dn_other, d_two, xhat, rstd, gain, wout, q, k, v, eq, ek, att, carried
):
    seq_len, cols = q.shape
    width = d_two.shape[1]
    first = carried is None
    if first:
        carried = [jnp.zeros((8, LANES), F32)] * 4
    operands = [dn_own, dn_other, d_two, xhat, rstd, gain, wout, q, k, v, eq, ek, att, *carried]
    specs = [full(a) for a in (dn_own, dn_other, d_two, xhat, rstd)]
    specs = specs + [full(gain), full(wout), rows_of(q, height, at)]
    specs = specs + [full(a) for a in (k, v, eq, ek, att)] + [full(a) for a in carried]
    outs = [
        sds((height, width), F32),
        sds((height, width), BF16),
        sds((height, cols), BF16),
        sds((8, width), F32),
        sds((seq_len, cols), F32),
        sds((seq_len, cols), F32),
        sds((2 * seq_len, cols), F32),
        sds((2 * seq_len, cols), F32),
    ]
    return pl.pallas_call(
        functools.partial(attend_back_kernel, at, first),
        grid=(1,),
        in_specs=specs,
        out_specs=[full(o) for o in outs],
        out_shape=outs,
        input_output_aliases={} if first else {13: 4, 14: 5, 15: 6, 16: 7},
        compiler_params=params(),
        cost_estimate=cost(8 << 30, 16 << 20),
        name=f"attend_back_{at}",
    )(*operands)


def feed_kernel(
    ctx_a_ref, ctx_b_ref, wout_ref, bout_ref, hidden_ref, gain_ref, shift_ref,
    win_ref, bin_ref, wdown_ref,
    xhat_ref, rstd_ref, normed_ref, act_ref, slope_ref, low_ref,
):
    ctx = jnp.concatenate([ctx_a_ref[...], ctx_b_ref[...]], axis=1).astype(BF16)
    mixed = dot_nn(ctx, wout_ref[...])
    resid = mixed + bout_ref[...].astype(F32) + hidden_ref[...].astype(F32)
    center = resid - jnp.mean(resid, axis=-1, keepdims=True)
    spread = jnp.mean(center * center, axis=-1, keepdims=True)
    rstd = lax.rsqrt(spread + EPSILON)
    xhat = center * rstd
    xhat_ref[...] = xhat
    rstd_ref[...] = rstd
    normed = xhat * gain_ref[...].astype(F32) + shift_ref[...].astype(F32)
    low = normed.astype(BF16)
    normed_ref[...] = low
    units = win_ref.shape[1]
    step = units // 3
    total = None
    for part in range(3):
        cols = slice(part * step, (part + 1) * step)
        inner = dot_nn(low, win_ref[:, cols]) + bin_ref[:, cols].astype(F32)
        phi = 0.5 * (1.0 + lax.erf(inner * math.sqrt(0.5)))
        act = (inner * phi).astype(BF16)
        slope = phi + inner * (jnp.exp(-0.5 * inner * inner) * (1.0 / math.sqrt(2 * math.pi)))
        act_ref[:, cols] = act
        slope_ref[:, cols] = slope
        term = dot_nn(act, wdown_ref[cols, :])
        total = term if total is None else total + term
    low_ref[...] = total


def feed(at, height, ctx_a, ctx_b, wout, bout, hidden, gain, shift, win, b_in, wdown):
    width = hidden.shape[1]
    units = win.shape[1]
    outs = [
        sds((height, width), F32),
        sds((height, 1), F32),
        sds((height, width), BF16),
        sds((height, units), BF16),
        sds((height, units), F32),
        sds((height, width), F32),
    ]
    return pl.pallas_call(
        feed_kernel,
        grid=(1,),
        in_specs=[full(ctx_a), full(ctx_b), full(wout), full(bout), rows_of(hidden, height, at)]
        + [full(a) for a in (gain, shift, win, b_in, wdown)],
        out_specs=[full(o) for o in outs],
        out_shape=outs,
        compiler_params=params(),
        cost_estimate=cost(3 << 30, 12 << 20),
        name=f"feed_{at}",
    )(ctx_a, ctx_b, wout, bout, hidden, gain, shift, win, b_in, wdown)


def feed_back_kernel(
    low_own_ref, low_other_ref, xhat_one_ref, gain_one_ref, shift_one_ref, bdown_ref,
    gain_ref, shift_ref, cot_ref, slope_ref, win_ref, wdown_ref,
    out_ref, d_two_ref, d_low_ref, d_inner_ref, dn_ref, vec_ref, bin_ref,
):
    normed = xhat_one_ref[...] * gain_one_ref[...].astype(F32) + shift_one_ref[...].astype(F32)
    resid = (low_own_ref[...] + low_other_ref[...]) + bdown_ref[...].astype(F32) + normed
    center = resid - jnp.mean(resid, axis=-1, keepdims=True)
    spread = jnp.mean(center * center, axis=-1, keepdims=True)
    rstd = lax.rsqrt(spread + EPSILON)
    xhat = center * rstd
    gain = gain_ref[...].astype(F32)
    out_ref[...] = (xhat * gain + shift_ref[...].astype(F32)).astype(BF16)
    err = cot_ref[...].astype(F32)
    vec_ref[0:1, :] = jnp.sum(err * xhat, axis=0, keepdims=True)
    vec_ref[1:2, :] = jnp.sum(err, axis=0, keepdims=True)
    scaled = err * gain
    mean_a = jnp.mean(scaled, axis=-1, keepdims=True)
    mean_b = jnp.mean(scaled * xhat, axis=-1, keepdims=True)
    d_two = rstd * (scaled - mean_a - xhat * mean_b)
    d_two_ref[...] = d_two
    vec_ref[2:3, :] = jnp.sum(d_two, axis=0, keepdims=True)
    low = d_two.astype(BF16)
    d_low_ref[...] = low
    units = win_ref.shape[1]
    step = units // 3
    total = None
    for part in range(3):
        cols = slice(part * step, (part + 1) * step)
        d_act = dot_nt(low, wdown_ref[cols, :])
        d_inner = (d_act * slope_ref[:, cols]).astype(BF16)
        d_inner_ref[:, cols] = d_inner
        bin_ref[0:1, cols] = jnp.sum(d_inner.astype(F32), axis=0, keepdims=True)
        term = dot_nt(d_inner, win_ref[:, cols])
        total = term if total is None else total + term
    dn_ref[...] = total


def feed_back(
    at, height, low_own, low_other, xhat, gain_one, shift_one, bdown, gain, shift, cot, slope, win,
    wdown,
):
    width = cot.shape[1]
    units = win.shape[1]
    outs = [
        sds((height, width), BF16),
        sds((height, width), F32),
        sds((height, width), BF16),
        sds((height, units), BF16),
        sds((height, width), F32),
        sds((8, width), F32),
        sds((8, units), F32),
    ]
    before = [full(a) for a in (low_own, low_other, xhat, gain_one, shift_one, bdown, gain, shift)]
    return pl.pallas_call(
        feed_back_kernel,
        grid=(1,),
        in_specs=before + [rows_of(cot, height, at), full(slope), full(win), full(wdown)],
        out_specs=[full(o) for o in outs],
        out_shape=outs,
        compiler_params=params(),
        cost_estimate=cost(3 << 30, 12 << 20),
        name=f"feed_back_{at}",
    )(low_own, low_other, xhat, gain_one, shift_one, bdown, gain, shift, cot, slope, win, wdown)


def grad_kernel(parts, pieces, me_ref, *refs):
    out_ref = refs[-1]
    total = None
    for piece in range(pieces):
        left_ref, right_ref = refs[2 * piece], refs[2 * piece + 1]
        term = dot_tn(left_ref[...], right_ref[...])
        total = term if total is None else total + term
    height = total.shape[0] // parts
    me = me_ref[0]
    for block in range(parts):
        out_ref[me ^ block] = total[block * height : (block + 1) * height]


def grad_blocks(name, parts, me, terms, step):
    width = terms[0][0].shape[1]
    cols = terms[0][1].shape[1]
    specs = [smem()]
    operands = [me]
    for left, right in terms:
        specs.append(pl.BlockSpec(left.shape, lambda i: (0, 0)))
        specs.append(pl.BlockSpec((right.shape[0], step), lambda i: (0, i)))
        operands += [left, right]
    return pl.pallas_call(
        functools.partial(grad_kernel, parts, len(terms)),
        grid=(cols // step,),
        in_specs=specs,
        out_specs=pl.BlockSpec((parts, width // parts, step), lambda i: (0, 0, i)),
        out_shape=sds((parts, width // parts, cols), F32),
        compiler_params=params(),
        cost_estimate=cost(2 * width * cols * 512 * len(terms), 4 * width * cols),
        name=name,
    )(*operands)


def rel_kernel(
    parts, me_ref, onehot_ref, deq_ref, dek_ref, wq_ref, wk_ref, dq_ref, dk_ref, dv_ref,
    one_ref, two_ref, unit_ref, relq_ref, relk_ref, dk_low_ref, dv_low_ref, part_ref,
):
    onehot = onehot_ref[...]
    deq, dek = deq_ref[...], dek_ref[...]
    d_rel_q = dot_tn(onehot, deq.astype(BF16)).astype(BF16)
    d_rel_k = dot_tn(onehot, dek.astype(BF16)).astype(BF16)
    relq_ref[...] = d_rel_q
    relk_ref[...] = d_rel_k
    total = dot_nt(d_rel_q, wq_ref[...]) + dot_nt(d_rel_k, wk_ref[...])
    height = total.shape[0] // parts
    width = total.shape[1]
    me = me_ref[0]
    for block in range(parts):
        part_ref[me ^ block, :, :width] = total[block * height : (block + 1) * height]
    dk_low = dk_ref[...].astype(BF16)
    dv_low = dv_ref[...].astype(BF16)
    dk_low_ref[...] = dk_low
    dv_low_ref[...] = dv_low

    def summed(value):
        return jnp.sum(value.astype(F32), axis=0, keepdims=True)

    one, two = one_ref[0], two_ref[0]
    unit = unit_ref[0]
    for stream in range(1, one_ref.shape[0]):
        one, two = one + one_ref[stream], two + two_ref[stream]
        unit = unit + unit_ref[stream]
    vectors = [
        summed(dq_ref[...]) + summed(deq),
        summed(dk_low) + summed(dek),
        summed(dv_low),
        one[2:3], one[0:1], one[1:2], unit[0:1], two[2:3], two[0:1], two[1:2],
    ]
    part_ref[:, :, width:] = jnp.zeros((parts, height, LANES), F32)
    row = 0
    for vector in vectors:
        for piece in range(vector.shape[1] // LANES):
            line = vector[:, piece * LANES : (piece + 1) * LANES]
            at = row % height
            part_ref[me ^ (row // height), at : at + 1, width:] = line
            row += 1


def rel_grads(parts, me, onehot, deq, dek, wq, wk, dq, dk, dv, one, two, unit):
    span = onehot.shape[1]
    width, cols = wq.shape
    outs = [sds((span, cols), BF16)] * 2 + [sds(dk.shape, BF16)] * 2
    outs = outs + [sds((parts, span // parts, width + LANES), F32)]
    arrays = (onehot, deq, dek, wq, wk, dq, dk, dv, one, two, unit)
    return pl.pallas_call(
        functools.partial(rel_kernel, parts),
        grid=(1,),
        in_specs=[smem()] + [full(a) for a in arrays],
        out_specs=[full(o) for o in outs],
        out_shape=outs,
        compiler_params=params(),
        cost_estimate=cost(2 << 30, 8 << 20),
        name="rel_grads",
    )(me, *arrays)


def unpack_kernel(parts, me_ref, shared_ref, table_ref, *vector_refs):
    width = table_ref.shape[2]
    height = shared_ref.shape[1]
    me = me_ref[0]
    for block in range(parts):
        table_ref[me ^ block] = shared_ref[block, :, :width]
    row = 0
    for ref in vector_refs:
        for piece in range(ref.shape[1] // LANES):
            at = row % height
            line = shared_ref[me ^ (row // height), at : at + 1, width:]
            ref[:, piece * LANES : (piece + 1) * LANES] = line
            row += 1


def unpack(parts, me, shared, sizes):
    height, wide = shared.shape[1:]
    outs = [sds((parts, height, wide - LANES), F32)] + [sds((1, size), F32) for size in sizes]
    return pl.pallas_call(
        functools.partial(unpack_kernel, parts),
        grid=(1,),
        in_specs=[smem(), full(shared)],
        out_specs=[full(o) for o in outs],
        out_shape=outs,
        compiler_params=params(),
        cost_estimate=cost(0, 4 << 20),
        name="unpack",
    )(me, shared)


def hidden_kernel(dq_ref, dk_ref, dv_ref, wq_ref, wk_ref, wv_ref, out_ref):
    out_ref[...] = (
        dot_nt(dq_ref[...], wq_ref[...])
        + dot_nt(dk_ref[...], wk_ref[...])
        + dot_nt(dv_ref[...], wv_ref[...])
    )


def hidden_grad(dq, dk, dv, wq, wk, wv):
    arrays = (dq, dk, dv, wq, wk, wv)
    out = sds((dq.shape[0], wq.shape[0]), F32)
    return pl.pallas_call(
        hidden_kernel,
        grid=(1,),
        in_specs=[full(a) for a in arrays],
        out_specs=full(out),
        out_shape=out,
        compiler_params=params(),
        cost_estimate=cost(1 << 30, 5 << 20),
        name="hidden_grad",
    )(*arrays)


def bits_of(parts):
    return [1 << b for b in range(parts.bit_length() - 1)]


def swap_head(value):
    return lax.ppermute(value, "head", [(0, 1), (1, 0)])


def scatter_sum(blocks, parts, order):
    alive = sorted(order, reverse=True)
    value = blocks.reshape(*([2] * len(alive)), *blocks.shape[1:])
    for bit in order:
        axis = alive.index(bit)
        kept = lax.index_in_dim(value, 0, axis, keepdims=False)
        sent = lax.index_in_dim(value, 1, axis, keepdims=False)
        pairs = [(i, i ^ bit) for i in range(parts)]
        value = kept + lax.ppermute(sent, "dp", pairs)
        alive.remove(bit)
    return value


def gather_blocks(value, parts, order):
    gathered = value[None]
    for bit in sorted(order):
        pairs = [(i, i ^ bit) for i in range(parts)]
        gathered = jnp.concatenate([gathered, lax.ppermute(gathered, "dp", pairs)], axis=0)
    return gathered


def on_device(parts, *arguments):
    (
        hidden_in, lengths, cotangent, w_query, b_query, w_key, b_key, w_value, b_value,
        w_out, b_out, ln1_gain, ln1_bias, w_in, b_in, w_down, b_down, ln2_gain, ln2_bias,
        rel_table,
    ) = arguments
    seq_len, width = hidden_in.shape
    height = seq_len // STREAMS
    streams = range(STREAMS)
    (
        b_query, b_key, b_value, b_out, ln1_gain, ln1_bias, b_in, b_down, ln2_gain, ln2_bias,
    ) = [
        vector.reshape(1, -1)
        for vector in (
            b_query, b_key, b_value, b_out, ln1_gain, ln1_bias, b_in, b_down, ln2_gain, ln2_bias,
        )
    ]
    me = lax.axis_index("dp").astype(jnp.int32).reshape(1)
    side = lax.axis_index("head").astype(jnp.int32).reshape(1)
    bits = bits_of(parts)

    half = w_out.shape[0] // 2
    odd = lax.rem(me, 2)
    mine = lax.dynamic_slice_in_dim(w_out, odd[0] * half, half, 0).astype(F32)
    fetched = swap_head(mine)
    paired = lax.ppermute(fetched, "dp", [(i, i ^ 1) for i in range(parts)])
    w_out_all = assemble(side, odd, w_out, fetched, paired)

    q, k, v, eq, ek, onehot = project(
        hidden_in, rel_table, w_query, b_query, w_key, b_key, w_value, b_value
    )
    contexts, attends = zip(
        *[attend(at, height, lengths, q, k, v, eq, ek) for at in streams], strict=True
    )
    fed = []
    for at in streams:
        other_ctx = swap_head(contexts[at])
        first = jnp.where(side[0] == 0, contexts[at], other_ctx)
        second = jnp.where(side[0] == 0, other_ctx, contexts[at])
        fed.append(
            feed(
                at, height, first, second, w_out_all, b_out, hidden_in, ln1_gain, ln1_bias, w_in,
                b_in, w_down,
            )
        )
    backs = []
    for at in streams:
        xhat, rstd, normed, act, slope, lowered = fed[at]
        backs.append(
            feed_back(
                at, height, lowered, swap_head(lowered), xhat, ln1_gain, ln1_bias, b_down,
                ln2_gain, ln2_bias, cotangent, slope, w_in, w_down,
            )
        )
    attn_backs = []
    carried = None
    for at in streams:
        xhat, rstd = fed[at][:2]
        d_two, dn = backs[at][1], backs[at][4]
        result = attend_back(
            at, height, dn, swap_head(dn), d_two, xhat, rstd, ln1_gain, w_out, q, k, v, eq, ek,
            attends[at], carried,
        )
        carried = result[4:]
        attn_backs.append(result)

    def tall(pieces):
        return jnp.concatenate(pieces, axis=0)

    output = tall([b[0] for b in backs])
    d_low = tall([b[2] for b in backs])
    d_inner = tall([b[3] for b in backs])
    normed = tall([f[2] for f in fed])
    activated = tall([f[3] for f in fed])
    g_down = grad_blocks("grad_down", parts, me, [(d_low, activated)], 512)
    g_in = grad_blocks("grad_in", parts, me, [(normed, d_inner)], 512)
    s_down = scatter_sum(g_down, parts, bits)
    s_in = scatter_sum(g_in, parts, bits)

    d_one = tall([a[0] for a in attn_backs])
    d_mixed = tall([a[1] for a in attn_backs])
    dq = tall([a[2] for a in attn_backs])
    dk_sum, dv_sum, deq, dek = carried
    context = tall(contexts).astype(BF16)

    relq, relk, dk, dv, rel_all = rel_grads(
        parts, me, onehot, deq, dek, w_query, w_key, dq, dk_sum, dv_sum,
        jnp.stack([a[3] for a in attn_backs]), jnp.stack([b[5] for b in backs]),
        jnp.stack([b[6] for b in backs]),
    )
    d_hidden = hidden_grad(dq, dk, dv, w_query, w_key, w_value)
    grad_input = ((d_hidden + swap_head(d_hidden)) + d_one).astype(BF16)

    rel_sum = scatter_sum(rel_all, parts, bits)
    rel_own = rel_sum[:, :width]
    rel_own = rel_own + swap_head(rel_own)
    shared = jnp.concatenate([rel_own, rel_sum[:, width:]], axis=1)
    shared = gather_blocks(shared, parts, bits)
    sizes = [q.shape[1]] * 3 + [width] * 3 + [w_in.shape[1]] + [width] * 3
    table_blocks, *pieces = unpack(parts, me, shared, sizes)
    grad_rel_table = table_blocks.reshape(rel_table.shape)
    (
        grad_b_query, grad_b_key, grad_b_value, grad_b_out, grad_ln1_gain, grad_ln1_bias,
        grad_b_in, grad_b_down, grad_ln2_gain, grad_ln2_bias,
    ) = [piece.reshape(-1) for piece in pieces]

    g_out = grad_blocks("grad_out", parts, me, [(d_mixed, context)], 384)
    g_q = grad_blocks("grad_q", parts, me, [(hidden_in, dq), (rel_table, relq)], 384)
    g_k = grad_blocks("grad_k", parts, me, [(hidden_in, dk), (rel_table, relk)], 384)
    g_v = grad_blocks("grad_v", parts, me, [(hidden_in, dv)], 384)
    s_out = scatter_sum(g_out, parts, bits)
    s_q = scatter_sum(g_q, parts, bits)
    s_k = scatter_sum(g_k, parts, bits)
    s_v = scatter_sum(g_v, parts, bits)
    return (
        output, grad_input, s_q, grad_b_query, s_k, grad_b_key, s_v, grad_b_value,
        s_out.T, grad_b_out, grad_ln1_gain, grad_ln1_bias, s_in, grad_b_in,
        s_down.T, grad_b_down, grad_ln2_gain, grad_ln2_bias, grad_rel_table,
    )


def solution(mesh):
    parts = mesh.shape["dp"]
    return jax.shard_map(
        functools.partial(on_device, parts),
        mesh=mesh,
        in_specs=(
            P("dp", None), P("dp"), P("dp", None),
            P(None, "head"), P("head"), P(None, "head"), P("head"), P(None, "head"), P("head"),
            P("head", None), P(), P(), P(),
            P(None, "head"), P("head"), P("head", None), P(), P(), P(), P(),
        ),
        out_specs=(
            P("dp", None), P("dp", None),
            P("dp", "head"), P("head"), P("dp", "head"), P("head"), P("dp", "head"), P("head"),
            P("head", "dp"), P(), P(), P(),
            P("dp", "head"), P("head"), P("head", "dp"), P(), P(), P(), P(),
        ),
        check_vma=False,
    )
```

```python
import functools
import math

import jax
import jax.numpy as jnp
import numpy as np
from jax import lax
from jax.experimental import pallas as pl
from jax.experimental.pallas import tpu as pltpu
from jax.sharding import PartitionSpec as P

HEAD_DIM = 64
SPAN = 256
MAXPOS = 512
EPSILON = 1e-07
MASKED = -1000000000.0
LANES = 128
STREAMS = 2
BACK_FLOPS = 64 << 30
VMEM_LIMIT = 20 * 1024 * 1024

BF16 = jnp.bfloat16
F32 = jnp.float32


def bucket_of(offsets, bucket_span, max_distance):
    middle = bucket_span // 2
    direction = np.sign(offsets)
    absolute = np.where((offsets < middle) & (offsets > -middle), middle - 1, np.abs(offsets))
    log_part = (
        np.ceil(np.log(absolute / middle) / np.log((max_distance - 1) / middle) * (middle - 1))
        + middle
    )
    bucket = np.where(absolute <= middle, offsets, log_part * direction).astype(np.int64)
    return np.clip(bucket + bucket_span, 0, 2 * bucket_span - 1).astype(np.int32)


def distance_buckets(seq_len):
    offsets = np.maximum(seq_len - 1 - np.arange(2 * seq_len), 1 - seq_len)
    return bucket_of(offsets, SPAN, MAXPOS)


def dot_nn(a, b):
    return lax.dot_general(a, b, (((1,), (0,)), ((), ())), preferred_element_type=F32)


def dot_nt(a, b):
    return lax.dot_general(a, b, (((1,), (1,)), ((), ())), preferred_element_type=F32)


def dot_tn(a, b):
    return lax.dot_general(a, b, (((0,), (0,)), ((), ())), preferred_element_type=F32)


def whole_call(
    kernel, name, outs, operands, aliases=None, scalars=0, scratch=(), flops=1024, resident=True
):
    space = pl.BlockSpec(memory_space=pltpu.VMEM) if resident else pl.BlockSpec()
    in_specs = [pl.BlockSpec(memory_space=pltpu.SMEM)] * scalars
    in_specs += [space] * (len(operands) - scalars)
    return pl.pallas_call(
        kernel,
        in_specs=in_specs,
        out_specs=[pl.BlockSpec(memory_space=pltpu.VMEM)] * len(outs),
        out_shape=outs,
        scratch_shapes=list(scratch),
        input_output_aliases=aliases or {},
        compiler_params=pltpu.CompilerParams(vmem_limit_bytes=VMEM_LIMIT),
        cost_estimate=pl.CostEstimate(flops=flops, bytes_accessed=1024, transcendentals=0),
        name=name,
    )(*operands)


def sds(shape, dtype):
    return jax.ShapeDtypeStruct(shape, dtype)


def onehot_of(bucket_ref, span):
    buckets = bucket_ref[...]
    hot = buckets == lax.broadcasted_iota(jnp.int32, (span, buckets.shape[1]), 0)
    return jnp.where(hot, 1.0, 0.0).astype(BF16)


def project_kernel(
    bucket_ref, hidden_ref, table_ref, wq_ref, bq_ref, wk_ref, bk_ref, wv_ref, bv_ref,
    q_ref, k_ref, v_ref, eq_ref, ek_ref,
):
    hidden = hidden_ref[...]
    table = table_ref[...]
    onehot = onehot_of(bucket_ref, table.shape[0])
    q_ref[...] = (dot_nn(hidden, wq_ref[...]) + bq_ref[...].astype(F32)[None, :]).astype(BF16)
    k_ref[...] = (dot_nn(hidden, wk_ref[...]) + bk_ref[...].astype(F32)[None, :]).astype(BF16)
    v_ref[...] = (dot_nn(hidden, wv_ref[...]) + bv_ref[...].astype(F32)[None, :]).astype(BF16)
    rel_q = (dot_nn(table, wq_ref[...]) + bq_ref[...].astype(F32)[None, :]).astype(BF16)
    rel_k = (dot_nn(table, wk_ref[...]) + bk_ref[...].astype(F32)[None, :]).astype(BF16)
    eq_ref[...] = dot_tn(onehot, rel_q).astype(BF16)
    ek_ref[...] = dot_tn(onehot, rel_k).astype(BF16)


def project(buckets, hidden, table, wq, bq, wk, bk, wv, bv):
    seq_len = hidden.shape[0]
    cols = wq.shape[1]
    outs = [sds((seq_len, cols), BF16)] * 3 + [sds((2 * seq_len, cols), BF16)] * 2
    operands = (buckets, hidden, table, wq, bq, wk, bk, wv, bv)
    return whole_call(project_kernel, "project", outs, operands, resident=False)


def assemble_kernel(side_ref, odd_ref, own_ref, fetched_ref, paired_ref, out_ref):
    side, odd = side_ref[0], odd_ref[0]
    out_ref[side] = own_ref[...]
    half = fetched_ref.shape[0]
    out_ref[1 - side, pl.ds(pl.multiple_of(odd * half, half), half), :] = fetched_ref[...].astype(BF16)
    out_ref[1 - side, pl.ds(pl.multiple_of((1 - odd) * half, half), half), :] = paired_ref[...].astype(BF16)


def assemble(side, odd, own, fetched, paired):
    rows, width = own.shape
    out = sds((2, rows, width), BF16)
    operands = (side, odd, own, fetched, paired)
    (joined,) = whole_call(assemble_kernel, "assemble", [out], operands, scalars=2)
    return joined.reshape(2 * rows, width)


def half_masks():
    lane = lax.broadcasted_iota(jnp.int32, (1, LANES), 1)
    return [lane // HEAD_DIM == side for side in range(LANES // HEAD_DIM)]


def attend_kernel(at, height, len_ref, q_ref, k_ref, v_ref, eq_ref, ek_ref, ctx_ref, att_ref):
    seq_len = k_ref.shape[0]
    length = len_ref[0]
    scale = 1.0 / math.sqrt(3 * HEAD_DIM)
    masks = half_masks()
    key_valid = lax.broadcasted_iota(jnp.int32, (1, seq_len), 1) < length
    rows = at * height + lax.broadcasted_iota(jnp.int32, (height, 1), 0)
    query_valid = rows < length
    row_start = seq_len - height - height * at
    for pair in range(q_ref.shape[1] // LANES):
        cols = slice(pair * LANES, (pair + 1) * LANES)
        q_pair = q_ref[at * height : (at + 1) * height, cols]
        k_pair = k_ref[:, cols]
        v_pair = v_ref[:, cols]
        rel_window = ek_ref[row_start : row_start + seq_len + height, cols]
        outs = []
        for side, mask in enumerate(masks):
            q_one = jnp.where(mask, q_pair, jnp.zeros_like(q_pair))
            k_one = jnp.where(mask, k_pair, jnp.zeros_like(k_pair))
            content = dot_nt(q_one, k_pair)
            wide = dot_nt(q_one, rel_window)
            picked = pltpu.roll(wide, seq_len + 1, 1, stride=1, stride_axis=0)[:, :seq_len]
            blocks = []
            for block in range(seq_len // LANES):
                start = seq_len - LANES - LANES * block + height * at
                window = eq_ref[start : start + LANES + height, cols]
                tall = dot_nt(k_one[block * LANES : (block + 1) * LANES], window)
                tall = pltpu.roll(tall, height + 1, 1, stride=1, stride_axis=0)[:, :height]
                blocks.append(tall.T)
            flipped = jnp.concatenate(blocks, axis=1)
            scores = jnp.where(key_valid, scale * (content + picked + flipped), MASKED)
            peak = jnp.max(scores, axis=-1, keepdims=True)
            weight = jnp.exp(scores - peak)
            total = jnp.sum(weight, axis=-1, keepdims=True)
            keep = jnp.where(query_valid, 1.0 / total, 0.0)
            attend = (weight * keep).astype(BF16)
            att_ref[pair * len(masks) + side] = attend
            outs.append(dot_nn(attend, v_pair))
        ctx = jnp.where(masks[0], outs[0], outs[1])
        ctx_ref[:, cols] = ctx.astype(BF16).astype(F32)


def attend(at, height, lengths, q, k, v, eq, ek):
    seq_len, cols = q.shape
    heads = cols // HEAD_DIM
    outs = [sds((height, cols), F32), sds((heads, height, seq_len), BF16)]
    return whole_call(
        functools.partial(attend_kernel, at, height), f"attend_{at}", outs,
        (lengths, q, k, v, eq, ek), scalars=1,
    )


def attend_back_kernel(
    at, height, first, last,
    dn_own_ref, dn_other_ref, d_two_ref, xhat_ref, rstd_ref, gain_ref, wout_ref,
    q_ref, k_ref, v_ref, eq_ref, ek_ref, att_ref,
    *refs,
):
    if not first:
        dk_in, dv_in, deq_in, dek_in = refs[:4]
        refs = refs[4:]
    d_one_ref, d_mixed_ref, dq_ref, vec_ref, dk_ref, dv_ref, deq_ref, dek_ref = refs[:8]
    seq_len = k_ref.shape[0]
    scale = 1.0 / math.sqrt(3 * HEAD_DIM)
    masks = half_masks()
    d_normed = (dn_own_ref[...] + dn_other_ref[...]) + d_two_ref[...]
    xhat = xhat_ref[...]
    vec_ref[0:1, :] = jnp.sum(d_normed * xhat, axis=0, keepdims=True)
    vec_ref[1:2, :] = jnp.sum(d_normed, axis=0, keepdims=True)
    scaled = d_normed * gain_ref[...].astype(F32)[None, :]
    mean_a = jnp.mean(scaled, axis=-1, keepdims=True)
    mean_b = jnp.mean(scaled * xhat, axis=-1, keepdims=True)
    d_one = rstd_ref[...] * (scaled - mean_a - xhat * mean_b)
    d_one_ref[...] = d_one
    vec_ref[2:3, :] = jnp.sum(d_one, axis=0, keepdims=True)
    d_mixed = d_one.astype(BF16)
    d_mixed_ref[...] = d_mixed
    d_ctx = dot_nt(d_mixed, wout_ref[...]).astype(BF16)

    def anti(size):
        row = lax.broadcasted_iota(jnp.int32, (size, size), 0)
        col = lax.broadcasted_iota(jnp.int32, (size, size), 1)
        return jnp.where(row + col == size - 1, 1.0, 0.0).astype(BF16)

    anti_rows = anti(height)
    anti_keys = anti(LANES)
    row_start = seq_len - height - height * at
    if first:
        dk_ref[...] = jnp.zeros_like(dk_ref)
        dv_ref[...] = jnp.zeros_like(dv_ref)
        deq_ref[...] = jnp.zeros_like(deq_ref)
        dek_ref[...] = jnp.zeros_like(dek_ref)
    else:
        dk_ref[...] = dk_in[...]
        dv_ref[...] = dv_in[...]
        deq_ref[...] = deq_in[...]
        dek_ref[...] = dek_in[...]
    for pair in range(q_ref.shape[1] // LANES):
        cols = slice(pair * LANES, (pair + 1) * LANES)
        q_pair = q_ref[at * height : (at + 1) * height, cols]
        k_pair = k_ref[:, cols]
        v_pair = v_ref[:, cols]
        ctx_pair = d_ctx[:, cols]
        q_turned = dot_nn(anti_rows, q_pair).astype(BF16)
        k_turned = [
            dot_nn(anti_keys, k_pair[b * LANES : (b + 1) * LANES]).astype(BF16)
            for b in range(seq_len // LANES)
        ]
        rel_window = ek_ref[row_start : row_start + seq_len + height, cols]
        d_q, d_q_turned, d_k, d_v, d_rel_k, d_rel_q, d_k_turned = [], [], [], [], [], [], []
        for side, mask in enumerate(masks):
            weight = att_ref[pair * len(masks) + side]
            ctx_one = jnp.where(mask, ctx_pair, jnp.zeros_like(ctx_pair))
            d_att = dot_nt(ctx_one, v_pair)
            soft = weight.astype(F32)
            inner = jnp.sum(d_att * soft, axis=-1, keepdims=True)
            d_scores = (soft * (d_att - inner)).astype(BF16)
            d_v.append(dot_tn(weight, ctx_pair))
            d_q.append(dot_nn(d_scores, k_pair))
            d_scores_t = d_scores.T
            d_k.append(dot_nn(d_scores_t, q_pair))
            turned = dot_nn(anti_rows, d_scores)
            turned = jnp.concatenate([turned, jnp.zeros((height, height), F32)], axis=1)
            turned = pltpu.roll(turned, 0, 1, stride=1, stride_axis=0).astype(BF16)
            d_q_turned.append(dot_nn(turned, rel_window))
            d_rel_k.append(dot_tn(turned, q_turned))
            d_rel_q.append([])
            d_k_turned.append([])
            for block in range(seq_len // LANES):
                start = seq_len - LANES - LANES * block + height * at
                window = eq_ref[start : start + LANES + height, cols]
                tall = dot_nn(anti_keys, d_scores_t[block * LANES : (block + 1) * LANES])
                tall = jnp.concatenate([tall, jnp.zeros((LANES, LANES), F32)], axis=1)
                tall = pltpu.roll(tall, 0, 1, stride=1, stride_axis=0).astype(BF16)
                d_k_turned[-1].append(dot_nn(tall, window))
                d_rel_q[-1].append(dot_tn(tall, k_turned[block]))

        def join(two):
            return jnp.where(masks[0], two[0], two[1])

        def turn_back(matrix, value):
            high = value.astype(BF16)
            rest = (value - high.astype(F32)).astype(BF16)
            return dot_nn(matrix, high) + dot_nn(matrix, rest)

        dq_ref[:, cols] = (scale * (join(d_q) + turn_back(anti_rows, join(d_q_turned)))).astype(BF16)
        dv_ref[:, cols] += join(d_v)
        dk_ref[:, cols] += scale * join(d_k)
        dek_ref[row_start : row_start + seq_len + height, cols] += scale * join(d_rel_k)
        for block in range(seq_len // LANES):
            start = seq_len - LANES - LANES * block + height * at
            back = turn_back(anti_keys, join([d_k_turned[0][block], d_k_turned[1][block]]))
            dk_ref[block * LANES : (block + 1) * LANES, cols] += scale * back
            deq_ref[start : start + LANES + height, cols] += scale * join(
                [d_rel_q[0][block], d_rel_q[1][block]]
            )
    if last:
        dk_low_ref, dv_low_ref = refs[8:]
        dk_low_ref[...] = dk_ref[...].astype(BF16)
        dv_low_ref[...] = dv_ref[...].astype(BF16)


def attend_back(
    at, height, last, dn_own, dn_other, d_two, xhat, rstd, gain, wout, q, k, v, eq, ek, att, carried
):
    seq_len, cols = q.shape
    width = d_two.shape[1]
    operands = [dn_own, dn_other, d_two, xhat, rstd, gain, wout, q, k, v, eq, ek, att, *carried]
    outs = [
        sds((height, width), F32),
        sds((height, width), BF16),
        sds((height, cols), BF16),
        sds((8, width), F32),
        sds((seq_len, cols), F32),
        sds((seq_len, cols), F32),
        sds((2 * seq_len, cols), F32),
        sds((2 * seq_len, cols), F32),
    ]
    if last:
        outs += [sds((seq_len, cols), BF16)] * 2
    return whole_call(
        functools.partial(attend_back_kernel, at, height, not carried, last), f"attend_back_{at}",
        outs, operands, aliases={13: 4, 14: 5, 15: 6, 16: 7} if carried else {}, flops=BACK_FLOPS,
    )


def feed_kernel(
    at, height, side_ref, ctx_a_ref, ctx_b_ref, wout_ref, bout_ref, hidden_ref, gain_ref, shift_ref,
    win_ref, bin_ref, wdown_ref,
    xhat_ref, rstd_ref, normed_ref, act_ref, slope_ref, low_ref,
):
    own, other = ctx_a_ref[...], ctx_b_ref[...]
    first = side_ref[0] == 0
    ctx = jnp.concatenate([jnp.where(first, own, other), jnp.where(first, other, own)], axis=1)
    ctx = ctx.astype(BF16)
    mixed = dot_nn(ctx, wout_ref[...])
    hidden = hidden_ref[at * height : (at + 1) * height].astype(F32)
    resid = mixed + bout_ref[...].astype(F32)[None, :] + hidden
    center = resid - jnp.mean(resid, axis=-1, keepdims=True)
    spread = jnp.mean(center * center, axis=-1, keepdims=True)
    rstd = lax.rsqrt(spread + EPSILON)
    xhat = center * rstd
    xhat_ref[...] = xhat
    rstd_ref[...] = rstd
    normed = xhat * gain_ref[...].astype(F32)[None, :] + shift_ref[...].astype(F32)[None, :]
    low = normed.astype(BF16)
    normed_ref[...] = low
    units = win_ref.shape[1]
    step = units // 3
    total = None
    bias = bin_ref[...].astype(F32)[None, :]
    for part in range(3):
        cols = slice(part * step, (part + 1) * step)
        inner = dot_nn(low, win_ref[:, cols]) + bias[:, cols]
        phi = 0.5 * (1.0 + lax.erf(inner * math.sqrt(0.5)))
        act = (inner * phi).astype(BF16)
        slope = phi + inner * (jnp.exp(-0.5 * inner * inner) * (1.0 / math.sqrt(2 * math.pi)))
        act_ref[:, cols] = act
        slope_ref[:, cols] = slope
        term = dot_nn(act, wdown_ref[cols, :])
        total = term if total is None else total + term
    low_ref[...] = total


def feed(at, height, side, ctx_a, ctx_b, wout, bout, hidden, gain, shift, win, b_in, wdown):
    width = hidden.shape[1]
    units = win.shape[1]
    outs = [
        sds((height, width), F32),
        sds((height, 1), F32),
        sds((height, width), BF16),
        sds((height, units), BF16),
        sds((height, units), F32),
        sds((height, width), F32),
    ]
    operands = (side, ctx_a, ctx_b, wout, bout, hidden, gain, shift, win, b_in, wdown)
    return whole_call(
        functools.partial(feed_kernel, at, height), f"feed_{at}", outs, operands, scalars=1,
        flops=BACK_FLOPS if at else 1024,
    )


def feed_back_kernel(
    at, height, low_own_ref, low_other_ref, xhat_one_ref, gain_one_ref, shift_one_ref, bdown_ref,
    gain_ref, shift_ref, cot_ref, slope_ref, win_ref, wdown_ref,
    out_ref, d_two_ref, d_low_ref, d_inner_ref, dn_ref, vec_ref, bin_ref,
):
    normed = xhat_one_ref[...] * gain_one_ref[...].astype(F32)[None, :]
    normed = normed + shift_one_ref[...].astype(F32)[None, :]
    resid = (low_own_ref[...] + low_other_ref[...]) + bdown_ref[...].astype(F32)[None, :] + normed
    center = resid - jnp.mean(resid, axis=-1, keepdims=True)
    spread = jnp.mean(center * center, axis=-1, keepdims=True)
    rstd = lax.rsqrt(spread + EPSILON)
    xhat = center * rstd
    gain = gain_ref[...].astype(F32)[None, :]
    out_ref[...] = (xhat * gain + shift_ref[...].astype(F32)[None, :]).astype(BF16)
    err = cot_ref[at * height : (at + 1) * height].astype(F32)
    vec_ref[0:1, :] = jnp.sum(err * xhat, axis=0, keepdims=True)
    vec_ref[1:2, :] = jnp.sum(err, axis=0, keepdims=True)
    scaled = err * gain
    mean_a = jnp.mean(scaled, axis=-1, keepdims=True)
    mean_b = jnp.mean(scaled * xhat, axis=-1, keepdims=True)
    d_two = rstd * (scaled - mean_a - xhat * mean_b)
    d_two_ref[...] = d_two
    vec_ref[2:3, :] = jnp.sum(d_two, axis=0, keepdims=True)
    low = d_two.astype(BF16)
    d_low_ref[...] = low
    units = win_ref.shape[1]
    step = units // 3
    total = None
    for part in range(3):
        cols = slice(part * step, (part + 1) * step)
        d_act = dot_nt(low, wdown_ref[cols, :])
        d_inner = (d_act * slope_ref[:, cols]).astype(BF16)
        d_inner_ref[:, cols] = d_inner
        bin_ref[0:1, cols] = jnp.sum(d_inner.astype(F32), axis=0, keepdims=True)
        term = dot_nt(d_inner, win_ref[:, cols])
        total = term if total is None else total + term
    dn_ref[...] = total


def feed_back(
    at, height, low_own, low_other, xhat, gain_one, shift_one, bdown, gain, shift, cot, slope, win,
    wdown,
):
    width = cot.shape[1]
    units = win.shape[1]
    outs = [
        sds((height, width), BF16),
        sds((height, width), F32),
        sds((height, width), BF16),
        sds((height, units), BF16),
        sds((height, width), F32),
        sds((8, width), F32),
        sds((8, units), F32),
    ]
    operands = (
        low_own, low_other, xhat, gain_one, shift_one, bdown, gain, shift, cot, slope, win, wdown
    )
    return whole_call(
        functools.partial(feed_back_kernel, at, height), f"feed_back_{at}", outs, operands
    )


def spread(order, me, total, kept_ref, sent_ref, cols):
    parts = 1 << len(order)
    height = total.shape[0] // parts
    for bit in (0, order[0]):

        @pl.when((me & order[0]) == bit)
        def _(bit=bit):
            for block in range(parts):
                origin = me ^ block
                place = 0
                for later in order[1:]:
                    place = 2 * place + ((origin >> (later.bit_length() - 1)) & 1)
                target = kept_ref if block & order[0] == bit else sent_ref
                target[place, :, cols] = total[block * height : (block + 1) * height]


def grad_kernel(order, groups, me_ref, *refs):
    kept_ref, sent_ref = refs[-2:]
    me = me_ref[0]
    at, start = 0, 0
    for count in groups:
        total = None
        for _ in range(count):
            left, right = refs[at][...], refs[at + 1][...].astype(BF16)
            at += 2
            term = dot_tn(left, right)
            total = term if total is None else total + term
        cols = slice(start, start + total.shape[1])
        start += total.shape[1]
        spread(order, me, total, kept_ref, sent_ref, cols)


def grad_blocks(name, order, me, groups):
    parts = 1 << len(order)
    width = groups[0][0][0].shape[1]
    cols = sum(group[0][1].shape[1] for group in groups)
    operands = [array for group in groups for term in group for array in term]
    counts = [len(group) for group in groups]
    outs = [sds((parts // 2, width // parts, cols), F32)] * 2
    return whole_call(
        functools.partial(grad_kernel, order, counts), name, outs, [me, *operands],
        scalars=1,
    )


def rel_kernel(
    order, streams, table_rows, me_ref, bucket_ref, deq_ref, dek_ref, wq_ref, wk_ref, dk_ref, dv_ref,
    *refs,
):
    dq_refs, refs = refs[:streams], refs[streams:]
    one_refs, refs = refs[:streams], refs[streams:]
    two_refs, refs = refs[:streams], refs[streams:]
    unit_refs, refs = refs[:streams], refs[streams:]
    relq_ref, relk_ref, kept_ref, sent_ref, pack_ref = refs
    onehot = onehot_of(bucket_ref, table_rows)
    deq, dek = deq_ref[...], dek_ref[...]
    d_rel_q = dot_nn(onehot, deq.astype(BF16)).astype(BF16)
    d_rel_k = dot_nn(onehot, dek.astype(BF16)).astype(BF16)
    relq_ref[...] = d_rel_q
    relk_ref[...] = d_rel_k
    total = dot_nt(d_rel_q, wq_ref[...]) + dot_nt(d_rel_k, wk_ref[...])
    width = total.shape[1]
    me = me_ref[0]
    spread(order, me, total, kept_ref, sent_ref, slice(0, width))

    def summed(value):
        return jnp.sum(value.astype(F32), axis=0, keepdims=True)

    def over(stream_refs):
        value = stream_refs[0][...]
        for ref in stream_refs[1:]:
            value = value + ref[...]
        return value

    one, two, unit = over(one_refs), over(two_refs), over(unit_refs)
    d_bias = summed(dq_refs[0][...])
    for ref in dq_refs[1:]:
        d_bias = d_bias + summed(ref[...])
    vectors = [
        d_bias + summed(deq),
        summed(dk_ref[...]) + summed(dek),
        summed(dv_ref[...]),
        one[2:3], one[0:1], one[1:2], unit[0:1], two[2:3], two[0:1], two[1:2],
    ]
    pack_ref[...] = jnp.zeros_like(pack_ref)
    row = 0
    for vector in vectors:
        for piece in range(vector.shape[1] // LANES):
            pack_ref[row : row + 1, :] = vector[:, piece * LANES : (piece + 1) * LANES]
            row += 1
    spread(order, me, pack_ref[...], kept_ref, sent_ref, slice(width, width + LANES))


def rel_grads(order, span, me, buckets, deq, dek, wq, wk, dk, dv, dq, one, two, unit):
    width, cols = wq.shape
    outs = [sds((span, cols), BF16)] * 2
    parts = 1 << len(order)
    outs = outs + [sds((parts // 2, span // parts, width + LANES), F32)] * 2
    operands = [me, buckets, deq, dek, wq, wk, dk, dv, *dq, *one, *two, *unit]
    return whole_call(
        functools.partial(rel_kernel, order, len(dq), span), "rel_grads", outs, operands,
        scalars=1, scratch=[pltpu.VMEM((span, LANES), F32)],
    )


def unpack_kernel(origins, count, me_ref, *refs):
    shared_refs, (table_ref, *vector_refs) = refs[:count], refs[count:]
    width = table_ref.shape[2]
    height = table_ref.shape[1]
    me = me_ref[0]
    places = [(ref, at) for ref in shared_refs for at in range(ref.shape[0])]
    rows = sum(ref.shape[0] for ref in vector_refs) // LANES
    lines = [
        (ref, piece) for ref in vector_refs for piece in range(ref.shape[0] // LANES)
    ]
    for (shared_ref, at), origin in zip(places, origins, strict=True):
        table_ref[me ^ origin] = shared_ref[at, :, :width]
        for block in range((rows + height - 1) // height):

            @pl.when(me ^ origin == block)
            def _(shared_ref=shared_ref, at=at, block=block):
                for row in range(block * height, min(rows, (block + 1) * height)):
                    ref, piece = lines[row]
                    inner = row % height
                    line = shared_ref[at, inner : inner + 1, width:]
                    ref[pl.ds(piece * LANES, LANES)] = line.reshape(LANES)


def unpack(origins, me, pieces, sizes):
    height, wide = pieces[0].shape[1:]
    outs = [sds((len(origins), height, wide - LANES), F32)] + [sds((size,), F32) for size in sizes]
    return whole_call(
        functools.partial(unpack_kernel, origins, len(pieces)), "unpack", outs, (me, *pieces),
        scalars=1,
    )


def hidden_kernel(streams, dk_ref, dv_ref, wq_ref, wk_ref, wv_ref, *refs):
    out_ref = refs[-1]
    out_ref[...] = dot_nt(dk_ref[...], wk_ref[...]) + dot_nt(dv_ref[...], wv_ref[...])
    height = out_ref.shape[0] // streams
    for at in range(streams):
        out_ref[at * height : (at + 1) * height] += dot_nt(refs[at][...], wq_ref[...])


def hidden_grad(dk, dv, wq, wk, wv, dq):
    out = sds((dk.shape[0], wq.shape[0]), F32)
    (total,) = whole_call(
        functools.partial(hidden_kernel, len(dq)), "hidden_grad", [out], (dk, dv, wq, wk, wv, *dq)
    )
    return total


def bits_of(parts):
    return [1 << b for b in range(parts.bit_length() - 1)]


def swap_head(value):
    return lax.ppermute(value, "head", [(0, 1), (1, 0)])


def flip(value, parts, bit):
    return lax.ppermute(value, "dp", [(i, i ^ bit) for i in range(parts)])


def scatter_step(value, arrived):
    half = value.shape[0] // 2
    return value[:half] + arrived[:half], value[half:] + arrived[half:]


def scatter_sum(kept, sent, parts, order):
    arrived = flip(sent, parts, order[0])
    for bit in order[1:]:
        kept, sent = scatter_step(kept, arrived)
        arrived = flip(sent, parts, bit)
    return (kept + arrived)[0]


def together(*values):
    return lax.optimization_barrier(values)


def gather_blocks(value, parts, order):
    pieces, origins = [value[None]], [0]
    for bit in order:
        sent = pieces[0] if len(pieces) == 1 else jnp.concatenate(pieces, axis=0)
        pieces.append(flip(sent, parts, bit))
        origins = origins + [origin ^ bit for origin in origins]
    return pieces, origins


def on_device(parts, *arguments):
    (
        hidden_in, lengths, cotangent, w_query, b_query, w_key, b_key, w_value, b_value,
        w_out, b_out, ln1_gain, ln1_bias, w_in, b_in, w_down, b_down, ln2_gain, ln2_bias,
        rel_table,
    ) = arguments
    seq_len, width = hidden_in.shape
    height = seq_len // STREAMS
    streams = range(STREAMS)
    me = lax.axis_index("dp").astype(jnp.int32).reshape(1)
    side = lax.axis_index("head").astype(jnp.int32).reshape(1)
    bits = bits_of(parts)

    half = w_out.shape[0] // 2
    odd = lax.rem(me, 2)
    buckets = jnp.asarray(distance_buckets(seq_len)[None, :])
    mine = lax.dynamic_slice_in_dim(w_out, odd[0] * half, half, 0).astype(F32)
    fetched = swap_head(mine)
    q, k, v, eq, ek = project(
        buckets, hidden_in, rel_table, w_query, b_query, w_key, b_key, w_value, b_value
    )
    contexts, attends = zip(
        *[attend(at, height, lengths, q, k, v, eq, ek) for at in streams], strict=True
    )
    contexts, attends = list(contexts), list(attends)
    fetched, contexts[0] = together(fetched, contexts[0])
    paired = flip(fetched, parts, 1)
    w_out_all = assemble(side, odd, w_out, fetched, paired)
    others = [swap_head(context) for context in contexts]
    others[0], contexts[1] = together(others[0], contexts[1])
    fed = []
    for at in streams:
        if at:
            previous = list(fed[-1])
            others[at], previous[1] = together(others[at], previous[1])
            fed[-1] = previous
        fed.append(
            feed(
                at, height, side, contexts[at], others[at], w_out_all, b_out, hidden_in, ln1_gain,
                ln1_bias, w_in, b_in, w_down,
            )
        )
    lowered_other = [swap_head(stage[5]) for stage in fed]
    backs = []
    for at in streams:
        xhat, rstd, normed, act, slope, lowered = fed[at]
        if at:
            previous = list(backs[-1])
            lowered_other[at], previous[5] = together(lowered_other[at], previous[5])
            backs[-1] = previous
        backs.append(
            feed_back(
                at, height, lowered, lowered_other[at], xhat, ln1_gain, ln1_bias, b_down, ln2_gain,
                ln2_bias, cotangent, slope, w_in, w_down,
            )
        )
    d_normed_other = [swap_head(stage[4]) for stage in backs]
    crossed = bits[:1] + bits[2:] + bits[1:2]
    g_down = grad_blocks(
        "grad_down", bits, me, [[(backs[at][2], fed[at][3]) for at in streams]]
    )
    g_in = grad_blocks(
        "grad_in", crossed, me, [[(fed[at][2], backs[at][3]) for at in streams]]
    )
    attends[0], *grads = together(attends[0], *g_down, *g_in)
    arrived = [flip(grads[1], parts, bits[0]), flip(grads[3], parts, crossed[0])]
    attn_backs = []
    carried = ()
    for at in streams:
        xhat, rstd = fed[at][:2]
        d_two, dn = backs[at][1], backs[at][4]
        result = attend_back(
            at, height, at == streams[-1], dn, d_normed_other[at], d_two, xhat, rstd, ln1_gain,
            w_out, q, k, v, eq, ek, attends[at], carried,
        )
        result = list(result)
        if at == 0:
            result[3], *arrived = together(result[3], *arrived)
            p_down = scatter_step(grads[0], arrived[0])
            p_in = scatter_step(grads[2], arrived[1])
            attends[1], *grads = together(attends[1], *p_down, *p_in)
            p_down = scatter_step(grads[0], flip(grads[1], parts, bits[1]))
            p_in = scatter_step(grads[2], flip(grads[3], parts, crossed[1]))
        carried = result[4:8]
        attn_backs.append(result)
    dk, dv = attn_backs[-1][8:]
    deq, dek = carried[2:]
    dq = [a[2] for a in attn_backs]

    def tall(pieces):
        return jnp.concatenate(pieces, axis=0)

    output = tall([b[0] for b in backs])
    d_hidden = hidden_grad(dk, dv, w_query, w_key, w_value, dq)
    relq, relk, *rel_all = rel_grads(
        bits, rel_table.shape[0], me, buckets, deq, dek, w_query, w_key, dk, dv, dq,
        [a[3] for a in attn_backs], [b[5] for b in backs], [b[6] for b in backs],
    )
    *rel_all, d_kept, d_sent, i_kept, i_sent = together(*rel_all, *p_down, *p_in)
    s_down = scatter_sum(d_kept, d_sent, parts, bits[2:])
    s_in = scatter_sum(i_kept, i_sent, parts, crossed[2:])
    d_one = tall([a[0] for a in attn_backs])
    grad_input = ((d_hidden + swap_head(d_hidden)) + d_one).astype(BF16)

    rel_sum = scatter_sum(*rel_all, parts, bits)
    rel_own = rel_sum[:, :width]
    rel_own = rel_own + swap_head(rel_own)
    shared = jnp.concatenate([rel_own, rel_sum[:, width:]], axis=1)
    shared, s_down, s_in = together(shared, s_down, s_in)
    gathered, origins = gather_blocks(shared, parts, bits[::-1])
    sizes = [q.shape[1]] * 3 + [width] * 3 + [w_in.shape[1]] + [width] * 3
    table_blocks, *pieces = unpack(origins, me, gathered, sizes)
    grad_rel_table = table_blocks.reshape(rel_table.shape)
    (
        grad_b_query, grad_b_key, grad_b_value, grad_b_out, grad_ln1_gain, grad_ln1_bias,
        grad_b_in, grad_b_down, grad_ln2_gain, grad_ln2_bias,
    ) = pieces

    hidden_parts = [hidden_in[at * height : (at + 1) * height] for at in streams]
    g_vo = grad_blocks(
        "grad_value_out", crossed, me,
        [
            [(hidden_in, dv)],
            [(attn_backs[at][1], contexts[at]) for at in streams],
        ],
    )
    g_qk = grad_blocks(
        "grad_query_key", bits, me,
        [
            [*zip(hidden_parts, dq, strict=True), (rel_table, relq)],
            [(hidden_in, dk), (rel_table, relk)],
        ],
    )
    s_vo = scatter_sum(*g_vo, parts, crossed)
    s_qk = scatter_sum(*g_qk, parts, bits)
    cols = q.shape[1]
    s_q, s_k = s_qk[:, :cols], s_qk[:, cols:]
    s_v, s_out = s_vo[:, :cols], s_vo[:, cols:]
    return (
        output, grad_input, s_q, grad_b_query, s_k, grad_b_key, s_v, grad_b_value,
        s_out.T, grad_b_out, grad_ln1_gain, grad_ln1_bias, s_in, grad_b_in,
        s_down.T, grad_b_down, grad_ln2_gain, grad_ln2_bias, grad_rel_table,
    )


def solution(mesh):
    parts = mesh.shape["dp"]
    return jax.shard_map(
        functools.partial(on_device, parts),
        mesh=mesh,
        in_specs=(
            P("dp", None), P("dp"), P("dp", None),
            P(None, "head"), P("head"), P(None, "head"), P("head"), P(None, "head"), P("head"),
            P("head", None), P(), P(), P(),
            P(None, "head"), P("head"), P("head", None), P(), P(), P(), P(),
        ),
        out_specs=(
            P("dp", None), P("dp", None),
            P("dp", "head"), P("head"), P("dp", "head"), P("head"), P("dp", "head"), P("head"),
            P("head", "dp"), P(), P(), P(),
            P("dp", "head"), P("head"), P("head", "dp"), P(), P(), P(), P(),
        ),
        check_vma=False,
    )
```

```python
import functools
import math

import jax
import jax.numpy as jnp
import numpy as np
from jax import lax
from jax.experimental import pallas as pl
from jax.experimental.pallas import tpu as pltpu
from jax.sharding import PartitionSpec as P

HEAD_DIM = 64
SPAN = 256
MAXPOS = 512
EPSILON = 1e-07
MASKED = -1000000000.0
LANES = 128
STREAMS = 2
BACK_FLOPS = 64 << 30
VMEM_LIMIT = 8 * 1024 * 1024

BF16 = jnp.bfloat16
F32 = jnp.float32


def bucket_of(offsets, bucket_span, max_distance):
    middle = bucket_span // 2
    direction = np.sign(offsets)
    absolute = np.where((offsets < middle) & (offsets > -middle), middle - 1, np.abs(offsets))
    log_part = (
        np.ceil(np.log(absolute / middle) / np.log((max_distance - 1) / middle) * (middle - 1))
        + middle
    )
    bucket = np.where(absolute <= middle, offsets, log_part * direction).astype(np.int64)
    return np.clip(bucket + bucket_span, 0, 2 * bucket_span - 1).astype(np.int32)


def distance_buckets(seq_len):
    offsets = np.maximum(seq_len - 1 - np.arange(2 * seq_len), 1 - seq_len)
    return bucket_of(offsets, SPAN, MAXPOS)


def dot_nn(a, b):
    return lax.dot_general(a, b, (((1,), (0,)), ((), ())), preferred_element_type=F32)


def dot_nt(a, b):
    return lax.dot_general(a, b, (((1,), (1,)), ((), ())), preferred_element_type=F32)


def dot_tn(a, b):
    return lax.dot_general(a, b, (((0,), (0,)), ((), ())), preferred_element_type=F32)


class Line:
    def __init__(self):
        self.last = ()

    def call(
        self, kernel, name, outs, operands, aliases=None, scalars=0, scratch=(), flops=1024,
        space=pltpu.VMEM,
    ):
        in_specs = [pl.BlockSpec(memory_space=pltpu.SMEM)] * scalars
        in_specs += [pl.BlockSpec(memory_space=space)] * (len(operands) - scalars)
        in_specs += [pl.BlockSpec(memory_space=pl.ANY)] * len(self.last)
        count, skipped = len(operands), len(self.last)

        def body(*refs):
            kernel(*refs[:count], *refs[count + skipped :])

        results = pl.pallas_call(
            body,
            in_specs=in_specs,
            out_specs=[pl.BlockSpec(memory_space=pltpu.VMEM)] * len(outs),
            out_shape=outs,
            scratch_shapes=list(scratch),
            input_output_aliases=aliases or {},
            compiler_params=pltpu.CompilerParams(vmem_limit_bytes=VMEM_LIMIT),
            cost_estimate=pl.CostEstimate(flops=flops, bytes_accessed=1024, transcendentals=0),
            name=name,
        )(*operands, *self.last)
        self.last = (min(results, key=lambda result: result.size * result.dtype.itemsize),)
        return results


def sds(shape, dtype):
    return jax.ShapeDtypeStruct(shape, dtype)


def onehot_of(bucket_ref, span):
    buckets = bucket_ref[...]
    hot = buckets == lax.broadcasted_iota(jnp.int32, (span, buckets.shape[1]), 0)
    return jnp.where(hot, 1.0, 0.0).astype(BF16)


def project_kernel(
    bucket_hbm, hidden_hbm, wq_hbm, bq_hbm, wk_hbm, bk_hbm, wv_hbm, bv_hbm, table_hbm,
    q_ref, k_ref, v_ref, eq_ref, ek_ref,
    bucket_ref, hidden_ref, wq_ref, bq_ref, wk_ref, bk_ref, wv_ref, bv_ref, table_ref, sems,
):
    sources = (
        hidden_hbm, wq_hbm, bq_hbm, wk_hbm, bk_hbm, wv_hbm, bv_hbm, table_hbm, bucket_hbm
    )
    targets = (
        hidden_ref, wq_ref, bq_ref, wk_ref, bk_ref, wv_ref, bv_ref, table_ref, bucket_ref
    )
    copies = [
        pltpu.make_async_copy(source, target, sems.at[at])
        for at, (source, target) in enumerate(zip(sources, targets, strict=True))
    ]
    for copy in copies:
        copy.start()

    def need(count):
        for copy in copies[:count]:
            copy.wait()
        del copies[:count]

    def biased(rows, weight_ref, bias_ref):
        return (dot_nn(rows, weight_ref[...]) + bias_ref[...].astype(F32)[None, :]).astype(BF16)

    need(3)
    hidden = hidden_ref[...]
    q_ref[...] = biased(hidden, wq_ref, bq_ref)
    need(2)
    k_ref[...] = biased(hidden, wk_ref, bk_ref)
    need(2)
    v_ref[...] = biased(hidden, wv_ref, bv_ref)
    need(2)
    table = table_ref[...]
    onehot = onehot_of(bucket_ref, table.shape[0])
    eq_ref[...] = dot_tn(onehot, biased(table, wq_ref, bq_ref)).astype(BF16)
    ek_ref[...] = dot_tn(onehot, biased(table, wk_ref, bk_ref)).astype(BF16)


def project(line, buckets, hidden, wq, bq, wk, bk, wv, bv, table):
    seq_len = hidden.shape[0]
    cols = wq.shape[1]
    outs = [sds((seq_len, cols), BF16)] * 3 + [sds((2 * seq_len, cols), BF16)] * 2
    operands = (buckets, hidden, wq, bq, wk, bk, wv, bv, table)
    scratch = [pltpu.VMEM(operand.shape, operand.dtype) for operand in operands]
    operands = [pltpu.with_memory_space_constraint(operand, pltpu.HBM) for operand in operands]
    scratch += [pltpu.SemaphoreType.DMA((len(operands),))]
    return line.call(
        project_kernel, "project", outs, operands, scratch=scratch, space=pltpu.HBM
    )


def assemble_kernel(own_ref, fetched_ref, paired_ref, out_ref):
    side, odd = lax.axis_index("head"), lax.rem(lax.axis_index("dp"), 2)
    out_ref[side] = own_ref[...]
    half = fetched_ref.shape[0]
    out_ref[1 - side, pl.ds(pl.multiple_of(odd * half, half), half), :] = fetched_ref[...].astype(BF16)
    out_ref[1 - side, pl.ds(pl.multiple_of((1 - odd) * half, half), half), :] = paired_ref[...].astype(BF16)


def assemble(line, own, fetched, paired):
    rows, width = own.shape
    out = sds((2, rows, width), BF16)
    operands = (own, fetched, paired)
    (joined,) = line.call(assemble_kernel, "assemble", [out], operands)
    return joined.reshape(2 * rows, width)


def half_masks():
    lane = lax.broadcasted_iota(jnp.int32, (1, LANES), 1)
    return [lane // HEAD_DIM == side for side in range(LANES // HEAD_DIM)]


def attend_kernel(at, height, len_ref, q_ref, k_ref, v_ref, eq_ref, ek_ref, ctx_ref, att_ref):
    seq_len = k_ref.shape[0]
    length = len_ref[0]
    scale = 1.0 / math.sqrt(3 * HEAD_DIM)
    masks = half_masks()
    key_valid = lax.broadcasted_iota(jnp.int32, (1, seq_len), 1) < length
    rows = at * height + lax.broadcasted_iota(jnp.int32, (height, 1), 0)
    query_valid = rows < length
    row_start = seq_len - height - height * at
    for pair in range(q_ref.shape[1] // LANES):
        cols = slice(pair * LANES, (pair + 1) * LANES)
        q_pair = q_ref[at * height : (at + 1) * height, cols]
        k_pair = k_ref[:, cols]
        v_pair = v_ref[:, cols]
        rel_window = ek_ref[row_start : row_start + seq_len + height, cols]
        outs = []
        for side, mask in enumerate(masks):
            q_one = jnp.where(mask, q_pair, jnp.zeros_like(q_pair))
            k_one = jnp.where(mask, k_pair, jnp.zeros_like(k_pair))
            content = dot_nt(q_one, k_pair)
            wide = dot_nt(q_one, rel_window)
            picked = pltpu.roll(wide, seq_len + 1, 1, stride=1, stride_axis=0)[:, :seq_len]
            blocks = []
            for block in range(seq_len // LANES):
                start = seq_len - LANES - LANES * block + height * at
                window = eq_ref[start : start + LANES + height, cols]
                tall = dot_nt(k_one[block * LANES : (block + 1) * LANES], window)
                tall = pltpu.roll(tall, height + 1, 1, stride=1, stride_axis=0)[:, :height]
                blocks.append(tall.T)
            flipped = jnp.concatenate(blocks, axis=1)
            scores = jnp.where(key_valid, scale * (content + picked + flipped), MASKED)
            peak = jnp.max(scores, axis=-1, keepdims=True)
            weight = jnp.exp(scores - peak)
            total = jnp.sum(weight, axis=-1, keepdims=True)
            keep = jnp.where(query_valid, 1.0 / total, 0.0)
            attend = (weight * keep).astype(BF16)
            att_ref[pair * len(masks) + side] = attend
            outs.append(dot_nn(attend, v_pair))
        ctx = jnp.where(masks[0], outs[0], outs[1])
        ctx_ref[:, cols] = ctx.astype(BF16).astype(F32)


def attend(line, at, height, lengths, q, k, v, eq, ek):
    seq_len, cols = q.shape
    heads = cols // HEAD_DIM
    outs = [sds((height, cols), F32), sds((heads, height, seq_len), BF16)]
    return line.call(
        functools.partial(attend_kernel, at, height), f"attend_{at}", outs,
        (lengths, q, k, v, eq, ek), scalars=1,
    )


def norm_back_kernel(
    dn_own_ref, dn_other_ref, d_two_ref, xhat_ref, rstd_ref, gain_ref, wout_ref,
    d_one_ref, d_mixed_ref, d_ctx_ref, vec_ref,
):
    d_normed = (dn_own_ref[...] + dn_other_ref[...]) + d_two_ref[...]
    xhat = xhat_ref[...]
    vec_ref[0:1, :] = jnp.sum(d_normed * xhat, axis=0, keepdims=True)
    vec_ref[1:2, :] = jnp.sum(d_normed, axis=0, keepdims=True)
    scaled = d_normed * gain_ref[...].astype(F32)[None, :]
    mean_a = jnp.mean(scaled, axis=-1, keepdims=True)
    mean_b = jnp.mean(scaled * xhat, axis=-1, keepdims=True)
    d_one = rstd_ref[...] * (scaled - mean_a - xhat * mean_b)
    d_one_ref[...] = d_one
    vec_ref[2:3, :] = jnp.sum(d_one, axis=0, keepdims=True)
    d_mixed = d_one.astype(BF16)
    d_mixed_ref[...] = d_mixed
    d_ctx_ref[...] = dot_nt(d_mixed, wout_ref[...]).astype(BF16)


def norm_back(line, at, dn_own, dn_other, d_two, xhat, rstd, gain, wout):
    height, width = d_two.shape
    outs = [
        sds((height, width), F32),
        sds((height, width), BF16),
        sds((height, wout.shape[0]), BF16),
        sds((8, width), F32),
    ]
    operands = (dn_own, dn_other, d_two, xhat, rstd, gain, wout)
    return line.call(norm_back_kernel, f"norm_back_{at}", outs, operands, flops=BACK_FLOPS)


def attend_back_kernel(
    at, height, first, last, d_ctx_ref, q_ref, k_ref, v_ref, eq_ref, ek_ref, att_ref, *refs
):
    if not first:
        dk_in, dv_in, deq_in, dek_in = refs[:4]
        refs = refs[4:]
    dq_ref, dk_ref, dv_ref, deq_ref, dek_ref = refs[:5]
    seq_len = k_ref.shape[0]
    scale = 1.0 / math.sqrt(3 * HEAD_DIM)
    masks = half_masks()
    d_ctx = d_ctx_ref[...]

    def anti(size):
        row = lax.broadcasted_iota(jnp.int32, (size, size), 0)
        col = lax.broadcasted_iota(jnp.int32, (size, size), 1)
        return jnp.where(row + col == size - 1, 1.0, 0.0).astype(BF16)

    anti_rows = anti(height)
    anti_keys = anti(LANES)
    row_start = seq_len - height - height * at
    if first:
        dk_ref[...] = jnp.zeros_like(dk_ref)
        dv_ref[...] = jnp.zeros_like(dv_ref)
        deq_ref[...] = jnp.zeros_like(deq_ref)
        dek_ref[...] = jnp.zeros_like(dek_ref)
    else:
        dk_ref[...] = dk_in[...]
        dv_ref[...] = dv_in[...]
        deq_ref[...] = deq_in[...]
        dek_ref[...] = dek_in[...]
    for pair in range(q_ref.shape[1] // LANES):
        cols = slice(pair * LANES, (pair + 1) * LANES)
        q_pair = q_ref[at * height : (at + 1) * height, cols]
        k_pair = k_ref[:, cols]
        v_pair = v_ref[:, cols]
        ctx_pair = d_ctx[:, cols]
        q_turned = dot_nn(anti_rows, q_pair).astype(BF16)
        k_turned = [
            dot_nn(anti_keys, k_pair[b * LANES : (b + 1) * LANES]).astype(BF16)
            for b in range(seq_len // LANES)
        ]
        rel_window = ek_ref[row_start : row_start + seq_len + height, cols]
        d_q, d_q_turned, d_k, d_v, d_rel_k, d_rel_q, d_k_turned = [], [], [], [], [], [], []
        for side, mask in enumerate(masks):
            weight = att_ref[pair * len(masks) + side]
            ctx_one = jnp.where(mask, ctx_pair, jnp.zeros_like(ctx_pair))
            d_att = dot_nt(ctx_one, v_pair)
            soft = weight.astype(F32)
            inner = jnp.sum(d_att * soft, axis=-1, keepdims=True)
            d_scores = (soft * (d_att - inner)).astype(BF16)
            d_v.append(dot_tn(weight, ctx_pair))
            d_q.append(dot_nn(d_scores, k_pair))
            d_scores_t = d_scores.T
            d_k.append(dot_nn(d_scores_t, q_pair))
            turned = dot_nn(anti_rows, d_scores)
            turned = jnp.concatenate([turned, jnp.zeros((height, height), F32)], axis=1)
            turned = pltpu.roll(turned, 0, 1, stride=1, stride_axis=0).astype(BF16)
            d_q_turned.append(dot_nn(turned, rel_window))
            d_rel_k.append(dot_tn(turned, q_turned))
            d_rel_q.append([])
            d_k_turned.append([])
            for block in range(seq_len // LANES):
                start = seq_len - LANES - LANES * block + height * at
                window = eq_ref[start : start + LANES + height, cols]
                tall = dot_nn(anti_keys, d_scores_t[block * LANES : (block + 1) * LANES])
                tall = jnp.concatenate([tall, jnp.zeros((LANES, LANES), F32)], axis=1)
                tall = pltpu.roll(tall, 0, 1, stride=1, stride_axis=0).astype(BF16)
                d_k_turned[-1].append(dot_nn(tall, window))
                d_rel_q[-1].append(dot_tn(tall, k_turned[block]))

        def join(two):
            return jnp.where(masks[0], two[0], two[1])

        def turn_back(matrix, value):
            high = value.astype(BF16)
            rest = (value - high.astype(F32)).astype(BF16)
            return dot_nn(matrix, high) + dot_nn(matrix, rest)

        dq_ref[:, cols] = (scale * (join(d_q) + turn_back(anti_rows, join(d_q_turned)))).astype(BF16)
        dv_ref[:, cols] += join(d_v)
        dk_ref[:, cols] += scale * join(d_k)
        dek_ref[row_start : row_start + seq_len + height, cols] += scale * join(d_rel_k)
        for block in range(seq_len // LANES):
            start = seq_len - LANES - LANES * block + height * at
            back = turn_back(anti_keys, join([d_k_turned[0][block], d_k_turned[1][block]]))
            dk_ref[block * LANES : (block + 1) * LANES, cols] += scale * back
            deq_ref[start : start + LANES + height, cols] += scale * join(
                [d_rel_q[0][block], d_rel_q[1][block]]
            )
    if last:
        dk_low_ref, dv_low_ref = refs[5:]
        dk_low_ref[...] = dk_ref[...].astype(BF16)
        dv_low_ref[...] = dv_ref[...].astype(BF16)


def attend_back(line, at, height, last, d_ctx, q, k, v, eq, ek, att, carried):
    seq_len, cols = q.shape
    operands = [d_ctx, q, k, v, eq, ek, att, *carried]
    outs = [
        sds((height, cols), BF16),
        sds((seq_len, cols), F32),
        sds((seq_len, cols), F32),
        sds((2 * seq_len, cols), F32),
        sds((2 * seq_len, cols), F32),
    ]
    if last:
        outs += [sds((seq_len, cols), BF16)] * 2
    return line.call(
        functools.partial(attend_back_kernel, at, height, not carried, last), f"attend_back_{at}",
        outs, operands, aliases={7: 1, 8: 2, 9: 3, 10: 4} if carried else {}, flops=BACK_FLOPS,
    )


def feed_kernel(
    at, height, ctx_a_ref, ctx_b_ref, wout_ref, bout_ref, hidden_ref, gain_ref, shift_ref,
    win_ref, bin_ref, wdown_ref,
    xhat_ref, rstd_ref, normed_ref, act_ref, slope_ref, low_ref,
):
    own, other = ctx_a_ref[...], ctx_b_ref[...]
    first = lax.axis_index("head") == 0
    ctx = jnp.concatenate([jnp.where(first, own, other), jnp.where(first, other, own)], axis=1)
    ctx = ctx.astype(BF16)
    mixed = dot_nn(ctx, wout_ref[...])
    hidden = hidden_ref[at * height : (at + 1) * height].astype(F32)
    resid = mixed + bout_ref[...].astype(F32)[None, :] + hidden
    center = resid - jnp.mean(resid, axis=-1, keepdims=True)
    spread = jnp.mean(center * center, axis=-1, keepdims=True)
    rstd = lax.rsqrt(spread + EPSILON)
    xhat = center * rstd
    xhat_ref[...] = xhat
    rstd_ref[...] = rstd
    normed = xhat * gain_ref[...].astype(F32)[None, :] + shift_ref[...].astype(F32)[None, :]
    low = normed.astype(BF16)
    normed_ref[...] = low
    units = win_ref.shape[1]
    step = units // 3
    total = None
    bias = bin_ref[...].astype(F32)[None, :]
    for part in range(3):
        cols = slice(part * step, (part + 1) * step)
        inner = dot_nn(low, win_ref[:, cols]) + bias[:, cols]
        phi = 0.5 * (1.0 + lax.erf(inner * math.sqrt(0.5)))
        act = (inner * phi).astype(BF16)
        slope = phi + inner * (jnp.exp(-0.5 * inner * inner) * (1.0 / math.sqrt(2 * math.pi)))
        act_ref[:, cols] = act
        slope_ref[:, cols] = slope
        term = dot_nn(act, wdown_ref[cols, :])
        total = term if total is None else total + term
    low_ref[...] = total


def feed(line, at, height, ctx_a, ctx_b, wout, bout, hidden, gain, shift, win, b_in, wdown):
    width = hidden.shape[1]
    units = win.shape[1]
    outs = [
        sds((height, width), F32),
        sds((height, 1), F32),
        sds((height, width), BF16),
        sds((height, units), BF16),
        sds((height, units), F32),
        sds((height, width), F32),
    ]
    operands = (ctx_a, ctx_b, wout, bout, hidden, gain, shift, win, b_in, wdown)
    return line.call(
        functools.partial(feed_kernel, at, height), f"feed_{at}", outs, operands,
        flops=BACK_FLOPS if at else 1024,
    )


def feed_back_kernel(
    at, height, low_own_ref, low_other_ref, xhat_one_ref, gain_one_ref, shift_one_ref, bdown_ref,
    gain_ref, shift_ref, cot_ref, slope_ref, win_ref, wdown_ref,
    out_ref, d_two_ref, d_low_ref, d_inner_ref, dn_ref, vec_ref, bin_ref,
):
    normed = xhat_one_ref[...] * gain_one_ref[...].astype(F32)[None, :]
    normed = normed + shift_one_ref[...].astype(F32)[None, :]
    resid = (low_own_ref[...] + low_other_ref[...]) + bdown_ref[...].astype(F32)[None, :] + normed
    center = resid - jnp.mean(resid, axis=-1, keepdims=True)
    spread = jnp.mean(center * center, axis=-1, keepdims=True)
    rstd = lax.rsqrt(spread + EPSILON)
    xhat = center * rstd
    gain = gain_ref[...].astype(F32)[None, :]
    out_ref[...] = (xhat * gain + shift_ref[...].astype(F32)[None, :]).astype(BF16)
    err = cot_ref[at * height : (at + 1) * height].astype(F32)
    vec_ref[0:1, :] = jnp.sum(err * xhat, axis=0, keepdims=True)
    vec_ref[1:2, :] = jnp.sum(err, axis=0, keepdims=True)
    scaled = err * gain
    mean_a = jnp.mean(scaled, axis=-1, keepdims=True)
    mean_b = jnp.mean(scaled * xhat, axis=-1, keepdims=True)
    d_two = rstd * (scaled - mean_a - xhat * mean_b)
    d_two_ref[...] = d_two
    vec_ref[2:3, :] = jnp.sum(d_two, axis=0, keepdims=True)
    low = d_two.astype(BF16)
    d_low_ref[...] = low
    units = win_ref.shape[1]
    step = units // 3
    total = None
    for part in range(3):
        cols = slice(part * step, (part + 1) * step)
        d_act = dot_nt(low, wdown_ref[cols, :])
        d_inner = (d_act * slope_ref[:, cols]).astype(BF16)
        d_inner_ref[:, cols] = d_inner
        bin_ref[0:1, cols] = jnp.sum(d_inner.astype(F32), axis=0, keepdims=True)
        term = dot_nt(d_inner, win_ref[:, cols])
        total = term if total is None else total + term
    dn_ref[...] = total


def feed_back(
    line, at, height, low_own, low_other, xhat, gain_one, shift_one, bdown, gain, shift, cot, slope, win,
    wdown,
):
    width = cot.shape[1]
    units = win.shape[1]
    outs = [
        sds((height, width), BF16),
        sds((height, width), F32),
        sds((height, width), BF16),
        sds((height, units), BF16),
        sds((height, width), F32),
        sds((8, width), F32),
        sds((8, units), F32),
    ]
    operands = (
        low_own, low_other, xhat, gain_one, shift_one, bdown, gain, shift, cot, slope, win, wdown
    )
    return line.call(
        functools.partial(feed_back_kernel, at, height), f"feed_back_{at}", outs, operands
    )


def spread(order, me, total, kept_ref, sent_ref, cols):
    parts = 1 << len(order)
    height = total.shape[0] // parts
    for bit in (0, order[0]):

        @pl.when((me & order[0]) == bit)
        def _(bit=bit):
            for block in range(parts):
                origin = me ^ block
                place = 0
                for later in order[1:]:
                    place = 2 * place + ((origin >> (later.bit_length() - 1)) & 1)
                target = kept_ref if block & order[0] == bit else sent_ref
                target[place, :, cols] = total[block * height : (block + 1) * height]


def grad_kernel(order, groups, *refs):
    kept_ref, sent_ref = refs[-2:]
    me = lax.axis_index("dp")
    at, start = 0, 0
    for count in groups:
        total = None
        for _ in range(count):
            left, right = refs[at][...], refs[at + 1][...].astype(BF16)
            at += 2
            term = dot_tn(left, right)
            total = term if total is None else total + term
        cols = slice(start, start + total.shape[1])
        start += total.shape[1]
        spread(order, me, total, kept_ref, sent_ref, cols)


def grad_blocks(line, name, order, groups):
    parts = 1 << len(order)
    width = groups[0][0][0].shape[1]
    cols = sum(group[0][1].shape[1] for group in groups)
    operands = [array for group in groups for term in group for array in term]
    counts = [len(group) for group in groups]
    outs = [sds((parts // 2, width // parts, cols), F32)] * 2
    return line.call(
        functools.partial(grad_kernel, order, counts), name, outs, operands
    )


def rel_kernel(
    order, streams, table_rows, bucket_ref, deq_ref, dek_ref, wq_ref, wk_ref, dk_ref, dv_ref,
    *refs,
):
    dq_refs, refs = refs[:streams], refs[streams:]
    one_refs, refs = refs[:streams], refs[streams:]
    two_refs, refs = refs[:streams], refs[streams:]
    unit_refs, refs = refs[:streams], refs[streams:]
    relq_ref, relk_ref, kept_ref, sent_ref, pack_ref = refs
    onehot = onehot_of(bucket_ref, table_rows)
    deq, dek = deq_ref[...], dek_ref[...]
    d_rel_q = dot_nn(onehot, deq.astype(BF16)).astype(BF16)
    d_rel_k = dot_nn(onehot, dek.astype(BF16)).astype(BF16)
    relq_ref[...] = d_rel_q
    relk_ref[...] = d_rel_k
    total = dot_nt(d_rel_q, wq_ref[...]) + dot_nt(d_rel_k, wk_ref[...])
    width = total.shape[1]
    me = lax.axis_index("dp")
    spread(order, me, total, kept_ref, sent_ref, slice(0, width))

    def summed(value):
        return jnp.sum(value.astype(F32), axis=0, keepdims=True)

    def over(stream_refs):
        value = stream_refs[0][...]
        for ref in stream_refs[1:]:
            value = value + ref[...]
        return value

    one, two, unit = over(one_refs), over(two_refs), over(unit_refs)
    d_bias = summed(dq_refs[0][...])
    for ref in dq_refs[1:]:
        d_bias = d_bias + summed(ref[...])
    vectors = [
        d_bias + summed(deq),
        summed(dk_ref[...]) + summed(dek),
        summed(dv_ref[...]),
        one[2:3], one[0:1], one[1:2], unit[0:1], two[2:3], two[0:1], two[1:2],
    ]
    pack_ref[...] = jnp.zeros_like(pack_ref)
    row = 0
    for vector in vectors:
        for piece in range(vector.shape[1] // LANES):
            pack_ref[row : row + 1, :] = vector[:, piece * LANES : (piece + 1) * LANES]
            row += 1
    spread(order, me, pack_ref[...], kept_ref, sent_ref, slice(width, width + LANES))


def rel_grads(line, order, span, buckets, deq, dek, wq, wk, dk, dv, dq, one, two, unit):
    width, cols = wq.shape
    outs = [sds((span, cols), BF16)] * 2
    parts = 1 << len(order)
    outs = outs + [sds((parts // 2, span // parts, width + LANES), F32)] * 2
    operands = [buckets, deq, dek, wq, wk, dk, dv, *dq, *one, *two, *unit]
    return line.call(
        functools.partial(rel_kernel, order, len(dq), span), "rel_grads", outs, operands,
        scratch=[pltpu.VMEM((span, LANES), F32)],
    )


def rel_join_kernel(own_ref, other_ref, vector_ref, out_ref):
    width = own_ref.shape[1]
    out_ref[0, :, :width] = own_ref[...] + other_ref[...]
    out_ref[0, :, width:] = vector_ref[...]


def rel_join(line, own, other, vector):
    rows, width = own.shape
    outs = [sds((1, rows, width + vector.shape[1]), F32)]
    return line.call(rel_join_kernel, "rel_join", outs, (own, other, vector))[0]


def hidden_join_kernel(own_ref, other_ref, *refs):
    out_ref = refs[-1]
    start = 0
    for ref in refs[:-1]:
        rows = slice(start, start + ref.shape[0])
        out_ref[rows] = ((own_ref[rows] + other_ref[rows]) + ref[...]).astype(BF16)
        start += ref.shape[0]


def hidden_join(line, own, other, d_one):
    outs = [sds(own.shape, BF16)]
    return line.call(hidden_join_kernel, "hidden_join", outs, (own, other, *d_one))[0]


def unpack_kernel(origins, count, *refs):
    shared_refs, (table_ref, *vector_refs) = refs[:count], refs[count:]
    width = table_ref.shape[2]
    height = table_ref.shape[1]
    me = lax.axis_index("dp")
    places = [(ref, at) for ref in shared_refs for at in range(ref.shape[0])]
    rows = sum(ref.shape[0] for ref in vector_refs) // LANES
    lines = [
        (ref, piece) for ref in vector_refs for piece in range(ref.shape[0] // LANES)
    ]
    for (shared_ref, at), origin in zip(places, origins, strict=True):
        table_ref[me ^ origin] = shared_ref[at, :, :width]
        for block in range((rows + height - 1) // height):

            @pl.when(me ^ origin == block)
            def _(shared_ref=shared_ref, at=at, block=block):
                for row in range(block * height, min(rows, (block + 1) * height)):
                    ref, piece = lines[row]
                    inner = row % height
                    line = shared_ref[at, inner : inner + 1, width:]
                    ref[pl.ds(piece * LANES, LANES)] = line.reshape(LANES)


def unpack(line, origins, pieces, sizes):
    height, wide = pieces[0].shape[1:]
    outs = [sds((len(origins), height, wide - LANES), F32)] + [sds((size,), F32) for size in sizes]
    return line.call(
        functools.partial(unpack_kernel, origins, len(pieces)), "unpack", outs, pieces
    )


def hidden_kernel(streams, dk_ref, dv_ref, wq_ref, wk_ref, wv_ref, *refs):
    out_ref = refs[-1]
    out_ref[...] = dot_nt(dk_ref[...], wk_ref[...]) + dot_nt(dv_ref[...], wv_ref[...])
    height = out_ref.shape[0] // streams
    for at in range(streams):
        out_ref[at * height : (at + 1) * height] += dot_nt(refs[at][...], wq_ref[...])


def hidden_grad(line, dk, dv, wq, wk, wv, dq):
    out = sds((dk.shape[0], wq.shape[0]), F32)
    (total,) = line.call(
        functools.partial(hidden_kernel, len(dq)), "hidden_grad", [out], (dk, dv, wq, wk, wv, *dq)
    )
    return total


def bits_of(parts):
    return [1 << b for b in range(parts.bit_length() - 1)]


def swap_head(value):
    return lax.ppermute(value, "head", [(0, 1), (1, 0)])


def flip(value, parts, bit):
    return lax.ppermute(value, "dp", [(i, i ^ bit) for i in range(parts)])


def together(*values):
    return lax.optimization_barrier(values)


def step_kernel(kept_ref, arrived_ref, kept_out, sent_out):
    half = kept_out.shape[0]
    kept_out[...] = kept_ref[:half] + arrived_ref[:half]
    sent_out[...] = kept_ref[half:] + arrived_ref[half:]


class Scatter:
    def __init__(self, line, name, kept, sent, order):
        self.line, self.name, self.order = line, name, list(order)
        self.parts = 1 << len(self.order)
        self.kept = kept
        self.send(sent)

    def send(self, sent):
        self.bit = self.order.pop(0)
        self.arrived = flip(sent, self.parts, self.bit)

    def step(self):
        shape = (self.kept.shape[0] // 2, *self.kept.shape[1:])
        self.kept, sent = self.line.call(
            step_kernel, f"{self.name}_{self.bit}", [sds(shape, F32)] * 2,
            (self.kept, self.arrived),
        )
        self.send(sent)

    def rest(self):
        while self.order:
            self.step()

    def finish(self, widths):
        def kernel(kept_ref, arrived_ref, *out_refs):
            start = 0
            for ref in out_refs:
                cols = slice(start, start + ref.shape[1])
                ref[...] = kept_ref[0, :, cols] + arrived_ref[0, :, cols]
                start += ref.shape[1]

        rows = self.kept.shape[1]
        return self.line.call(
            kernel, f"{self.name}_sum", [sds((rows, width), F32) for width in widths],
            (self.kept, self.arrived),
        )


def pack_kernel(*refs):
    start = 0
    for ref in refs[:-1]:
        refs[-1][start : start + ref.shape[0]] = ref[...]
        start += ref.shape[0]


class Gather:
    def __init__(self, line, value, parts, order):
        self.line, self.parts, self.order = line, parts, list(order)
        self.pieces, self.origins = [value], [0]
        self.send(value)

    def send(self, sent):
        bit = self.order.pop(0)
        self.pieces.append(flip(sent, self.parts, bit))
        self.origins = self.origins + [origin ^ bit for origin in self.origins]

    def step(self):
        if self.order:
            shape = (len(self.origins), *self.pieces[0].shape[1:])
            (sent,) = self.line.call(
                pack_kernel, f"pack_{len(self.origins)}", [sds(shape, F32)], self.pieces
            )
            self.send(sent)

    def rest(self):
        while self.order:
            self.step()


def on_device(parts, *arguments):
    (
        hidden_in, lengths, cotangent, w_query, b_query, w_key, b_key, w_value, b_value,
        w_out, b_out, ln1_gain, ln1_bias, w_in, b_in, w_down, b_down, ln2_gain, ln2_bias,
        rel_table,
    ) = arguments
    seq_len, width = hidden_in.shape
    height = seq_len // STREAMS
    streams = range(STREAMS)
    me = lax.axis_index("dp").astype(jnp.int32).reshape(1)
    bits = bits_of(parts)

    half = w_out.shape[0] // 2
    odd = lax.rem(me, 2)
    buckets = jnp.asarray(distance_buckets(seq_len)[None, :])
    mine = lax.dynamic_slice_in_dim(w_out, odd[0] * half, half, 0).astype(F32)
    fetched = swap_head(mine)
    line = Line()
    q, k, v, eq, ek = project(
        line, buckets, hidden_in, w_query, b_query, w_key, b_key, w_value, b_value, rel_table
    )
    contexts, attends = [], []
    for at in streams:
        context, attended = attend(line, at, height, lengths, q, k, v, eq, ek)
        contexts.append(context)
        attends.append(attended)
    fetched, contexts[0] = together(fetched, contexts[0])
    paired = flip(fetched, parts, 1)
    w_out_all = assemble(line, w_out, fetched, paired)
    fed = [
        feed(
            line, at, height, contexts[at], swap_head(contexts[at]), w_out_all, b_out,
            hidden_in, ln1_gain, ln1_bias, w_in, b_in, w_down,
        )
        for at in streams
    ]
    backs = []
    for at in streams:
        xhat, rstd, normed, act, slope, lowered = fed[at]
        backs.append(
            feed_back(
                line, at, height, lowered, swap_head(lowered), xhat, ln1_gain, ln1_bias, b_down,
                ln2_gain, ln2_bias, cotangent, slope, w_in, w_down,
            )
        )
    crossed = bits[:1] + bits[2:] + bits[1:2]
    g_down = grad_blocks(
        line, "grad_down", bits, [[(backs[at][2], fed[at][3]) for at in streams]]
    )
    down = Scatter(line, "down", *g_down, bits)
    g_in = grad_blocks(
        line, "grad_in", crossed, [[(fed[at][2], backs[at][3]) for at in streams]]
    )
    inner = Scatter(line, "inner", *g_in, crossed)
    norms, attn_backs = [], []
    carried = ()
    for at in streams:
        xhat, rstd = fed[at][:2]
        d_two, dn = backs[at][1], backs[at][4]
        norms.append(
            norm_back(line, at, dn, swap_head(dn), d_two, xhat, rstd, ln1_gain, w_out)
        )
        if at == 0:
            down.step()
            inner.step()
        attn_backs.append(
            attend_back(
                line, at, height, at == streams[-1], norms[at][2], q, k, v, eq, ek, attends[at],
                carried,
            )
        )
        carried = attn_backs[at][1:5]
    dk, dv = attn_backs[-1][5:]
    deq, dek = carried[2:]
    dq = [a[0] for a in attn_backs]
    output = jnp.concatenate([b[0] for b in backs], axis=0)
    relq, relk, *rel_all = rel_grads(
        line, bits, rel_table.shape[0], buckets, deq, dek, w_query, w_key, dk, dv, dq,
        [n[3] for n in norms], [b[5] for b in backs], [b[6] for b in backs],
    )
    rel = Scatter(line, "rel", *rel_all, bits)
    hidden_parts = [hidden_in[at * height : (at + 1) * height] for at in streams]
    g_vo = grad_blocks(
        line, "grad_value_out", bits,
        [
            [(hidden_in, dv)],
            [(norms[at][1], contexts[at]) for at in streams],
        ],
    )
    value_out = Scatter(line, "value_out", *g_vo, bits)
    g_qk = grad_blocks(
        line, "grad_query_key", bits,
        [
            [*zip(hidden_parts, dq, strict=True), (rel_table, relq)],
            [(hidden_in, dk), (rel_table, relk)],
        ],
    )
    query_key = Scatter(line, "query_key", *g_qk, bits)
    d_hidden = hidden_grad(line, dk, dv, w_query, w_key, w_value, dq)
    d_hidden_other = swap_head(d_hidden)
    down.step()
    inner.step()
    rel.step()
    value_out.step()
    query_key.step()
    rel.step()
    down.step()
    rel.step()
    value_out.step()
    inner.step()
    rel.rest()
    rel_own, vectors = rel.finish([width, LANES])
    rel_other = swap_head(rel_own)
    query_key.step()
    shared = Gather(line, rel_join(line, rel_own, rel_other, vectors), parts, bits[::-1])
    down.rest()
    (s_down,) = down.finish([w_in.shape[1]])
    value_out.rest()
    shared.step()
    query_key.rest()
    inner.rest()
    (s_in,) = inner.finish([w_in.shape[1]])
    shared.step()
    grad_input = hidden_join(line, d_hidden, d_hidden_other, [n[0] for n in norms])
    cols = q.shape[1]
    s_v, s_out = value_out.finish([cols, cols])
    s_q, s_k = query_key.finish([cols, cols])
    shared.rest()
    sizes = [cols] * 3 + [width] * 3 + [w_in.shape[1]] + [width] * 3
    table_blocks, *pieces = unpack(line, shared.origins, shared.pieces, sizes)
    grad_rel_table = table_blocks.reshape(rel_table.shape)
    (
        grad_b_query, grad_b_key, grad_b_value, grad_b_out, grad_ln1_gain, grad_ln1_bias,
        grad_b_in, grad_b_down, grad_ln2_gain, grad_ln2_bias,
    ) = pieces
    return (
        output, grad_input, s_q, grad_b_query, s_k, grad_b_key, s_v, grad_b_value,
        s_out.T, grad_b_out, grad_ln1_gain, grad_ln1_bias, s_in, grad_b_in,
        s_down.T, grad_b_down, grad_ln2_gain, grad_ln2_bias, grad_rel_table,
    )


def solution(mesh):
    parts = mesh.shape["dp"]
    return jax.shard_map(
        functools.partial(on_device, parts),
        mesh=mesh,
        in_specs=(
            P("dp", None), P("dp"), P("dp", None),
            P(None, "head"), P("head"), P(None, "head"), P("head"), P(None, "head"), P("head"),
            P("head", None), P(), P(), P(),
            P(None, "head"), P("head"), P("head", None), P(), P(), P(), P(),
        ),
        out_specs=(
            P("dp", None), P("dp", None),
            P("dp", "head"), P("head"), P("dp", "head"), P("head"), P("dp", "head"), P("head"),
            P("head", "dp"), P(), P(), P(),
            P("dp", "head"), P("head"), P("head", "dp"), P(), P(), P(), P(),
        ),
        check_vma=False,
    )
```

```python
import functools
import math

import jax
import jax.numpy as jnp
import numpy as np
from jax import lax
from jax.experimental import pallas as pl
from jax.experimental.pallas import tpu as pltpu
from jax.sharding import PartitionSpec as P

HEAD_DIM = 64
SPAN = 256
MAXPOS = 512
EPSILON = 1e-07
MASKED = -1000000000.0
LANES = 128
STREAMS = 2
CONTEXTS = 1
TAIL = "LGKYDIRVQRDXVISQJiQqPVHdPv"
REL_PIECES = 1
HEAD_PIECES = 1
QUARTERS = 4
COLUMNS = 384
BACK_FLOPS = 64 << 30
REL_FLOPS = 1024
STEP_FLOPS = 1024
GRAD_FLOPS = 1024
VMEM_LIMIT = 8 * 1024 * 1024

BF16 = jnp.bfloat16
F32 = jnp.float32


def bucket_of(offsets, bucket_span, max_distance):
    middle = bucket_span // 2
    direction = np.sign(offsets)
    absolute = np.where((offsets < middle) & (offsets > -middle), middle - 1, np.abs(offsets))
    log_part = (
        np.ceil(np.log(absolute / middle) / np.log((max_distance - 1) / middle) * (middle - 1))
        + middle
    )
    bucket = np.where(absolute <= middle, offsets, log_part * direction).astype(np.int64)
    return np.clip(bucket + bucket_span, 0, 2 * bucket_span - 1).astype(np.int32)


def distance_buckets(seq_len):
    offsets = np.maximum(seq_len - 1 - np.arange(2 * seq_len), 1 - seq_len)
    return bucket_of(offsets, SPAN, MAXPOS)


def dot_nn(a, b):
    return lax.dot_general(a, b, (((1,), (0,)), ((), ())), preferred_element_type=F32)


def dot_nt(a, b):
    return lax.dot_general(a, b, (((1,), (1,)), ((), ())), preferred_element_type=F32)


def dot_tn(a, b):
    return lax.dot_general(a, b, (((0,), (0,)), ((), ())), preferred_element_type=F32)


class Line:
    def __init__(self):
        self.last = ()

    def call(
        self, kernel, name, outs, operands, aliases=None, scalars=0, scratch=(), flops=1024,
        space=pltpu.VMEM, direct=(),
    ):
        in_specs = [pl.BlockSpec(memory_space=pltpu.SMEM)] * scalars
        in_specs += [pl.BlockSpec(memory_space=space)] * (len(operands) - scalars)
        in_specs += [pl.BlockSpec(memory_space=pl.ANY)] * len(self.last)
        count, skipped = len(operands), len(self.last)

        def body(*refs):
            kernel(*refs[:count], *refs[count + skipped :])

        results = pl.pallas_call(
            body,
            in_specs=in_specs,
            out_specs=[
                pl.BlockSpec() if at in direct else pl.BlockSpec(memory_space=pltpu.VMEM)
                for at in range(len(outs))
            ],
            out_shape=outs,
            scratch_shapes=list(scratch),
            input_output_aliases=aliases or {},
            compiler_params=pltpu.CompilerParams(vmem_limit_bytes=VMEM_LIMIT),
            cost_estimate=pl.CostEstimate(flops=flops, bytes_accessed=1024, transcendentals=0),
            name=name,
        )(*operands, *self.last)
        self.last = (min(results, key=lambda result: result.size * result.dtype.itemsize),)
        return results


def sds(shape, dtype):
    return jax.ShapeDtypeStruct(shape, dtype)


def onehot_of(bucket_ref, span):
    buckets = bucket_ref[...]
    hot = buckets == lax.broadcasted_iota(jnp.int32, (span, buckets.shape[1]), 0)
    return jnp.where(hot, 1.0, 0.0).astype(BF16)


def project_kernel(
    bucket_hbm, hidden_hbm, wq_hbm, bq_hbm, wk_hbm, bk_hbm, wv_hbm, bv_hbm, table_hbm, wout_hbm,
    q_ref, k_ref, v_ref, eq_ref, ek_ref, mine_ref,
    bucket_ref, hidden_ref, wq_ref, bq_ref, wk_ref, bk_ref, wv_ref, bv_ref, table_ref, quarter_ref,
    sems,
):
    rows = quarter_ref.shape[0]
    first = pl.multiple_of(lax.rem(lax.axis_index("dp"), QUARTERS) * rows, rows)
    sources = (
        wout_hbm.at[pl.ds(first, rows)], hidden_hbm, wq_hbm, bq_hbm, wk_hbm, bk_hbm, wv_hbm, bv_hbm, table_hbm, bucket_hbm
    )
    targets = (
        quarter_ref, hidden_ref, wq_ref, bq_ref, wk_ref, bk_ref, wv_ref, bv_ref, table_ref, bucket_ref
    )
    copies = [
        pltpu.make_async_copy(source, target, sems.at[at])
        for at, (source, target) in enumerate(zip(sources, targets, strict=True))
    ]
    for copy in copies:
        copy.start()

    def need(count):
        for copy in copies[:count]:
            copy.wait()
        del copies[:count]

    def biased(rows, weight_ref, bias_ref):
        return (dot_nn(rows, weight_ref[...]) + bias_ref[...].astype(F32)[None, :]).astype(BF16)

    need(1)
    mine_ref[...] = quarter_ref[...].astype(F32)
    need(3)
    hidden = hidden_ref[...]
    q_ref[...] = biased(hidden, wq_ref, bq_ref)
    need(2)
    k_ref[...] = biased(hidden, wk_ref, bk_ref)
    need(2)
    v_ref[...] = biased(hidden, wv_ref, bv_ref)
    need(2)
    table = table_ref[...]
    onehot = onehot_of(bucket_ref, table.shape[0])
    eq_ref[...] = dot_tn(onehot, biased(table, wq_ref, bq_ref)).astype(BF16)
    ek_ref[...] = dot_tn(onehot, biased(table, wk_ref, bk_ref)).astype(BF16)


def project(line, buckets, hidden, wq, bq, wk, bk, wv, bv, table, wout):
    seq_len = hidden.shape[0]
    cols = wq.shape[1]
    rows = wout.shape[0] // QUARTERS
    outs = [sds((seq_len, cols), BF16)] * 3 + [sds((2 * seq_len, cols), BF16)] * 2
    outs += [sds((rows, wout.shape[1]), F32)]
    operands = (buckets, hidden, wq, bq, wk, bk, wv, bv, table, wout)
    scratch = [pltpu.VMEM(operand.shape, operand.dtype) for operand in operands[:-1]]
    scratch += [pltpu.VMEM((rows, wout.shape[1]), wout.dtype)]
    operands = [pltpu.with_memory_space_constraint(operand, pltpu.HBM) for operand in operands]
    scratch += [pltpu.SemaphoreType.DMA((len(operands),))]
    return line.call(
        project_kernel, "project", outs, operands, scratch=scratch, space=pltpu.HBM
    )


def assemble_kernel(own_ref, *refs):
    out_ref = refs[-1]
    side, me = lax.axis_index("head"), lax.rem(lax.axis_index("dp"), QUARTERS)
    out_ref[side] = own_ref[...]
    for origin, ref in enumerate(refs[:-1]):
        rows = ref.shape[0]
        first = pl.multiple_of((me ^ origin) * rows, rows)
        out_ref[1 - side, pl.ds(first, rows), :] = ref[...].astype(BF16)


def assemble(line, own, quarters):
    rows, width = own.shape
    out = sds((2, rows, width), BF16)
    (joined,) = line.call(assemble_kernel, "assemble", [out], (own, *quarters))
    return joined.reshape(2 * rows, width)


def half_masks():
    lane = lax.broadcasted_iota(jnp.int32, (1, LANES), 1)
    return [lane // HEAD_DIM == side for side in range(LANES // HEAD_DIM)]


def apart(masks, value):
    zero = jnp.zeros_like(value)
    return jnp.concatenate([jnp.where(mask, value, zero) for mask in masks], axis=0)


def join(masks, stacked):
    rows = stacked.shape[0] // 2
    return jnp.where(masks[0], stacked[:rows], stacked[rows:])


def skewed(stacked, shift):
    rows = stacked.shape[0] // 2
    parts = [
        pltpu.roll(part, shift, 1, stride=1, stride_axis=0)
        for part in (stacked[:rows], stacked[rows:])
    ]
    return jnp.concatenate(parts, axis=0)


def attend_kernel(at, height, len_ref, q_ref, k_ref, v_ref, eq_ref, ek_ref, ctx_ref, att_ref):
    seq_len = k_ref.shape[0]
    length = len_ref[0]
    scale = 1.0 / math.sqrt(3 * HEAD_DIM)
    masks = half_masks()
    key_valid = lax.broadcasted_iota(jnp.int32, (1, seq_len), 1) < length
    rows = at * height + lax.broadcasted_iota(jnp.int32, (height, 1), 0)
    rows = jnp.concatenate([rows, rows], axis=0)
    query_valid = rows < length
    row_start = seq_len - height - height * at
    @pl.loop(0, q_ref.shape[1] // LANES)
    def _(pair):
        cols = pl.ds(pl.multiple_of(pair * LANES, LANES), LANES)
        q_pair = q_ref[at * height : (at + 1) * height, cols]
        k_pair = k_ref[:, cols]
        v_pair = v_ref[:, cols]
        rel_window = ek_ref[row_start : row_start + seq_len + height, cols]
        q_two = apart(masks, q_pair)
        content = dot_nt(q_two, k_pair)
        picked = skewed(dot_nt(q_two, rel_window), seq_len + 1)[:, :seq_len]
        blocks = []
        for block in range(seq_len // LANES):
            start = seq_len - LANES - LANES * block + height * at
            window = eq_ref[start : start + LANES + height, cols]
            k_two = apart(masks, k_pair[block * LANES : (block + 1) * LANES])
            tall = skewed(dot_nt(k_two, window), height + 1)[:, :height]
            blocks.append(jnp.concatenate([tall[:LANES].T, tall[LANES:].T], axis=0))
        flipped = jnp.concatenate(blocks, axis=1)
        scores = jnp.where(key_valid, scale * (content + picked + flipped), MASKED)
        peak = jnp.max(scores, axis=-1, keepdims=True)
        weight = jnp.exp(scores - peak)
        total = jnp.sum(weight, axis=-1, keepdims=True)
        keep = jnp.where(query_valid, 1.0 / total, 0.0)
        attend = (weight * keep).astype(BF16)
        att_ref[2 * pair] = attend[:height]
        att_ref[2 * pair + 1] = attend[height:]
        ctx_ref[:, cols] = join(masks, dot_nn(attend, v_pair)).astype(BF16).astype(F32)


def attend(line, at, height, lengths, q, k, v, eq, ek):
    seq_len, cols = q.shape
    heads = cols // HEAD_DIM
    outs = [sds((height, cols), F32), sds((heads, height, seq_len), BF16)]
    return line.call(
        functools.partial(attend_kernel, at, height), f"attend_{at}", outs,
        (lengths, q, k, v, eq, ek), scalars=1,
    )


def norm_back_kernel(
    start, dn_own_ref, dn_other_ref, d_two_ref, xhat_ref, rstd_ref, gain_ref, wout_ref,
    d_one_ref, d_mixed_ref, d_ctx_ref, vec_ref,
):
    rows = slice(start, start + dn_own_ref.shape[0])
    d_normed = (dn_own_ref[...] + dn_other_ref[...]) + d_two_ref[rows]
    xhat = xhat_ref[rows]
    vec_ref[0:1, :] = jnp.sum(d_normed * xhat, axis=0, keepdims=True)
    vec_ref[1:2, :] = jnp.sum(d_normed, axis=0, keepdims=True)
    scaled = d_normed * gain_ref[...].astype(F32)[None, :]
    mean_a = jnp.mean(scaled, axis=-1, keepdims=True)
    mean_b = jnp.mean(scaled * xhat, axis=-1, keepdims=True)
    d_one = rstd_ref[rows] * (scaled - mean_a - xhat * mean_b)
    d_one_ref[...] = d_one
    vec_ref[2:3, :] = jnp.sum(d_one, axis=0, keepdims=True)
    d_mixed = d_one.astype(BF16)
    d_mixed_ref[...] = d_mixed
    d_ctx_ref[...] = dot_nt(d_mixed, wout_ref[...]).astype(BF16)


def norm_back(line, at, start, dn_own, dn_other, d_two, xhat, rstd, gain, wout):
    height, width = dn_own.shape
    outs = [
        sds((height, width), F32),
        sds((height, width), BF16),
        sds((height, wout.shape[0]), BF16),
        sds((8, width), F32),
    ]
    operands = (dn_own, dn_other, d_two, xhat, rstd, gain, wout)
    return line.call(
        functools.partial(norm_back_kernel, start), f"norm_back_{at}", outs, operands,
        flops=BACK_FLOPS,
    )


def attend_back_kernel(
    at, height, count, first, last, d_ctx_ref, q_ref, k_ref, v_ref, eq_ref, ek_ref, *refs
):
    att_refs, refs = refs[:count], refs[count:]
    if not first:
        refs = refs[4:]
    dq_ref, dk_ref, dv_ref, deq_ref, dek_ref = refs[:5]
    seq_len = k_ref.shape[0]
    scale = 1.0 / math.sqrt(3 * HEAD_DIM)
    masks = half_masks()

    def anti(size):
        row = lax.broadcasted_iota(jnp.int32, (size, size), 0)
        col = lax.broadcasted_iota(jnp.int32, (size, size), 1)
        return jnp.where(row + col == size - 1, 1.0, 0.0).astype(BF16)

    anti_rows = anti(height)
    anti_keys = anti(LANES)
    row_start = seq_len - height - height * at
    if first:
        dk_ref[...] = jnp.zeros_like(dk_ref)
        dv_ref[...] = jnp.zeros_like(dv_ref)
        deq_ref[...] = jnp.zeros_like(deq_ref)
        dek_ref[...] = jnp.zeros_like(dek_ref)

    @pl.loop(0, q_ref.shape[1] // LANES)
    def _(pair):
        cols = pl.ds(pl.multiple_of(pair * LANES, LANES), LANES)
        q_pair = q_ref[at * height : (at + 1) * height, cols]
        k_pair = k_ref[:, cols]
        v_pair = v_ref[:, cols]
        ctx_pair = d_ctx_ref[:, cols]
        rel_window = ek_ref[row_start : row_start + seq_len + height, cols]
        q_turned = dot_nn(anti_rows, q_pair).astype(BF16)
        weight = jnp.concatenate(
            [jnp.concatenate([ref[2 * pair + side] for ref in att_refs], axis=0) for side in range(2)],
            axis=0,
        )
        d_att = dot_nt(apart(masks, ctx_pair), v_pair)
        soft = weight.astype(F32)
        inner = jnp.sum(d_att * soft, axis=-1, keepdims=True)
        d_scores = (soft * (d_att - inner)).astype(BF16)
        sides = [d_scores[:height], d_scores[height:]]
        weight_wide = jnp.concatenate([weight[:height], weight[height:]], axis=1)
        dv_ref[:, cols] += join(masks, dot_tn(weight_wide, ctx_pair))
        d_q = join(masks, dot_nn(d_scores, k_pair))
        d_scores_t = [side.T for side in sides]
        d_k = join(masks, dot_nn(jnp.concatenate(d_scores_t, axis=0), q_pair))
        turned = dot_nn(anti_rows, jnp.concatenate(sides, axis=1))
        space = jnp.zeros((height, height), F32)
        turned = [
            jnp.concatenate([turned[:, side * seq_len : (side + 1) * seq_len], space], axis=1)
            for side in range(2)
        ]
        turned = skewed(jnp.concatenate(turned, axis=0), 0).astype(BF16)
        d_q_turned = join(masks, dot_nn(turned, rel_window))
        turned_wide = jnp.concatenate([turned[:height], turned[height:]], axis=1)
        d_rel_k = join(masks, dot_tn(turned_wide, q_turned))
        dek_ref[row_start : row_start + seq_len + height, cols] += scale * d_rel_k

        def turn_back(matrix, value):
            high = value.astype(BF16)
            rest = (value - high.astype(F32)).astype(BF16)
            both = dot_nn(matrix, jnp.concatenate([high, rest], axis=1))
            return both[:, :LANES] + both[:, LANES:]

        dq_ref[:, cols] = (scale * (d_q + turn_back(anti_rows, d_q_turned))).astype(BF16)
        backs = []
        for block in range(seq_len // LANES):
            start = seq_len - LANES - LANES * block + height * at
            rows = slice(block * LANES, (block + 1) * LANES)
            window = eq_ref[start : start + LANES + height, cols]
            tall = dot_nn(anti_keys, jnp.concatenate([side[rows] for side in d_scores_t], axis=1))
            space = jnp.zeros((LANES, LANES), F32)
            tall = [
                jnp.concatenate([tall[:, side * height : (side + 1) * height], space], axis=1)
                for side in range(2)
            ]
            tall = skewed(jnp.concatenate(tall, axis=0), 0).astype(BF16)
            backs.append(join(masks, dot_nn(tall, window)))
            k_turned = apart(masks, dot_nn(anti_keys, k_pair[rows]).astype(BF16))
            deq_ref[start : start + LANES + height, cols] += scale * dot_tn(tall, k_turned)
        for block, value in enumerate(backs):
            rows = slice(block * LANES, (block + 1) * LANES)
            dk_ref[rows, cols] += scale * (d_k[rows] + turn_back(anti_keys, value))
    if last:
        dk_low_ref, dv_low_ref = refs[5:]
        dk_low_ref[...] = dk_ref[...].astype(BF16)
        dv_low_ref[...] = dv_ref[...].astype(BF16)


def attend_back(line, at, height, last, d_ctx, q, k, v, eq, ek, att, carried):
    seq_len, cols = q.shape
    operands = [d_ctx, q, k, v, eq, ek, *att, *carried]
    outs = [
        sds((height, cols), BF16),
        sds((seq_len, cols), F32),
        sds((seq_len, cols), F32),
        sds((2 * seq_len, cols), F32),
        sds((2 * seq_len, cols), F32),
    ]
    if last:
        outs += [sds((seq_len, cols), BF16)] * 2
    base = 6 + len(att)
    return line.call(
        functools.partial(attend_back_kernel, at, height, len(att), not carried, last),
        f"attend_back_{at}", outs, operands,
        aliases={base + place: 1 + place for place in range(4)} if carried else {},
        flops=BACK_FLOPS,
    )


def feed_kernel(
    at, height, count, wout_ref, bout_ref, hidden_ref, gain_ref, shift_ref, win_ref, bin_ref,
    wdown_ref, *refs,
):
    own_refs, other_refs = refs[:count], refs[count : 2 * count]
    xhat_ref, rstd_ref, normed_ref, act_ref, slope_ref, low_ref = refs[2 * count :]
    own = jnp.concatenate([ref[...] for ref in own_refs], axis=0)
    other = jnp.concatenate([ref[...] for ref in other_refs], axis=0)
    first = lax.axis_index("head") == 0
    ctx = jnp.concatenate([jnp.where(first, own, other), jnp.where(first, other, own)], axis=1)
    ctx = ctx.astype(BF16)
    mixed = dot_nn(ctx, wout_ref[...])
    hidden = hidden_ref[at * height : (at + 1) * height].astype(F32)
    resid = mixed + bout_ref[...].astype(F32)[None, :] + hidden
    center = resid - jnp.mean(resid, axis=-1, keepdims=True)
    spread = jnp.mean(center * center, axis=-1, keepdims=True)
    rstd = lax.rsqrt(spread + EPSILON)
    xhat = center * rstd
    xhat_ref[...] = xhat
    rstd_ref[...] = rstd
    normed = xhat * gain_ref[...].astype(F32)[None, :] + shift_ref[...].astype(F32)[None, :]
    low = normed.astype(BF16)
    normed_ref[...] = low
    units = win_ref.shape[1]
    step = units // 3
    total = None
    bias = bin_ref[...].astype(F32)[None, :]
    for part in range(3):
        cols = slice(part * step, (part + 1) * step)
        inner = dot_nn(low, win_ref[:, cols]) + bias[:, cols]
        phi = 0.5 * (1.0 + lax.erf(inner * math.sqrt(0.5)))
        act = (inner * phi).astype(BF16)
        slope = phi + inner * (jnp.exp(-0.5 * inner * inner) * (1.0 / math.sqrt(2 * math.pi)))
        act_ref[:, cols] = act
        slope_ref[:, cols] = slope
        term = dot_nn(act, wdown_ref[cols, :])
        total = term if total is None else total + term
    low_ref[...] = total


def feed(line, at, height, own, other, wout, bout, hidden, gain, shift, win, b_in, wdown):
    width = hidden.shape[1]
    units = win.shape[1]
    outs = [
        sds((height, width), F32),
        sds((height, 1), F32),
        sds((height, width), BF16),
        sds((height, units), BF16),
        sds((height, units), F32),
        sds((height, width), F32),
    ]
    operands = (wout, bout, hidden, gain, shift, win, b_in, wdown, *own, *other)
    return line.call(
        functools.partial(feed_kernel, at, height, len(own)), f"feed_{at}", outs, operands,
        flops=BACK_FLOPS if at else 1024,
    )


def feed_back_kernel(
    at, height, count, low_own_ref, low_other_ref, xhat_one_ref, gain_one_ref, shift_one_ref, bdown_ref,
    gain_ref, shift_ref, cot_ref, slope_ref, win_ref, wdown_ref,
    *refs,
):
    before, refs = refs[:count], refs[count:]
    out_ref, d_two_ref, d_low_ref, d_inner_ref, vec_ref, bin_ref, *dn_refs = refs
    normed = xhat_one_ref[...] * gain_one_ref[...].astype(F32)[None, :]
    normed = normed + shift_one_ref[...].astype(F32)[None, :]
    resid = (low_own_ref[...] + low_other_ref[...]) + bdown_ref[...].astype(F32)[None, :] + normed
    center = resid - jnp.mean(resid, axis=-1, keepdims=True)
    spread = jnp.mean(center * center, axis=-1, keepdims=True)
    rstd = lax.rsqrt(spread + EPSILON)
    xhat = center * rstd
    gain = gain_ref[...].astype(F32)[None, :]
    value = (xhat * gain + shift_ref[...].astype(F32)[None, :]).astype(BF16)
    if out_ref.shape[0] == height:
        out_ref[...] = value
    else:
        for stream, ref in enumerate(before):
            out_ref[stream * height : (stream + 1) * height] = ref[...]
        out_ref[at * height : (at + 1) * height] = value
    err = cot_ref[at * height : (at + 1) * height].astype(F32)
    vec_ref[0:1, :] = jnp.sum(err * xhat, axis=0, keepdims=True)
    vec_ref[1:2, :] = jnp.sum(err, axis=0, keepdims=True)
    scaled = err * gain
    mean_a = jnp.mean(scaled, axis=-1, keepdims=True)
    mean_b = jnp.mean(scaled * xhat, axis=-1, keepdims=True)
    d_two = rstd * (scaled - mean_a - xhat * mean_b)
    d_two_ref[...] = d_two
    vec_ref[2:3, :] = jnp.sum(d_two, axis=0, keepdims=True)
    low = d_two.astype(BF16)
    d_low_ref[...] = low
    units = win_ref.shape[1]
    step = units // 3
    total = None
    for part in range(3):
        cols = slice(part * step, (part + 1) * step)
        d_act = dot_nt(low, wdown_ref[cols, :])
        d_inner = (d_act * slope_ref[:, cols]).astype(BF16)
        d_inner_ref[:, cols] = d_inner
        bin_ref[0:1, cols] = jnp.sum(d_inner.astype(F32), axis=0, keepdims=True)
        term = dot_nt(d_inner, win_ref[:, cols])
        total = term if total is None else total + term
    rows = dn_refs[0].shape[0]
    for piece, ref in enumerate(dn_refs):
        ref[...] = total[piece * rows : (piece + 1) * rows]


def feed_back(
    line, at, height, rows, before, low_own, low_other, xhat, gain_one, shift_one, bdown, gain,
    shift, cot, slope, win, wdown,
):
    width = cot.shape[1]
    units = win.shape[1]
    last = (at + 1) * height == cot.shape[0]
    before = before if last else []
    outs = [
        sds(cot.shape if last else (height, width), BF16),
        sds((height, width), F32),
        sds((height, width), BF16),
        sds((height, units), BF16),
        sds((8, width), F32),
        sds((8, units), F32),
    ]
    outs += [sds((rows, width), F32)] * (height // rows)
    operands = (
        low_own, low_other, xhat, gain_one, shift_one, bdown, gain, shift, cot, slope, win, wdown,
        *before,
    )
    return line.call(
        functools.partial(feed_back_kernel, at, height, len(before)), f"feed_back_{at}", outs,
        operands, direct=(0,) if last else (),
    )


def spread(order, me, total, kept_ref, sent_refs, cols):
    parts = 1 << len(order)
    height = total.shape[0] // parts
    for bit in (0, order[0]):

        @pl.when((me & order[0]) == bit)
        def _(bit=bit):
            for block in range(parts):
                origin = me ^ block
                place = 0
                for later in order[1:]:
                    place = 2 * place + ((origin >> (later.bit_length() - 1)) & 1)
                top = block * height
                if block & order[0] == bit:
                    kept_ref[place, :, cols] = total[top : top + height]
                else:
                    for ref in sent_refs:
                        ref[place, :, cols] = total[top : top + ref.shape[1]]
                        top += ref.shape[1]


def grad_kernel(order, groups, pieces, *refs):
    kept_ref, *sent_refs = refs[-1 - pieces :]
    me = lax.axis_index("dp")
    at, start = 0, 0
    for count in groups:
        terms = []
        for rights in count:
            terms.append((refs[at], refs[at + 1 : at + 1 + rights]))
            at += 1 + rights
        width = terms[0][1][0].shape[1]

        def part(index, terms=terms, start=start):
            total = None
            columns = pl.ds(pl.multiple_of(index * COLUMNS, COLUMNS), COLUMNS)
            for left_ref, right_refs in terms:
                right = jnp.concatenate([ref[:, columns] for ref in right_refs], axis=0)
                term = dot_tn(left_ref[...], right.astype(BF16))
                total = term if total is None else total + term
            target = pl.ds(pl.multiple_of(start + index * COLUMNS, COLUMNS), COLUMNS)
            spread(order, me, total, kept_ref, sent_refs, target)

        pl.loop(0, width // COLUMNS)(part)
        start += width


def halves(order, rows, cols, pieces):
    half, height = (1 << len(order)) // 2, rows >> len(order)
    return [sds((half, height, cols), F32)] + [sds((half, height // pieces, cols), F32)] * pieces


def grad_blocks(line, name, order, groups, pieces=1):
    width = groups[0][0][0].shape[1]
    cols = sum(group[0][1][0].shape[1] for group in groups)
    operands = [array for group in groups for left, right in group for array in (left, *right)]
    counts = [[len(right) for _, right in group] for group in groups]
    outs = halves(order, width, cols, pieces)
    return line.call(
        functools.partial(grad_kernel, order, counts, pieces), name, outs, operands,
        flops=GRAD_FLOPS,
    )


def rel_kernel(
    order, counts, table_rows, bucket_ref, deq_ref, dek_ref, wq_ref, wk_ref, dk_ref, dv_ref,
    *refs,
):
    groups = []
    for count in counts:
        groups.append(refs[:count])
        refs = refs[count:]
    dq_refs, one_refs, two_refs, unit_refs = groups
    relq_ref, relk_ref, kept_ref, *sent_refs, pack_ref = refs
    onehot = onehot_of(bucket_ref, table_rows)
    deq, dek = deq_ref[...], dek_ref[...]
    d_rel_q = dot_nn(onehot, deq.astype(BF16)).astype(BF16)
    d_rel_k = dot_nn(onehot, dek.astype(BF16)).astype(BF16)
    relq_ref[...] = d_rel_q
    relk_ref[...] = d_rel_k
    total = dot_nt(d_rel_q, wq_ref[...]) + dot_nt(d_rel_k, wk_ref[...])
    width = total.shape[1]
    me = lax.axis_index("dp")
    spread(order, me, total, kept_ref, sent_refs, slice(0, width))

    def summed(value):
        return jnp.sum(value.astype(F32), axis=0, keepdims=True)

    def over(stream_refs):
        value = stream_refs[0][...]
        for ref in stream_refs[1:]:
            value = value + ref[...]
        return value

    one, two, unit = over(one_refs), over(two_refs), over(unit_refs)
    d_bias = summed(dq_refs[0][...])
    for ref in dq_refs[1:]:
        d_bias = d_bias + summed(ref[...])
    vectors = [
        d_bias + summed(deq),
        summed(dk_ref[...]) + summed(dek),
        summed(dv_ref[...]),
        one[2:3], one[0:1], one[1:2], unit[0:1], two[2:3], two[0:1], two[1:2],
    ]
    pack_ref[...] = jnp.zeros_like(pack_ref)
    row = 0
    for vector in vectors:
        for piece in range(vector.shape[1] // LANES):
            pack_ref[row : row + 1, :] = vector[:, piece * LANES : (piece + 1) * LANES]
            row += 1
    spread(order, me, pack_ref[...], kept_ref, sent_refs, slice(width, width + LANES))


def rel_grads(line, order, span, buckets, deq, dek, wq, wk, dk, dv, dq, one, two, unit):
    width, cols = wq.shape
    outs = [sds((span, cols), BF16)] * 2
    outs = outs + halves(order, span, width + LANES, REL_PIECES)
    operands = [buckets, deq, dek, wq, wk, dk, dv, *dq, *one, *two, *unit]
    return line.call(
        functools.partial(rel_kernel, order, [len(g) for g in (dq, one, two, unit)], span), "rel_grads", outs, operands,
        scratch=[pltpu.VMEM((span, LANES), F32)],
    )


def rel_split_kernel(own_ref, other_ref, table_ref, vector_ref):
    width = table_ref.shape[2]
    for at in range(2):
        total = own_ref[at] + other_ref[1 - at]
        table_ref[at] = total[:, :width]
        vector_ref[at] = total[:, width:]


def rel_split(line, own, other):
    count, rows, wide = own.shape
    outs = [sds((count, rows, wide - LANES), F32), sds((count, rows, LANES), F32)]
    return line.call(rel_split_kernel, "rel_split", outs, (own, other), flops=REL_FLOPS)


def rel_join_kernel(own_ref, other_ref, vector_ref, out_ref):
    width = own_ref.shape[2]
    out_ref[:, :, :width] = own_ref[...] + other_ref[...]
    out_ref[:, :, width:] = vector_ref[...]


def rel_join(line, own, other, vector):
    count, rows, width = own.shape
    outs = [sds((count, rows, width + vector.shape[2]), F32)]
    return line.call(
        rel_join_kernel, "rel_join", outs, (own, other, vector), flops=REL_FLOPS
    )[0]


def hidden_join_kernel(own_ref, other_ref, *refs):
    out_ref = refs[-1]
    start = 0
    for ref in refs[:-1]:
        rows = slice(start, start + ref.shape[0])
        out_ref[rows] = ((own_ref[rows] + other_ref[rows]) + ref[...]).astype(BF16)
        start += ref.shape[0]


def hidden_join(line, own, other, d_one):
    outs = [sds(own.shape, BF16)]
    return line.call(hidden_join_kernel, "hidden_join", outs, (own, other, *d_one), direct=(0,))[0]


def unpack_kernel(origins, count, *refs):
    shared_refs, (table_ref, *vector_refs) = refs[:count], refs[count:]
    width = table_ref.shape[2]
    height = table_ref.shape[1]
    me = lax.axis_index("dp")
    places = [(ref, at) for ref in shared_refs for at in range(ref.shape[0])]
    rows = sum(ref.shape[0] for ref in vector_refs) // LANES
    lines = [
        (ref, piece) for ref in vector_refs for piece in range(ref.shape[0] // LANES)
    ]
    for (shared_ref, at), origin in zip(places, origins, strict=True):
        table_ref[me ^ origin] = shared_ref[at, :, :width]
        for block in range((rows + height - 1) // height):

            @pl.when(me ^ origin == block)
            def _(shared_ref=shared_ref, at=at, block=block):
                for row in range(block * height, min(rows, (block + 1) * height)):
                    ref, piece = lines[row]
                    inner = row % height
                    line = shared_ref[at, inner : inner + 1, width:]
                    ref[pl.ds(piece * LANES, LANES)] = line.reshape(LANES)


def unpack(line, origins, pieces, sizes):
    height, wide = pieces[0].shape[1:]
    outs = [sds((len(origins), height, wide - LANES), F32)] + [sds((size,), F32) for size in sizes]
    return line.call(
        functools.partial(unpack_kernel, origins, len(pieces)), "unpack", outs, pieces,
        direct=range(len(outs)),
    )


def hidden_kernel(dk_ref, dv_ref, wq_ref, wk_ref, wv_ref, *refs):
    out_ref = refs[-1]
    out_ref[...] = dot_nt(dk_ref[...], wk_ref[...]) + dot_nt(dv_ref[...], wv_ref[...])
    start = 0
    for ref in refs[:-1]:
        out_ref[start : start + ref.shape[0]] += dot_nt(ref[...], wq_ref[...])
        start += ref.shape[0]


def hidden_grad(line, dk, dv, wq, wk, wv, dq):
    out = sds((dk.shape[0], wq.shape[0]), F32)
    (total,) = line.call(
        hidden_kernel, "hidden_grad", [out], (dk, dv, wq, wk, wv, *dq)
    )
    return total


def bits_of(parts):
    return [1 << b for b in range(parts.bit_length() - 1)]


def swap_head(value):
    return lax.ppermute(value, "head", [(0, 1), (1, 0)])


def flip(value, parts, bit):
    return lax.ppermute(value, "dp", [(i, i ^ bit) for i in range(parts)])


def together(*values):
    return lax.optimization_barrier(values)


def step_kernel(kept_ref, *refs):
    *arrived_refs, kept_out, sent_out = refs
    half = kept_out.shape[0]
    top = 0
    for ref in arrived_refs:
        rows = slice(top, top + ref.shape[1])
        kept_out[:, rows] = kept_ref[:half, rows] + ref[:half]
        sent_out[:, rows] = kept_ref[half:, rows] + ref[half:]
        top += ref.shape[1]


class Scatter:
    def __init__(self, line, name, kept, *sent, order):
        self.line, self.name, self.order = line, name, list(order)
        self.parts = 1 << len(self.order)
        self.kept = kept
        self.send(sent)

    def send(self, sent):
        self.bit = self.order.pop(0)
        self.arrived = [flip(piece, self.parts, self.bit) for piece in sent]

    def step(self):
        shape = (self.kept.shape[0] // 2, *self.kept.shape[1:])
        self.kept, sent = self.line.call(
            step_kernel, f"{self.name}_{self.bit}", [sds(shape, F32)] * 2,
            (self.kept, *self.arrived), flops=REL_FLOPS if self.name == "rel" else STEP_FLOPS,
        )
        self.send([sent])

    def rest(self, left=0):
        while len(self.order) > left:
            self.step()

    def exchange(self):
        def add(kept_ref, arrived_ref, out_ref):
            out_ref[...] = kept_ref[...] + arrived_ref[...]

        outs = [sds(self.kept.shape, F32)]
        operands = (self.kept, *self.arrived)
        (both,) = self.line.call(
            add, f"{self.name}_{self.bit}", outs, operands, flops=REL_FLOPS
        )
        bit = self.order.pop(0)
        return both, flip(both, self.parts, bit), [0, bit]

    def finish(self, widths, direct=True):
        def kernel(kept_ref, arrived_ref, *out_refs):
            start = 0
            for ref in out_refs:
                cols = slice(start, start + ref.shape[1])
                ref[...] = kept_ref[0, :, cols] + arrived_ref[0, :, cols]
                start += ref.shape[1]

        rows = self.kept.shape[1]
        return self.line.call(
            kernel, f"{self.name}_sum", [sds((rows, width), F32) for width in widths],
            (self.kept, *self.arrived), direct=range(len(widths)) if direct else (),
        )


def pack_kernel(*refs):
    start = 0
    for ref in refs[:-1]:
        refs[-1][start : start + ref.shape[0]] = ref[...]
        start += ref.shape[0]


class Gather:
    def __init__(self, line, value, origins, parts, order):
        self.line, self.parts, self.order = line, parts, list(order)
        self.pieces, self.origins = [value], origins
        self.send(value)

    def send(self, sent):
        bit = self.order.pop(0)
        self.pieces.append(flip(sent, self.parts, bit))
        self.origins = self.origins + [origin ^ bit for origin in self.origins]

    def step(self):
        if self.order:
            shape = (len(self.origins), *self.pieces[0].shape[1:])
            (sent,) = self.line.call(
                pack_kernel, f"pack_{len(self.origins)}", [sds(shape, F32)], self.pieces
            )
            self.send(sent)

    def rest(self):
        while self.order:
            self.step()


def on_device(parts, *arguments):
    (
        hidden_in, lengths, cotangent, w_query, b_query, w_key, b_key, w_value, b_value,
        w_out, b_out, ln1_gain, ln1_bias, w_in, b_in, w_down, b_down, ln2_gain, ln2_bias,
        rel_table,
    ) = arguments
    seq_len, width = hidden_in.shape
    height = seq_len // STREAMS
    streams = range(STREAMS)
    bits = bits_of(parts)

    buckets = jnp.asarray(distance_buckets(seq_len)[None, :])
    line = Line()
    q, k, v, eq, ek, mine = project(
        line, buckets, hidden_in, w_query, b_query, w_key, b_key, w_value, b_value, rel_table,
        w_out,
    )
    fetched = swap_head(mine)
    contexts, attends = [], []
    for at in range(CONTEXTS * STREAMS):
        context, attended = attend(line, at, height // CONTEXTS, lengths, q, k, v, eq, ek)
        contexts.append(context)
        attends.append(attended)
    fetched, contexts[0] = together(fetched, contexts[0])
    quarters = [fetched, flip(fetched, parts, 1), flip(fetched, parts, 2)]
    quarters.append(flip(quarters[2], parts, 1))
    w_out_all = assemble(line, w_out, quarters)
    others = [swap_head(context) for context in contexts]
    of_stream = [slice(CONTEXTS * at, CONTEXTS * (at + 1)) for at in streams]
    fed = [
        feed(
            line, at, height, contexts[of_stream[at]], others[of_stream[at]],
            w_out_all, b_out, hidden_in, ln1_gain, ln1_bias, w_in, b_in, w_down,
        )
        for at in streams
    ]
    backs = []
    for at in streams:
        xhat, rstd, normed, act, slope, lowered = fed[at]
        backs.append(
            feed_back(
                line, at, height, height, [b[0] for b in backs], lowered, swap_head(lowered), xhat,
                ln1_gain, ln1_bias, b_down, ln2_gain, ln2_bias, cotangent, slope, w_in, w_down,
            )
        )
    output = backs[-1][0]
    crossed = bits[:1] + bits[2:] + bits[1:2]
    g_down = grad_blocks(
        line, "grad_down", bits, [[(backs[at][2], fed[at][3:4]) for at in streams]]
    )
    down = Scatter(line, "down", *g_down, order=bits)
    g_in = grad_blocks(
        line, "grad_in", crossed, [[(fed[at][2], backs[at][3:4]) for at in streams]]
    )
    inner = Scatter(line, "inner", *g_in, order=crossed)
    norms, dq = [], []
    carried = ()
    for at in streams:
        xhat, rstd = fed[at][:2]
        d_two, dn = backs[at][1], backs[at][6]
        norms.append(
            norm_back(line, at, 0, dn, swap_head(dn), d_two, xhat, rstd, ln1_gain, w_out)
        )
        if at == 0:
            down.step()
            inner.step()
        d_q, *carried = attend_back(
            line, at, height, at == streams[-1], norms[at][2], q, k, v, eq, ek,
            attends[of_stream[at]], carried,
        )
        dq.append(d_q)
    deq, dek, dk, dv = carried[2:]
    cols = q.shape[1]
    hidden_parts = [hidden_in[at * height : (at + 1) * height] for at in streams]
    chains = {"d": down, "i": inner}
    made = {}

    def start_rel():
        made["relq"], made["relk"], *blocks = rel_grads(
            line, bits, rel_table.shape[0], buckets, deq, dek, w_query, w_key, dk, dv, dq,
            [n[3] for n in norms], [b[4] for b in backs], [b[5] for b in backs],
        )
        chains["r"] = Scatter(line, "rel", *blocks, order=bits)

    def start_value_out():
        blocks = grad_blocks(
            line, "grad_value_out", bits,
            [
                [(hidden_in, [dv])],
                [(norms[at][1], contexts[of_stream[at]]) for at in streams],
            ],
            HEAD_PIECES,
        )
        chains["v"] = Scatter(line, "value_out", *blocks, order=bits)

    def start_query_key():
        blocks = grad_blocks(
            line, "grad_query_key", bits,
            [
                [*zip(hidden_parts, [[d] for d in dq], strict=True), (rel_table, [made["relq"]])],
                [(hidden_in, [dk]), (rel_table, [made["relk"]])],
            ],
            HEAD_PIECES,
        )
        chains["q"] = Scatter(line, "query_key", *blocks, order=bits)

    def start_hidden():
        made["hidden"] = hidden_grad(line, dk, dv, w_query, w_key, w_value, dq)
        made["hidden_other"] = swap_head(made["hidden"])

    def exchange_rel():
        chains["r"].rest(1)
        made["both"], made["both_other"], made["origins"] = chains["r"].exchange()

    def swap_rel():
        made["own"], made["vectors"] = rel_split(line, made["both"], made["both_other"])
        made["own_other"] = swap_head(made["own"])

    def gather_rel():
        joined = rel_join(line, made["own"], made["own_other"], made["vectors"])
        chains["p"] = Gather(line, joined, made["origins"], parts, bits[-2::-1])

    def end_hidden():
        made["grad_input"] = hidden_join(
            line, made["hidden"], made["hidden_other"], [n[0] for n in norms]
        )

    def end(name, widths):
        chains[name].rest()
        made[name] = chains[name].finish(widths)

    actions = {
        "L": start_rel, "G": start_value_out, "K": start_query_key, "Y": start_hidden,
        "X": exchange_rel, "S": swap_rel, "J": gather_rel, "H": end_hidden,
        "d": lambda: end("d", [w_in.shape[1]]), "i": lambda: end("i", [w_in.shape[1]]),
        "v": lambda: end("v", [cols, cols]), "q": lambda: end("q", [cols, cols]),
    }
    for letter in TAIL:
        if letter in actions:
            actions[letter]()
        else:
            chains[letter.lower()].step()
    (s_down,), (s_in,) = made["d"], made["i"]
    (s_q, s_k), (s_v, s_out) = made["q"], made["v"]
    grad_input = made["grad_input"]
    shared = chains["p"]
    shared.rest()
    sizes = [cols] * 3 + [width] * 3 + [w_in.shape[1]] + [width] * 3
    table_blocks, *pieces = unpack(line, shared.origins, shared.pieces, sizes)
    grad_rel_table = table_blocks.reshape(rel_table.shape)
    (
        grad_b_query, grad_b_key, grad_b_value, grad_b_out, grad_ln1_gain, grad_ln1_bias,
        grad_b_in, grad_b_down, grad_ln2_gain, grad_ln2_bias,
    ) = pieces
    return (
        output, grad_input, s_q, grad_b_query, s_k, grad_b_key, s_v, grad_b_value,
        s_out.T, grad_b_out, grad_ln1_gain, grad_ln1_bias, s_in, grad_b_in,
        s_down.T, grad_b_down, grad_ln2_gain, grad_ln2_bias, grad_rel_table,
    )


def solution(mesh):
    parts = mesh.shape["dp"]
    return jax.shard_map(
        functools.partial(on_device, parts),
        mesh=mesh,
        in_specs=(
            P("dp", None), P("dp"), P("dp", None),
            P(None, "head"), P("head"), P(None, "head"), P("head"), P(None, "head"), P("head"),
            P("head", None), P(), P(), P(),
            P(None, "head"), P("head"), P("head", None), P(), P(), P(), P(),
        ),
        out_specs=(
            P("dp", None), P("dp", None),
            P("dp", "head"), P("head"), P("dp", "head"), P("head"), P("dp", "head"), P("head"),
            P("head", "dp"), P(), P(), P(),
            P("dp", "head"), P("head"), P("head", "dp"), P(), P(), P(), P(),
        ),
        check_vma=False,
    )
```

```python
import functools
import itertools
import math

import jax
import jax.numpy as jnp
import numpy as np
from jax import lax
from jax.experimental import pallas as pl
from jax.experimental.pallas import tpu as pltpu
from jax.sharding import PartitionSpec as P

HEAD_DIM = 64
SPAN = 256
MAXPOS = 512
EPSILON = 1e-07
MASKED = -1000000000.0
LANES = 128
STREAMS = 2
CONTEXTS = 1
TAIL = "LGKYDIR(VQ)RDXVISQJQiqP(VH)dP(vU)"
REL_PIECES = 1
HEAD_PIECES = 1
QUARTERS = 4
COLUMNS = 384
BACK_FLOPS = 64 << 30
STEP_FLOPS = 1024
GRAD_FLOPS = 1024
VMEM_LIMIT = 8 * 1024 * 1024

BF16 = jnp.bfloat16
F32 = jnp.float32


def bucket_of(offsets, bucket_span, max_distance):
    middle = bucket_span // 2
    direction = np.sign(offsets)
    absolute = np.where((offsets < middle) & (offsets > -middle), middle - 1, np.abs(offsets))
    log_part = (
        np.ceil(np.log(absolute / middle) / np.log((max_distance - 1) / middle) * (middle - 1))
        + middle
    )
    bucket = np.where(absolute <= middle, offsets, log_part * direction).astype(np.int64)
    return np.clip(bucket + bucket_span, 0, 2 * bucket_span - 1).astype(np.int32)


def distance_buckets(seq_len):
    offsets = np.maximum(seq_len - 1 - np.arange(2 * seq_len), 1 - seq_len)
    return bucket_of(offsets, SPAN, MAXPOS)


def dot_nn(a, b):
    return lax.dot_general(a, b, (((1,), (0,)), ((), ())), preferred_element_type=F32)


def dot_nt(a, b):
    return lax.dot_general(a, b, (((1,), (1,)), ((), ())), preferred_element_type=F32)


def dot_tn(a, b):
    return lax.dot_general(a, b, (((0,), (0,)), ((), ())), preferred_element_type=F32)


def resume(work, results):
    try:
        yield work.send(results)
    except StopIteration:
        return


class Line:
    def __init__(self):
        self.last = ()

    def call(
        self, kernel, name, outs, operands, aliases=None, scalars=0, scratch=(), flops=1024,
        space=pltpu.VMEM, direct=(),
    ):
        in_specs = [pl.BlockSpec(memory_space=pltpu.SMEM)] * scalars
        in_specs += [pl.BlockSpec(memory_space=space)] * (len(operands) - scalars)
        in_specs += [pl.BlockSpec(memory_space=pl.ANY)] * len(self.last)
        count, skipped = len(operands), len(self.last)

        def body(*refs):
            kernel(*refs[:count], *refs[count + skipped :])

        results = pl.pallas_call(
            body,
            in_specs=in_specs,
            out_specs=[
                pl.BlockSpec() if at in direct else pl.BlockSpec(memory_space=pltpu.VMEM)
                for at in range(len(outs))
            ],
            out_shape=outs,
            scratch_shapes=list(scratch),
            input_output_aliases=aliases or {},
            compiler_params=pltpu.CompilerParams(vmem_limit_bytes=VMEM_LIMIT),
            cost_estimate=pl.CostEstimate(flops=flops, bytes_accessed=1024, transcendentals=0),
            name=name,
        )(*operands, *self.last)
        self.last = (min(results, key=lambda result: result.size * result.dtype.itemsize),)
        return results


    def group(self, works):
        calls = [next(work) for work in works]
        ins = [len(call[3]) for call in calls]
        sizes = [len(call[2]) for call in calls]

        def kernel(*refs):
            in_refs, out_refs = refs[: sum(ins)], refs[sum(ins) :]
            for call, count, size in zip(calls, ins, sizes, strict=True):
                call[0](*in_refs[:count], *out_refs[:size])
                in_refs, out_refs = in_refs[count:], out_refs[size:]

        outs, operands, direct = [], [], []
        for _, _, call_outs, call_operands, call_direct in calls:
            direct += [len(outs) + at for at in call_direct]
            outs += call_outs
            operands += call_operands
        name = "__".join(call[1] for call in calls)
        results = self.call(kernel, name, outs, operands, direct=direct, flops=STEP_FLOPS)
        for work, size in zip(works, sizes, strict=True):
            part, results = results[:size], results[size:]
            for _ in itertools.islice(resume(work, part), 1):
                raise ValueError("second call")


def sds(shape, dtype):
    return jax.ShapeDtypeStruct(shape, dtype)


def onehot_of(bucket_ref, span):
    buckets = bucket_ref[...]
    hot = buckets == lax.broadcasted_iota(jnp.int32, (span, buckets.shape[1]), 0)
    return jnp.where(hot, 1.0, 0.0).astype(BF16)


def project_kernel(
    bucket_hbm, hidden_hbm, wq_hbm, bq_hbm, wk_hbm, bk_hbm, wv_hbm, bv_hbm, table_hbm, wout_hbm,
    q_ref, k_ref, v_ref, eq_ref, ek_ref, mine_ref,
    bucket_ref, hidden_ref, weight_ref, bq_ref, bk_ref, bv_ref, table_ref, quarter_ref, sems,
):
    rows = quarter_ref.shape[0]
    first = pl.multiple_of(lax.rem(lax.axis_index("dp"), QUARTERS) * rows, rows)
    cols = q_ref.shape[1]
    weights = [weight_ref.at[:, at * cols : (at + 1) * cols] for at in range(3)]
    sources = (
        wout_hbm.at[pl.ds(first, rows)], hidden_hbm, wq_hbm, wk_hbm, wv_hbm, bq_hbm, bk_hbm, bv_hbm,
        table_hbm, bucket_hbm,
    )
    targets = (
        quarter_ref, hidden_ref, *weights, bq_ref, bk_ref, bv_ref, table_ref, bucket_ref,
    )
    copies = [
        pltpu.make_async_copy(source, target, sems.at[at])
        for at, (source, target) in enumerate(zip(sources, targets, strict=True))
    ]
    for copy in copies:
        copy.start()
    copies[0].wait()
    mine_ref[...] = quarter_ref[...].astype(F32)
    for copy in copies[1:8]:
        copy.wait()
    bias = jnp.concatenate([ref[...].astype(F32)[None, :] for ref in (bq_ref, bk_ref, bv_ref)], axis=1)
    rows = (dot_nn(hidden_ref[...], weight_ref[...]) + bias).astype(BF16)
    for at, ref in enumerate((q_ref, k_ref, v_ref)):
        ref[...] = rows[:, at * cols : (at + 1) * cols]
    for copy in copies[8:]:
        copy.wait()
    table = table_ref[...]
    onehot = onehot_of(bucket_ref, table.shape[0])
    both = (dot_nn(table, weight_ref[:, : 2 * cols]) + bias[:, : 2 * cols]).astype(BF16)
    spread_out = dot_tn(onehot, both).astype(BF16)
    eq_ref[...] = spread_out[:, :cols]
    ek_ref[...] = spread_out[:, cols:]


def project(line, buckets, hidden, wq, bq, wk, bk, wv, bv, table, wout):
    seq_len = hidden.shape[0]
    cols = wq.shape[1]
    rows = wout.shape[0] // QUARTERS
    outs = [sds((seq_len, cols), BF16)] * 3 + [sds((2 * seq_len, cols), BF16)] * 2
    outs += [sds((rows, wout.shape[1]), F32)]
    operands = (buckets, hidden, wq, bq, wk, bk, wv, bv, table, wout)
    shapes = [buckets, hidden, sds((wq.shape[0], 3 * cols), wq.dtype), bq, bk, bv, table]
    scratch = [pltpu.VMEM(array.shape, array.dtype) for array in shapes]
    scratch += [pltpu.VMEM((rows, wout.shape[1]), wout.dtype)]
    operands = [pltpu.with_memory_space_constraint(operand, pltpu.HBM) for operand in operands]
    scratch += [pltpu.SemaphoreType.DMA((len(operands),))]
    return line.call(
        project_kernel, "project", outs, operands, scratch=scratch, space=pltpu.HBM
    )


def assemble_kernel(own_ref, *refs):
    out_ref = refs[-1]
    side, me = lax.axis_index("head"), lax.rem(lax.axis_index("dp"), QUARTERS)
    out_ref[side] = own_ref[...]
    for origin, ref in enumerate(refs[:-1]):
        rows = ref.shape[0]
        first = pl.multiple_of((me ^ origin) * rows, rows)
        out_ref[1 - side, pl.ds(first, rows), :] = ref[...].astype(BF16)


def assemble(line, own, quarters):
    rows, width = own.shape
    out = sds((2, rows, width), BF16)
    (joined,) = line.call(assemble_kernel, "assemble", [out], (own, *quarters))
    return joined.reshape(2 * rows, width)


def half_masks():
    lane = lax.broadcasted_iota(jnp.int32, (1, LANES), 1)
    return [lane // HEAD_DIM == side for side in range(LANES // HEAD_DIM)]


def apart(masks, value):
    zero = jnp.zeros_like(value)
    return jnp.concatenate([jnp.where(mask, value, zero) for mask in masks], axis=0)


def join(masks, stacked):
    rows = stacked.shape[0] // 2
    return jnp.where(masks[0], stacked[:rows], stacked[rows:])


def skewed(stacked, shift):
    rows = stacked.shape[0] // 2
    parts = [
        pltpu.roll(part, shift, 1, stride=1, stride_axis=0)
        for part in (stacked[:rows], stacked[rows:])
    ]
    return jnp.concatenate(parts, axis=0)


def attend_kernel(at, height, len_ref, q_ref, k_ref, v_ref, eq_ref, ek_ref, ctx_ref, att_ref):
    seq_len = k_ref.shape[0]
    length = len_ref[0]
    scale = 1.0 / math.sqrt(3 * HEAD_DIM)
    masks = half_masks()
    key_valid = lax.broadcasted_iota(jnp.int32, (1, seq_len), 1) < length
    rows = at * height + lax.broadcasted_iota(jnp.int32, (height, 1), 0)
    rows = jnp.concatenate([rows, rows], axis=0)
    query_valid = rows < length
    row_start = seq_len - height - height * at
    @pl.loop(0, q_ref.shape[1] // LANES, unroll=True)
    def _(pair):
        cols = pl.ds(pl.multiple_of(pair * LANES, LANES), LANES)
        q_pair = q_ref[at * height : (at + 1) * height, cols]
        k_pair = k_ref[:, cols]
        v_pair = v_ref[:, cols]
        rel_window = ek_ref[row_start : row_start + seq_len + height, cols]
        q_two = apart(masks, q_pair)
        content = dot_nt(q_two, k_pair)
        picked = skewed(dot_nt(q_two, rel_window), seq_len + 1)[:, :seq_len]
        blocks = []
        for block in range(seq_len // LANES):
            start = seq_len - LANES - LANES * block + height * at
            window = eq_ref[start : start + LANES + height, cols]
            k_two = apart(masks, k_pair[block * LANES : (block + 1) * LANES])
            tall = skewed(dot_nt(k_two, window), height + 1)[:, :height]
            blocks.append(jnp.concatenate([tall[:LANES].T, tall[LANES:].T], axis=0))
        flipped = jnp.concatenate(blocks, axis=1)
        scores = jnp.where(key_valid, scale * (content + picked + flipped), MASKED)
        peak = jnp.max(scores, axis=-1, keepdims=True)
        weight = jnp.exp(scores - peak)
        total = jnp.sum(weight, axis=-1, keepdims=True)
        keep = jnp.where(query_valid, 1.0 / total, 0.0)
        attend = (weight * keep).astype(BF16)
        att_ref[2 * pair] = attend[:height]
        att_ref[2 * pair + 1] = attend[height:]
        ctx_ref[:, cols] = join(masks, dot_nn(attend, v_pair)).astype(BF16).astype(F32)


def attend(line, at, height, lengths, q, k, v, eq, ek):
    seq_len, cols = q.shape
    heads = cols // HEAD_DIM
    outs = [sds((height, cols), F32), sds((heads, height, seq_len), BF16)]
    return line.call(
        functools.partial(attend_kernel, at, height), f"attend_{at}", outs,
        (lengths, q, k, v, eq, ek), scalars=1,
    )


def norm_back_kernel(
    start, dn_own_ref, dn_other_ref, d_two_ref, xhat_ref, rstd_ref, gain_ref, wout_ref,
    d_one_ref, d_mixed_ref, d_ctx_ref, vec_ref,
):
    rows = slice(start, start + dn_own_ref.shape[0])
    d_normed = (dn_own_ref[...] + dn_other_ref[...]) + d_two_ref[rows]
    xhat = xhat_ref[rows]
    vec_ref[0:1, :] = jnp.sum(d_normed * xhat, axis=0, keepdims=True)
    vec_ref[1:2, :] = jnp.sum(d_normed, axis=0, keepdims=True)
    scaled = d_normed * gain_ref[...].astype(F32)[None, :]
    mean_a = jnp.mean(scaled, axis=-1, keepdims=True)
    mean_b = jnp.mean(scaled * xhat, axis=-1, keepdims=True)
    d_one = rstd_ref[rows] * (scaled - mean_a - xhat * mean_b)
    d_one_ref[...] = d_one
    vec_ref[2:3, :] = jnp.sum(d_one, axis=0, keepdims=True)
    d_mixed = d_one.astype(BF16)
    d_mixed_ref[...] = d_mixed
    d_ctx_ref[...] = dot_nt(d_mixed, wout_ref[...]).astype(BF16)


def norm_back(line, at, start, dn_own, dn_other, d_two, xhat, rstd, gain, wout):
    height, width = dn_own.shape
    outs = [
        sds((height, width), F32),
        sds((height, width), BF16),
        sds((height, wout.shape[0]), BF16),
        sds((8, width), F32),
    ]
    operands = (dn_own, dn_other, d_two, xhat, rstd, gain, wout)
    return line.call(
        functools.partial(norm_back_kernel, start), f"norm_back_{at}", outs, operands,
        flops=BACK_FLOPS,
    )


def attend_back_kernel(
    at, height, count, first, last, d_ctx_ref, q_ref, k_ref, v_ref, eq_ref, ek_ref, *refs
):
    att_refs, refs = refs[:count], refs[count:]
    if not first:
        refs = refs[4:]
    dq_ref, dk_ref, dv_ref, deq_ref, dek_ref = refs[:5]
    seq_len = k_ref.shape[0]
    scale = 1.0 / math.sqrt(3 * HEAD_DIM)
    masks = half_masks()

    def anti(size):
        row = lax.broadcasted_iota(jnp.int32, (size, size), 0)
        col = lax.broadcasted_iota(jnp.int32, (size, size), 1)
        return jnp.where(row + col == size - 1, 1.0, 0.0).astype(BF16)

    anti_rows = anti(height)
    anti_keys = anti(LANES)
    row_start = seq_len - height - height * at
    if first:
        dk_ref[...] = jnp.zeros_like(dk_ref)
        dv_ref[...] = jnp.zeros_like(dv_ref)
        deq_ref[...] = jnp.zeros_like(deq_ref)
        dek_ref[...] = jnp.zeros_like(dek_ref)

    @pl.loop(0, q_ref.shape[1] // LANES, unroll=True)
    def _(pair):
        cols = pl.ds(pl.multiple_of(pair * LANES, LANES), LANES)
        q_pair = q_ref[at * height : (at + 1) * height, cols]
        k_pair = k_ref[:, cols]
        v_pair = v_ref[:, cols]
        ctx_pair = d_ctx_ref[:, cols]
        rel_window = ek_ref[row_start : row_start + seq_len + height, cols]
        q_turned = dot_nn(anti_rows, q_pair).astype(BF16)
        weight = jnp.concatenate(
            [jnp.concatenate([ref[2 * pair + side] for ref in att_refs], axis=0) for side in range(2)],
            axis=0,
        )
        d_att = dot_nt(apart(masks, ctx_pair), v_pair)
        soft = weight.astype(F32)
        inner = jnp.sum(d_att * soft, axis=-1, keepdims=True)
        d_scores = (soft * (d_att - inner)).astype(BF16)
        sides = [d_scores[:height], d_scores[height:]]
        weight_wide = jnp.concatenate([weight[:height], weight[height:]], axis=1)
        dv_ref[:, cols] += join(masks, dot_tn(weight_wide, ctx_pair))
        d_q = join(masks, dot_nn(d_scores, k_pair))
        d_scores_t = [side.T for side in sides]
        d_k = join(masks, dot_nn(jnp.concatenate(d_scores_t, axis=0), q_pair))
        turned = dot_nn(anti_rows, jnp.concatenate(sides, axis=1))
        space = jnp.zeros((height, height), F32)
        turned = [
            jnp.concatenate([turned[:, side * seq_len : (side + 1) * seq_len], space], axis=1)
            for side in range(2)
        ]
        turned = skewed(jnp.concatenate(turned, axis=0), 0).astype(BF16)
        d_q_turned = join(masks, dot_nn(turned, rel_window))
        turned_wide = jnp.concatenate([turned[:height], turned[height:]], axis=1)
        d_rel_k = join(masks, dot_tn(turned_wide, q_turned))
        dek_ref[row_start : row_start + seq_len + height, cols] += scale * d_rel_k

        def turn_back(matrix, value):
            high = value.astype(BF16)
            rest = (value - high.astype(F32)).astype(BF16)
            both = dot_nn(matrix, jnp.concatenate([high, rest], axis=1))
            return both[:, :LANES] + both[:, LANES:]

        dq_ref[:, cols] = (scale * (d_q + turn_back(anti_rows, d_q_turned))).astype(BF16)
        backs = []
        for block in range(seq_len // LANES):
            start = seq_len - LANES - LANES * block + height * at
            rows = slice(block * LANES, (block + 1) * LANES)
            window = eq_ref[start : start + LANES + height, cols]
            tall = dot_nn(anti_keys, jnp.concatenate([side[rows] for side in d_scores_t], axis=1))
            space = jnp.zeros((LANES, LANES), F32)
            tall = [
                jnp.concatenate([tall[:, side * height : (side + 1) * height], space], axis=1)
                for side in range(2)
            ]
            tall = skewed(jnp.concatenate(tall, axis=0), 0).astype(BF16)
            backs.append(join(masks, dot_nn(tall, window)))
            k_turned = apart(masks, dot_nn(anti_keys, k_pair[rows]).astype(BF16))
            deq_ref[start : start + LANES + height, cols] += scale * dot_tn(tall, k_turned)
        for block, value in enumerate(backs):
            rows = slice(block * LANES, (block + 1) * LANES)
            dk_ref[rows, cols] += scale * (d_k[rows] + turn_back(anti_keys, value))
    if last:
        dk_low_ref, dv_low_ref = refs[5:]
        dk_low_ref[...] = dk_ref[...].astype(BF16)
        dv_low_ref[...] = dv_ref[...].astype(BF16)


def attend_back(line, at, height, last, d_ctx, q, k, v, eq, ek, att, carried):
    seq_len, cols = q.shape
    operands = [d_ctx, q, k, v, eq, ek, *att, *carried]
    outs = [
        sds((height, cols), BF16),
        sds((seq_len, cols), F32),
        sds((seq_len, cols), F32),
        sds((2 * seq_len, cols), F32),
        sds((2 * seq_len, cols), F32),
    ]
    if last:
        outs += [sds((seq_len, cols), BF16)] * 2
    base = 6 + len(att)
    return line.call(
        functools.partial(attend_back_kernel, at, height, len(att), not carried, last),
        f"attend_back_{at}", outs, operands,
        aliases={base + place: 1 + place for place in range(4)} if carried else {},
        flops=BACK_FLOPS,
    )


def feed_kernel(
    at, height, count, wout_ref, bout_ref, hidden_ref, gain_ref, shift_ref, win_ref, bin_ref,
    wdown_ref, *refs,
):
    own_refs, other_refs = refs[:count], refs[count : 2 * count]
    xhat_ref, rstd_ref, normed_ref, act_ref, slope_ref, low_ref = refs[2 * count :]
    own = jnp.concatenate([ref[...] for ref in own_refs], axis=0)
    other = jnp.concatenate([ref[...] for ref in other_refs], axis=0)
    first = lax.axis_index("head") == 0
    ctx = jnp.concatenate([jnp.where(first, own, other), jnp.where(first, other, own)], axis=1)
    ctx = ctx.astype(BF16)
    mixed = dot_nn(ctx, wout_ref[...])
    hidden = hidden_ref[at * height : (at + 1) * height].astype(F32)
    resid = mixed + bout_ref[...].astype(F32)[None, :] + hidden
    center = resid - jnp.mean(resid, axis=-1, keepdims=True)
    spread = jnp.mean(center * center, axis=-1, keepdims=True)
    rstd = lax.rsqrt(spread + EPSILON)
    xhat = center * rstd
    xhat_ref[...] = xhat
    rstd_ref[...] = rstd
    normed = xhat * gain_ref[...].astype(F32)[None, :] + shift_ref[...].astype(F32)[None, :]
    low = normed.astype(BF16)
    normed_ref[...] = low
    units = win_ref.shape[1]
    step = units // 3
    total = None
    bias = bin_ref[...].astype(F32)[None, :]
    for part in range(3):
        cols = slice(part * step, (part + 1) * step)
        inner = dot_nn(low, win_ref[:, cols]) + bias[:, cols]
        phi = 0.5 * (1.0 + lax.erf(inner * math.sqrt(0.5)))
        act = (inner * phi).astype(BF16)
        slope = phi + inner * (jnp.exp(-0.5 * inner * inner) * (1.0 / math.sqrt(2 * math.pi)))
        act_ref[:, cols] = act
        slope_ref[:, cols] = slope
        term = dot_nn(act, wdown_ref[cols, :])
        total = term if total is None else total + term
    low_ref[...] = total


def feed(line, at, height, own, other, wout, bout, hidden, gain, shift, win, b_in, wdown):
    width = hidden.shape[1]
    units = win.shape[1]
    outs = [
        sds((height, width), F32),
        sds((height, 1), F32),
        sds((height, width), BF16),
        sds((height, units), BF16),
        sds((height, units), F32),
        sds((height, width), F32),
    ]
    operands = (wout, bout, hidden, gain, shift, win, b_in, wdown, *own, *other)
    return line.call(
        functools.partial(feed_kernel, at, height, len(own)), f"feed_{at}", outs, operands,
        flops=BACK_FLOPS if at else 1024,
    )


def feed_back_kernel(
    at, height, count, low_own_ref, low_other_ref, xhat_one_ref, gain_one_ref, shift_one_ref, bdown_ref,
    gain_ref, shift_ref, cot_ref, slope_ref, win_ref, wdown_ref,
    *refs,
):
    before, refs = refs[:count], refs[count:]
    out_ref, d_two_ref, d_low_ref, d_inner_ref, vec_ref, bin_ref, *dn_refs = refs
    normed = xhat_one_ref[...] * gain_one_ref[...].astype(F32)[None, :]
    normed = normed + shift_one_ref[...].astype(F32)[None, :]
    resid = (low_own_ref[...] + low_other_ref[...]) + bdown_ref[...].astype(F32)[None, :] + normed
    center = resid - jnp.mean(resid, axis=-1, keepdims=True)
    spread = jnp.mean(center * center, axis=-1, keepdims=True)
    rstd = lax.rsqrt(spread + EPSILON)
    xhat = center * rstd
    gain = gain_ref[...].astype(F32)[None, :]
    value = (xhat * gain + shift_ref[...].astype(F32)[None, :]).astype(BF16)
    if out_ref.shape[0] == height:
        out_ref[...] = value
    else:
        for stream, ref in enumerate(before):
            out_ref[stream * height : (stream + 1) * height] = ref[...]
        out_ref[at * height : (at + 1) * height] = value
    err = cot_ref[at * height : (at + 1) * height].astype(F32)
    vec_ref[0:1, :] = jnp.sum(err * xhat, axis=0, keepdims=True)
    vec_ref[1:2, :] = jnp.sum(err, axis=0, keepdims=True)
    scaled = err * gain
    mean_a = jnp.mean(scaled, axis=-1, keepdims=True)
    mean_b = jnp.mean(scaled * xhat, axis=-1, keepdims=True)
    d_two = rstd * (scaled - mean_a - xhat * mean_b)
    d_two_ref[...] = d_two
    vec_ref[2:3, :] = jnp.sum(d_two, axis=0, keepdims=True)
    low = d_two.astype(BF16)
    d_low_ref[...] = low
    units = win_ref.shape[1]
    step = units // 3
    total = None
    for part in range(3):
        cols = slice(part * step, (part + 1) * step)
        d_act = dot_nt(low, wdown_ref[cols, :])
        d_inner = (d_act * slope_ref[:, cols]).astype(BF16)
        d_inner_ref[:, cols] = d_inner
        bin_ref[0:1, cols] = jnp.sum(d_inner.astype(F32), axis=0, keepdims=True)
        term = dot_nt(d_inner, win_ref[:, cols])
        total = term if total is None else total + term
    rows = dn_refs[0].shape[0]
    for piece, ref in enumerate(dn_refs):
        ref[...] = total[piece * rows : (piece + 1) * rows]


def feed_back(
    line, at, height, rows, before, low_own, low_other, xhat, gain_one, shift_one, bdown, gain,
    shift, cot, slope, win, wdown,
):
    width = cot.shape[1]
    units = win.shape[1]
    last = (at + 1) * height == cot.shape[0]
    before = before if last else []
    outs = [
        sds(cot.shape if last else (height, width), BF16),
        sds((height, width), F32),
        sds((height, width), BF16),
        sds((height, units), BF16),
        sds((8, width), F32),
        sds((8, units), F32),
    ]
    outs += [sds((rows, width), F32)] * (height // rows)
    operands = (
        low_own, low_other, xhat, gain_one, shift_one, bdown, gain, shift, cot, slope, win, wdown,
        *before,
    )
    return line.call(
        functools.partial(feed_back_kernel, at, height, len(before)), f"feed_back_{at}", outs,
        operands, direct=(0,) if last else (),
    )


def spread(order, me, total, kept_ref, sent_refs, cols):
    parts = 1 << len(order)
    height = total.shape[0] // parts
    for bit in (0, order[0]):

        @pl.when((me & order[0]) == bit)
        def _(bit=bit):
            for block in range(parts):
                origin = me ^ block
                place = 0
                for later in order[1:]:
                    place = 2 * place + ((origin >> (later.bit_length() - 1)) & 1)
                top = block * height
                if block & order[0] == bit:
                    kept_ref[place, :, cols] = total[top : top + height]
                else:
                    for ref in sent_refs:
                        ref[place, :, cols] = total[top : top + ref.shape[1]]
                        top += ref.shape[1]


def grad_kernel(order, groups, pieces, *refs):
    kept_ref, *sent_refs = refs[-1 - pieces :]
    me = lax.axis_index("dp")
    at, start = 0, 0
    for count in groups:
        terms = []
        for rights in count:
            terms.append((refs[at], refs[at + 1 : at + 1 + rights]))
            at += 1 + rights
        width = terms[0][1][0].shape[1]

        def part(index, terms=terms, start=start):
            total = None
            columns = pl.ds(pl.multiple_of(index * COLUMNS, COLUMNS), COLUMNS)
            for left_ref, right_refs in terms:
                right = jnp.concatenate([ref[:, columns] for ref in right_refs], axis=0)
                term = dot_tn(left_ref[...], right.astype(BF16))
                total = term if total is None else total + term
            target = pl.ds(pl.multiple_of(start + index * COLUMNS, COLUMNS), COLUMNS)
            spread(order, me, total, kept_ref, sent_refs, target)

        pl.loop(0, width // COLUMNS)(part)
        start += width


def halves(order, rows, cols, pieces):
    half, height = (1 << len(order)) // 2, rows >> len(order)
    return [sds((half, height, cols), F32)] + [sds((half, height // pieces, cols), F32)] * pieces


def grad_blocks(line, name, order, groups, pieces=1):
    width = groups[0][0][0].shape[1]
    cols = sum(group[0][1][0].shape[1] for group in groups)
    operands = [array for group in groups for left, right in group for array in (left, *right)]
    counts = [[len(right) for _, right in group] for group in groups]
    outs = halves(order, width, cols, pieces)
    return line.call(
        functools.partial(grad_kernel, order, counts, pieces), name, outs, operands,
        flops=GRAD_FLOPS,
    )


def rel_kernel(
    order, counts, table_rows, bucket_ref, deq_ref, dek_ref, wq_ref, wk_ref, dk_ref, dv_ref,
    *refs,
):
    groups = []
    for count in counts:
        groups.append(refs[:count])
        refs = refs[count:]
    dq_refs, one_refs, two_refs, unit_refs = groups
    relq_ref, relk_ref, kept_ref, *sent_refs, pack_ref = refs
    onehot = onehot_of(bucket_ref, table_rows)
    deq, dek = deq_ref[...], dek_ref[...]
    cols = deq.shape[1]
    d_rel = dot_nn(onehot, jnp.concatenate([deq, dek], axis=1).astype(BF16)).astype(BF16)
    relq_ref[...] = d_rel[:, :cols]
    relk_ref[...] = d_rel[:, cols:]
    total = dot_nt(d_rel, jnp.concatenate([wq_ref[...], wk_ref[...]], axis=1))
    width = total.shape[1]
    me = lax.axis_index("dp")
    spread(order, me, total, kept_ref, sent_refs, slice(0, width))

    def summed(value):
        return jnp.sum(value.astype(F32), axis=0, keepdims=True)

    def over(stream_refs):
        value = stream_refs[0][...]
        for ref in stream_refs[1:]:
            value = value + ref[...]
        return value

    one, two, unit = over(one_refs), over(two_refs), over(unit_refs)
    d_bias = summed(dq_refs[0][...])
    for ref in dq_refs[1:]:
        d_bias = d_bias + summed(ref[...])
    vectors = [
        d_bias + summed(deq),
        summed(dk_ref[...]) + summed(dek),
        summed(dv_ref[...]),
        one[2:3], one[0:1], one[1:2], unit[0:1], two[2:3], two[0:1], two[1:2],
    ]
    pack_ref[...] = jnp.zeros_like(pack_ref)
    row = 0
    for vector in vectors:
        for piece in range(vector.shape[1] // LANES):
            pack_ref[row : row + 1, :] = vector[:, piece * LANES : (piece + 1) * LANES]
            row += 1
    spread(order, me, pack_ref[...], kept_ref, sent_refs, slice(width, width + LANES))


def rel_grads(line, order, span, buckets, deq, dek, wq, wk, dk, dv, dq, one, two, unit):
    width, cols = wq.shape
    outs = [sds((span, cols), BF16)] * 2
    outs = outs + halves(order, span, width + LANES, REL_PIECES)
    operands = [buckets, deq, dek, wq, wk, dk, dv, *dq, *one, *two, *unit]
    return line.call(
        functools.partial(rel_kernel, order, [len(g) for g in (dq, one, two, unit)], span), "rel_grads", outs, operands,
        scratch=[pltpu.VMEM((span, LANES), F32)],
    )


def rel_split_kernel(own_ref, other_ref, table_ref, vector_ref):
    width = table_ref.shape[2]
    for at in range(2):
        total = own_ref[at] + other_ref[1 - at]
        table_ref[at] = total[:, :width]
        vector_ref[at] = total[:, width:]


def rel_split(own, other):
    count, rows, wide = own.shape
    outs = [sds((count, rows, wide - LANES), F32), sds((count, rows, LANES), F32)]
    return rel_split_kernel, "rel_split", outs, [own, other], ()


def rel_join_kernel(own_ref, other_ref, vector_ref, out_ref):
    width = own_ref.shape[2]
    out_ref[:, :, :width] = own_ref[...] + other_ref[...]
    out_ref[:, :, width:] = vector_ref[...]


def rel_join(own, other, vector):
    count, rows, width = own.shape
    outs = [sds((count, rows, width + vector.shape[2]), F32)]
    return rel_join_kernel, "rel_join", outs, [own, other, vector], ()


def hidden_join_kernel(own_ref, other_ref, *refs):
    out_ref = refs[-1]
    start = 0
    for ref in refs[:-1]:
        rows = slice(start, start + ref.shape[0])
        out_ref[rows] = ((own_ref[rows] + other_ref[rows]) + ref[...]).astype(BF16)
        start += ref.shape[0]


def hidden_join(own, other, d_one):
    outs = [sds(own.shape, BF16)]
    return hidden_join_kernel, "hidden_join", outs, [own, other, *d_one], (0,)


def unpack_kernel(origins, count, *refs):
    shared_refs, (table_ref, *vector_refs) = refs[:count], refs[count:]
    width = table_ref.shape[2]
    height = table_ref.shape[1]
    me = lax.axis_index("dp")
    places = [(ref, at) for ref in shared_refs for at in range(ref.shape[0])]
    rows = sum(ref.shape[0] for ref in vector_refs) // LANES
    lines = [
        (ref, piece) for ref in vector_refs for piece in range(ref.shape[0] // LANES)
    ]
    for (shared_ref, at), origin in zip(places, origins, strict=True):
        table_ref[me ^ origin] = shared_ref[at, :, :width]
        for block in range((rows + height - 1) // height):

            @pl.when(me ^ origin == block)
            def _(shared_ref=shared_ref, at=at, block=block):
                for row in range(block * height, min(rows, (block + 1) * height)):
                    ref, piece = lines[row]
                    inner = row % height
                    line = shared_ref[at, inner : inner + 1, width:]
                    ref[pl.ds(piece * LANES, LANES)] = line.reshape(LANES)


def unpack(origins, pieces, sizes):
    height, wide = pieces[0].shape[1:]
    outs = [sds((len(origins), height, wide - LANES), F32)] + [sds((size,), F32) for size in sizes]
    kernel = functools.partial(unpack_kernel, origins, len(pieces))
    return kernel, "unpack", outs, list(pieces), range(len(outs))


def hidden_kernel(dk_ref, dv_ref, wq_ref, wk_ref, wv_ref, *refs):
    out_ref = refs[-1]
    out_ref[...] = dot_nt(dk_ref[...], wk_ref[...]) + dot_nt(dv_ref[...], wv_ref[...])
    start = 0
    for ref in refs[:-1]:
        out_ref[start : start + ref.shape[0]] += dot_nt(ref[...], wq_ref[...])
        start += ref.shape[0]


def hidden_grad(line, dk, dv, wq, wk, wv, dq):
    out = sds((dk.shape[0], wq.shape[0]), F32)
    (total,) = line.call(
        hidden_kernel, "hidden_grad", [out], (dk, dv, wq, wk, wv, *dq)
    )
    return total


def bits_of(parts):
    return [1 << b for b in range(parts.bit_length() - 1)]


def swap_head(value):
    return lax.ppermute(value, "head", [(0, 1), (1, 0)])


def flip(value, parts, bit):
    return lax.ppermute(value, "dp", [(i, i ^ bit) for i in range(parts)])


def together(*values):
    return lax.optimization_barrier(values)


def step_kernel(kept_ref, *refs):
    *arrived_refs, kept_out, sent_out = refs
    half = kept_out.shape[0]
    top = 0
    for ref in arrived_refs:
        rows = slice(top, top + ref.shape[1])
        kept_out[:, rows] = kept_ref[:half, rows] + ref[:half]
        sent_out[:, rows] = kept_ref[half:, rows] + ref[half:]
        top += ref.shape[1]


class Scatter:
    def __init__(self, line, name, kept, *sent, order):
        self.line, self.name, self.order = line, name, list(order)
        self.parts = 1 << len(self.order)
        self.kept = kept
        self.send(sent)

    def send(self, sent):
        self.bit = self.order.pop(0)
        self.arrived = [flip(piece, self.parts, self.bit) for piece in sent]

    def step(self):
        shape = (self.kept.shape[0] // 2, *self.kept.shape[1:])
        self.kept, sent = yield (
            step_kernel, f"{self.name}_{self.bit}", [sds(shape, F32)] * 2,
            [self.kept, *self.arrived], (),
        )
        self.send([sent])

    def rest(self, left=0):
        while len(self.order) > left:
            self.line.group([self.step()])

    def exchange(self):
        def add(kept_ref, arrived_ref, out_ref):
            out_ref[...] = kept_ref[...] + arrived_ref[...]

        self.rest(1)
        outs = [sds(self.kept.shape, F32)]
        (self.both,) = yield add, f"{self.name}_{self.bit}", outs, [self.kept, *self.arrived], ()
        bit = self.order.pop(0)
        self.both_other, self.origins = flip(self.both, self.parts, bit), [0, bit]

    def finish(self, widths):
        def kernel(kept_ref, arrived_ref, *out_refs):
            start = 0
            for ref in out_refs:
                cols = slice(start, start + ref.shape[1])
                ref[...] = kept_ref[0, :, cols] + arrived_ref[0, :, cols]
                start += ref.shape[1]

        self.rest()
        outs = [sds((self.kept.shape[1], width), F32) for width in widths]
        operands = [self.kept, *self.arrived]
        self.sums = yield kernel, f"{self.name}_sum", outs, operands, range(len(outs))


def pack_kernel(*refs):
    start = 0
    for ref in refs[:-1]:
        refs[-1][start : start + ref.shape[0]] = ref[...]
        start += ref.shape[0]


class Gather:
    def __init__(self, line, value, origins, parts, order):
        self.line, self.parts, self.order = line, parts, list(order)
        self.pieces, self.origins = [value], origins
        self.send(value)

    def send(self, sent):
        bit = self.order.pop(0)
        self.pieces.append(flip(sent, self.parts, bit))
        self.origins = self.origins + [origin ^ bit for origin in self.origins]

    def step(self):
        shape = (len(self.origins), *self.pieces[0].shape[1:])
        name = f"pack_{len(self.origins)}"
        (sent,) = yield pack_kernel, name, [sds(shape, F32)], list(self.pieces), ()
        self.send(sent)

    def rest(self):
        while self.order:
            self.line.group([self.step()])


def words_of(text):
    words, open_word = [], None
    for letter in text:
        if letter == "(":
            open_word = ""
        elif letter == ")":
            words.append(open_word)
            open_word = None
        elif open_word is not None:
            open_word += letter
        else:
            words.append(letter)
    return words


def on_device(parts, *arguments):
    (
        hidden_in, lengths, cotangent, w_query, b_query, w_key, b_key, w_value, b_value,
        w_out, b_out, ln1_gain, ln1_bias, w_in, b_in, w_down, b_down, ln2_gain, ln2_bias,
        rel_table,
    ) = arguments
    seq_len, width = hidden_in.shape
    height = seq_len // STREAMS
    streams = range(STREAMS)
    bits = bits_of(parts)

    buckets = jnp.asarray(distance_buckets(seq_len)[None, :])
    line = Line()
    q, k, v, eq, ek, mine = project(
        line, buckets, hidden_in, w_query, b_query, w_key, b_key, w_value, b_value, rel_table,
        w_out,
    )
    fetched = swap_head(mine)
    contexts, attends = [], []
    for at in range(CONTEXTS * STREAMS):
        context, attended = attend(line, at, height // CONTEXTS, lengths, q, k, v, eq, ek)
        contexts.append(context)
        attends.append(attended)
    fetched, contexts[0] = together(fetched, contexts[0])
    quarters = [fetched, flip(fetched, parts, 1), flip(fetched, parts, 2)]
    quarters.append(flip(quarters[2], parts, 1))
    w_out_all = assemble(line, w_out, quarters)
    others = [swap_head(context) for context in contexts]
    of_stream = [slice(CONTEXTS * at, CONTEXTS * (at + 1)) for at in streams]
    fed = [
        feed(
            line, at, height, contexts[of_stream[at]], others[of_stream[at]],
            w_out_all, b_out, hidden_in, ln1_gain, ln1_bias, w_in, b_in, w_down,
        )
        for at in streams
    ]
    backs = []
    for at in streams:
        xhat, rstd, normed, act, slope, lowered = fed[at]
        backs.append(
            feed_back(
                line, at, height, height, [b[0] for b in backs], lowered, swap_head(lowered), xhat,
                ln1_gain, ln1_bias, b_down, ln2_gain, ln2_bias, cotangent, slope, w_in, w_down,
            )
        )
    output = backs[-1][0]
    crossed = bits[:1] + bits[2:] + bits[1:2]
    g_down = grad_blocks(
        line, "grad_down", bits, [[(backs[at][2], fed[at][3:4]) for at in streams]]
    )
    down = Scatter(line, "down", *g_down, order=bits)
    g_in = grad_blocks(
        line, "grad_in", crossed, [[(fed[at][2], backs[at][3:4]) for at in streams]]
    )
    inner = Scatter(line, "inner", *g_in, order=crossed)
    norms, dq = [], []
    carried = ()
    for at in streams:
        xhat, rstd = fed[at][:2]
        d_two, dn = backs[at][1], backs[at][6]
        norms.append(
            norm_back(line, at, 0, dn, swap_head(dn), d_two, xhat, rstd, ln1_gain, w_out)
        )
        if at == 0:
            line.group([down.step()])
            line.group([inner.step()])
        d_q, *carried = attend_back(
            line, at, height, at == streams[-1], norms[at][2], q, k, v, eq, ek,
            attends[of_stream[at]], carried,
        )
        dq.append(d_q)
    deq, dek, dk, dv = carried[2:]
    cols = q.shape[1]
    hidden_parts = [hidden_in[at * height : (at + 1) * height] for at in streams]
    chains = {"d": down, "i": inner}
    made = {}

    def start_rel():
        made["relq"], made["relk"], *blocks = rel_grads(
            line, bits, rel_table.shape[0], buckets, deq, dek, w_query, w_key, dk, dv, dq,
            [n[3] for n in norms], [b[4] for b in backs], [b[5] for b in backs],
        )
        chains["r"] = Scatter(line, "rel", *blocks, order=bits)

    def start_value_out():
        blocks = grad_blocks(
            line, "grad_value_out", bits,
            [
                [(hidden_in, [dv])],
                [(norms[at][1], contexts[of_stream[at]]) for at in streams],
            ],
            HEAD_PIECES,
        )
        chains["v"] = Scatter(line, "value_out", *blocks, order=bits)

    def start_query_key():
        blocks = grad_blocks(
            line, "grad_query_key", bits,
            [
                [*zip(hidden_parts, [[d] for d in dq], strict=True), (rel_table, [made["relq"]])],
                [(hidden_in, [dk]), (rel_table, [made["relk"]])],
            ],
            HEAD_PIECES,
        )
        chains["q"] = Scatter(line, "query_key", *blocks, order=bits)

    def start_hidden():
        made["hidden"] = hidden_grad(line, dk, dv, w_query, w_key, w_value, dq)
        made["hidden_other"] = swap_head(made["hidden"])

    def swap_rel():
        both, other = chains["r"].both, chains["r"].both_other
        made["own"], made["vectors"] = yield rel_split(both, other)
        made["own_other"] = swap_head(made["own"])

    def gather_rel():
        (joined,) = yield rel_join(made["own"], made["own_other"], made["vectors"])
        chains["p"] = Gather(line, joined, chains["r"].origins, parts, bits[-2::-1])

    def end_hidden():
        d_one = [n[0] for n in norms]
        made["grad_input"] = yield hidden_join(made["hidden"], made["hidden_other"], d_one)

    def end_rel():
        chains["p"].rest()
        sizes = [cols] * 3 + [width] * 3 + [w_in.shape[1]] + [width] * 3
        made["shared"] = yield unpack(chains["p"].origins, chains["p"].pieces, sizes)

    starters = {
        "L": start_rel, "G": start_value_out, "K": start_query_key, "Y": start_hidden,
    }
    steps = {
        "X": lambda: chains["r"].exchange(), "S": swap_rel, "J": gather_rel, "H": end_hidden,
        "U": end_rel,
    }
    widths = {"d": [w_in.shape[1]], "i": [w_in.shape[1]], "v": [cols, cols], "q": [cols, cols]}

    def work(letter):
        if letter in widths:
            return chains[letter].finish(widths[letter])
        return steps[letter]() if letter in steps else chains[letter.lower()].step()

    for word in words_of(TAIL):
        if word in starters:
            starters[word]()
        else:
            line.group([work(letter) for letter in word])
    (s_down,), (s_in,) = chains["d"].sums, chains["i"].sums
    (s_q, s_k), (s_v, s_out) = chains["q"].sums, chains["v"].sums
    (grad_input,) = made["grad_input"]
    table_blocks, *pieces = made["shared"]
    grad_rel_table = table_blocks.reshape(rel_table.shape)
    (
        grad_b_query, grad_b_key, grad_b_value, grad_b_out, grad_ln1_gain, grad_ln1_bias,
        grad_b_in, grad_b_down, grad_ln2_gain, grad_ln2_bias,
    ) = pieces
    return (
        output, grad_input, s_q, grad_b_query, s_k, grad_b_key, s_v, grad_b_value,
        s_out.T, grad_b_out, grad_ln1_gain, grad_ln1_bias, s_in, grad_b_in,
        s_down.T, grad_b_down, grad_ln2_gain, grad_ln2_bias, grad_rel_table,
    )


def solution(mesh):
    parts = mesh.shape["dp"]
    return jax.shard_map(
        functools.partial(on_device, parts),
        mesh=mesh,
        in_specs=(
            P("dp", None), P("dp"), P("dp", None),
            P(None, "head"), P("head"), P(None, "head"), P("head"), P(None, "head"), P("head"),
            P("head", None), P(), P(), P(),
            P(None, "head"), P("head"), P("head", None), P(), P(), P(), P(),
        ),
        out_specs=(
            P("dp", None), P("dp", None),
            P("dp", "head"), P("head"), P("dp", "head"), P("head"), P("dp", "head"), P("head"),
            P("head", "dp"), P(), P(), P(),
            P("dp", "head"), P("head"), P("head", "dp"), P(), P(), P(), P(),
        ),
        check_vma=False,
    )
```

```python
import functools
import itertools
import math

import jax
import jax.numpy as jnp
import numpy as np
from jax import lax
from jax.experimental import pallas as pl
from jax.experimental.pallas import tpu as pltpu
from jax.sharding import PartitionSpec as P

HEAD_DIM = 64
SPAN = 256
MAXPOS = 512
EPSILON = 1e-07
MASKED = -1000000000.0
LANES = 128
STREAMS = 2
CONTEXTS = 1
TAIL = "YLKGDIR(VQ)RDVXISQJiQqP(VH)dP(vU)"
REL_PIECES = 1
HEAD_PIECES = 1
QUARTERS = 4
COLUMNS = 384
BACK_FLOPS = 64 << 30
STEP_FLOPS = 1024
GRAD_FLOPS = 1024
VMEM_LIMIT = 8 * 1024 * 1024

BF16 = jnp.bfloat16
F32 = jnp.float32


def bucket_of(offsets, bucket_span, max_distance):
    middle = bucket_span // 2
    direction = np.sign(offsets)
    absolute = np.where((offsets < middle) & (offsets > -middle), middle - 1, np.abs(offsets))
    log_part = (
        np.ceil(np.log(absolute / middle) / np.log((max_distance - 1) / middle) * (middle - 1))
        + middle
    )
    bucket = np.where(absolute <= middle, offsets, log_part * direction).astype(np.int64)
    return np.clip(bucket + bucket_span, 0, 2 * bucket_span - 1).astype(np.int32)


def distance_buckets(seq_len):
    offsets = np.maximum(seq_len - 1 - np.arange(2 * seq_len), 1 - seq_len)
    return bucket_of(offsets, SPAN, MAXPOS)


def dot_nn(a, b):
    return lax.dot_general(a, b, (((1,), (0,)), ((), ())), preferred_element_type=F32)


def dot_nt(a, b):
    return lax.dot_general(a, b, (((1,), (1,)), ((), ())), preferred_element_type=F32)


def dot_tn(a, b):
    return lax.dot_general(a, b, (((0,), (0,)), ((), ())), preferred_element_type=F32)


def resume(work, results):
    try:
        yield work.send(results)
    except StopIteration:
        return


class Line:
    def __init__(self):
        self.last = ()

    def call(
        self, kernel, name, outs, operands, aliases=None, scalars=0, scratch=(), flops=1024,
        space=pltpu.VMEM, direct=(),
    ):
        in_specs = [pl.BlockSpec(memory_space=pltpu.SMEM)] * scalars
        in_specs += [pl.BlockSpec(memory_space=space)] * (len(operands) - scalars)
        in_specs += [pl.BlockSpec(memory_space=pl.ANY)] * len(self.last)
        count, skipped = len(operands), len(self.last)

        def body(*refs):
            kernel(*refs[:count], *refs[count + skipped :])

        results = pl.pallas_call(
            body,
            in_specs=in_specs,
            out_specs=[
                pl.BlockSpec() if at in direct else pl.BlockSpec(memory_space=pltpu.VMEM)
                for at in range(len(outs))
            ],
            out_shape=outs,
            scratch_shapes=list(scratch),
            input_output_aliases=aliases or {},
            compiler_params=pltpu.CompilerParams(vmem_limit_bytes=VMEM_LIMIT),
            cost_estimate=pl.CostEstimate(flops=flops, bytes_accessed=1024, transcendentals=0),
            name=name,
        )(*operands, *self.last)
        self.last = (min(results, key=lambda result: result.size * result.dtype.itemsize),)
        return results


    def group(self, works):
        calls = [next(work) for work in works]
        ins = [len(call[3]) for call in calls]
        sizes = [len(call[2]) for call in calls]

        def kernel(*refs):
            in_refs, out_refs = refs[: sum(ins)], refs[sum(ins) :]
            for call, count, size in zip(calls, ins, sizes, strict=True):
                call[0](*in_refs[:count], *out_refs[:size])
                in_refs, out_refs = in_refs[count:], out_refs[size:]

        outs, operands, direct = [], [], []
        for _, _, call_outs, call_operands, call_direct in calls:
            direct += [len(outs) + at for at in call_direct]
            outs += call_outs
            operands += call_operands
        name = "__".join(call[1] for call in calls)
        results = self.call(kernel, name, outs, operands, direct=direct, flops=STEP_FLOPS)
        for work, size in zip(works, sizes, strict=True):
            part, results = results[:size], results[size:]
            for _ in itertools.islice(resume(work, part), 1):
                raise ValueError("second call")


def sds(shape, dtype):
    return jax.ShapeDtypeStruct(shape, dtype)


def onehot_of(bucket_ref, span):
    buckets = bucket_ref[...]
    hot = buckets == lax.broadcasted_iota(jnp.int32, (span, buckets.shape[1]), 0)
    return jnp.where(hot, 1.0, 0.0).astype(BF16)


def project_kernel(
    bucket_hbm, hidden_hbm, wq_hbm, bq_hbm, wk_hbm, bk_hbm, wv_hbm, bv_hbm, table_hbm, wout_hbm,
    q_ref, k_ref, v_ref, eq_ref, ek_ref, mine_ref,
    bucket_ref, hidden_ref, weight_ref, bq_ref, bk_ref, bv_ref, table_ref, quarter_ref, sems,
):
    rows = quarter_ref.shape[0]
    first = pl.multiple_of(lax.rem(lax.axis_index("dp"), QUARTERS) * rows, rows)
    cols = q_ref.shape[1]
    weights = [weight_ref.at[:, at * cols : (at + 1) * cols] for at in range(3)]
    sources = (
        wout_hbm.at[pl.ds(first, rows)], hidden_hbm, wq_hbm, wk_hbm, wv_hbm, bq_hbm, bk_hbm, bv_hbm,
        table_hbm, bucket_hbm,
    )
    targets = (
        quarter_ref, hidden_ref, *weights, bq_ref, bk_ref, bv_ref, table_ref, bucket_ref,
    )
    copies = [
        pltpu.make_async_copy(source, target, sems.at[at])
        for at, (source, target) in enumerate(zip(sources, targets, strict=True))
    ]
    for copy in copies:
        copy.start()
    copies[0].wait()
    mine_ref[...] = quarter_ref[...].astype(F32)
    for copy in copies[1:8]:
        copy.wait()
    bias = jnp.concatenate([ref[...].astype(F32)[None, :] for ref in (bq_ref, bk_ref, bv_ref)], axis=1)
    rows = (dot_nn(hidden_ref[...], weight_ref[...]) + bias).astype(BF16)
    for at, ref in enumerate((q_ref, k_ref, v_ref)):
        ref[...] = rows[:, at * cols : (at + 1) * cols]
    for copy in copies[8:]:
        copy.wait()
    table = table_ref[...]
    onehot = onehot_of(bucket_ref, table.shape[0])
    both = (dot_nn(table, weight_ref[:, : 2 * cols]) + bias[:, : 2 * cols]).astype(BF16)
    spread_out = dot_tn(onehot, both).astype(BF16)
    eq_ref[...] = spread_out[:, :cols]
    ek_ref[...] = spread_out[:, cols:]


def project(line, buckets, hidden, wq, bq, wk, bk, wv, bv, table, wout):
    seq_len = hidden.shape[0]
    cols = wq.shape[1]
    rows = wout.shape[0] // QUARTERS
    outs = [sds((seq_len, cols), BF16)] * 3 + [sds((2 * seq_len, cols), BF16)] * 2
    outs += [sds((rows, wout.shape[1]), F32)]
    operands = (buckets, hidden, wq, bq, wk, bk, wv, bv, table, wout)
    shapes = [buckets, hidden, sds((wq.shape[0], 3 * cols), wq.dtype), bq, bk, bv, table]
    scratch = [pltpu.VMEM(array.shape, array.dtype) for array in shapes]
    scratch += [pltpu.VMEM((rows, wout.shape[1]), wout.dtype)]
    operands = [pltpu.with_memory_space_constraint(operand, pltpu.HBM) for operand in operands]
    scratch += [pltpu.SemaphoreType.DMA((len(operands),))]
    return line.call(
        project_kernel, "project", outs, operands, scratch=scratch, space=pltpu.HBM
    )


def assemble_kernel(own_ref, *refs):
    out_ref = refs[-1]
    side, me = lax.axis_index("head"), lax.rem(lax.axis_index("dp"), QUARTERS)
    out_ref[side] = own_ref[...]
    for origin, ref in enumerate(refs[:-1]):
        rows = ref.shape[0]
        first = pl.multiple_of((me ^ origin) * rows, rows)
        out_ref[1 - side, pl.ds(first, rows), :] = ref[...].astype(BF16)


def assemble(line, own, quarters):
    rows, width = own.shape
    out = sds((2, rows, width), BF16)
    (joined,) = line.call(assemble_kernel, "assemble", [out], (own, *quarters))
    return joined.reshape(2 * rows, width)


def half_masks():
    lane = lax.broadcasted_iota(jnp.int32, (1, LANES), 1)
    return [lane // HEAD_DIM == side for side in range(LANES // HEAD_DIM)]


def apart(masks, value):
    zero = jnp.zeros_like(value)
    return jnp.concatenate([jnp.where(mask, value, zero) for mask in masks], axis=0)


def join(masks, stacked):
    rows = stacked.shape[0] // 2
    return jnp.where(masks[0], stacked[:rows], stacked[rows:])


def skewed(stacked, shift):
    rows = stacked.shape[0] // 2
    parts = [
        pltpu.roll(part, shift, 1, stride=1, stride_axis=0)
        for part in (stacked[:rows], stacked[rows:])
    ]
    return jnp.concatenate(parts, axis=0)


def attend_kernel(at, height, len_ref, q_ref, k_ref, v_ref, eq_ref, ek_ref, ctx_ref, att_ref):
    seq_len = k_ref.shape[0]
    length = len_ref[0]
    scale = 1.0 / math.sqrt(3 * HEAD_DIM)
    masks = half_masks()
    key_valid = lax.broadcasted_iota(jnp.int32, (1, seq_len), 1) < length
    rows = at * height + lax.broadcasted_iota(jnp.int32, (height, 1), 0)
    rows = jnp.concatenate([rows, rows], axis=0)
    query_valid = rows < length
    row_start = seq_len - height - height * at
    @pl.loop(0, q_ref.shape[1] // LANES)
    def _(pair):
        cols = pl.ds(pl.multiple_of(pair * LANES, LANES), LANES)
        q_pair = q_ref[at * height : (at + 1) * height, cols]
        k_pair = k_ref[:, cols]
        v_pair = v_ref[:, cols]
        rel_window = ek_ref[row_start : row_start + seq_len + height, cols]
        q_two = apart(masks, q_pair)
        content = dot_nt(q_two, k_pair)
        picked = skewed(dot_nt(q_two, rel_window), seq_len + 1)[:, :seq_len]
        blocks = []
        for block in range(seq_len // LANES):
            start = seq_len - LANES - LANES * block + height * at
            window = eq_ref[start : start + LANES + height, cols]
            k_two = apart(masks, k_pair[block * LANES : (block + 1) * LANES])
            tall = skewed(dot_nt(k_two, window), height + 1)[:, :height]
            blocks.append(jnp.concatenate([tall[:LANES].T, tall[LANES:].T], axis=0))
        flipped = jnp.concatenate(blocks, axis=1)
        scores = jnp.where(key_valid, scale * (content + picked + flipped), MASKED)
        peak = jnp.max(scores, axis=-1, keepdims=True)
        weight = jnp.exp(scores - peak)
        total = jnp.sum(weight, axis=-1, keepdims=True)
        keep = jnp.where(query_valid, 1.0 / total, 0.0)
        attend = (weight * keep).astype(BF16)
        att_ref[2 * pair] = attend[:height]
        att_ref[2 * pair + 1] = attend[height:]
        ctx_ref[:, cols] = join(masks, dot_nn(attend, v_pair)).astype(BF16).astype(F32)


def attend(line, at, height, lengths, q, k, v, eq, ek):
    seq_len, cols = q.shape
    heads = cols // HEAD_DIM
    outs = [sds((height, cols), F32), sds((heads, height, seq_len), BF16)]
    return line.call(
        functools.partial(attend_kernel, at, height), f"attend_{at}", outs,
        (lengths, q, k, v, eq, ek), scalars=1,
    )


def norm_back_kernel(
    start, dn_own_ref, dn_other_ref, d_two_ref, xhat_ref, rstd_ref, gain_ref, wout_ref,
    d_one_ref, d_mixed_ref, d_ctx_ref, vec_ref,
):
    rows = slice(start, start + dn_own_ref.shape[0])
    d_normed = (dn_own_ref[...] + dn_other_ref[...]) + d_two_ref[rows]
    xhat = xhat_ref[rows]
    vec_ref[0:1, :] = jnp.sum(d_normed * xhat, axis=0, keepdims=True)
    vec_ref[1:2, :] = jnp.sum(d_normed, axis=0, keepdims=True)
    scaled = d_normed * gain_ref[...].astype(F32)[None, :]
    mean_a = jnp.mean(scaled, axis=-1, keepdims=True)
    mean_b = jnp.mean(scaled * xhat, axis=-1, keepdims=True)
    d_one = rstd_ref[rows] * (scaled - mean_a - xhat * mean_b)
    d_one_ref[...] = d_one
    vec_ref[2:3, :] = jnp.sum(d_one, axis=0, keepdims=True)
    d_mixed = d_one.astype(BF16)
    d_mixed_ref[...] = d_mixed
    d_ctx_ref[...] = dot_nt(d_mixed, wout_ref[...]).astype(BF16)


def norm_back(line, at, start, dn_own, dn_other, d_two, xhat, rstd, gain, wout):
    height, width = dn_own.shape
    outs = [
        sds((height, width), F32),
        sds((height, width), BF16),
        sds((height, wout.shape[0]), BF16),
        sds((8, width), F32),
    ]
    operands = (dn_own, dn_other, d_two, xhat, rstd, gain, wout)
    return line.call(
        functools.partial(norm_back_kernel, start), f"norm_back_{at}", outs, operands,
        flops=BACK_FLOPS,
    )


def attend_back_kernel(
    at, height, count, first, last, d_ctx_ref, q_ref, k_ref, v_ref, eq_ref, ek_ref, *refs
):
    att_refs, refs = refs[:count], refs[count:]
    if not first:
        refs = refs[4:]
    dq_ref, dk_ref, dv_ref, deq_ref, dek_ref = refs[:5]
    seq_len = k_ref.shape[0]
    scale = 1.0 / math.sqrt(3 * HEAD_DIM)
    masks = half_masks()

    def anti(size):
        row = lax.broadcasted_iota(jnp.int32, (size, size), 0)
        col = lax.broadcasted_iota(jnp.int32, (size, size), 1)
        return jnp.where(row + col == size - 1, 1.0, 0.0).astype(BF16)

    anti_rows = anti(height)
    anti_keys = anti(LANES)
    row_start = seq_len - height - height * at
    if first:
        dk_ref[...] = jnp.zeros_like(dk_ref)
        dv_ref[...] = jnp.zeros_like(dv_ref)
        deq_ref[...] = jnp.zeros_like(deq_ref)
        dek_ref[...] = jnp.zeros_like(dek_ref)

    @pl.loop(0, q_ref.shape[1] // LANES)
    def _(pair):
        cols = pl.ds(pl.multiple_of(pair * LANES, LANES), LANES)
        q_pair = q_ref[at * height : (at + 1) * height, cols]
        k_pair = k_ref[:, cols]
        v_pair = v_ref[:, cols]
        ctx_pair = d_ctx_ref[:, cols]
        rel_window = ek_ref[row_start : row_start + seq_len + height, cols]
        q_turned = dot_nn(anti_rows, q_pair).astype(BF16)
        weight = jnp.concatenate(
            [jnp.concatenate([ref[2 * pair + side] for ref in att_refs], axis=0) for side in range(2)],
            axis=0,
        )
        d_att = dot_nt(apart(masks, ctx_pair), v_pair)
        soft = weight.astype(F32)
        inner = jnp.sum(d_att * soft, axis=-1, keepdims=True)
        d_scores = (soft * (d_att - inner)).astype(BF16)
        sides = [d_scores[:height], d_scores[height:]]
        weight_wide = jnp.concatenate([weight[:height], weight[height:]], axis=1)
        dv_ref[:, cols] += join(masks, dot_tn(weight_wide, ctx_pair))
        d_q = join(masks, dot_nn(d_scores, k_pair))
        d_scores_t = [side.T for side in sides]
        d_k = join(masks, dot_nn(jnp.concatenate(d_scores_t, axis=0), q_pair))
        turned = dot_nn(anti_rows, jnp.concatenate(sides, axis=1))
        space = jnp.zeros((height, height), F32)
        turned = [
            jnp.concatenate([turned[:, side * seq_len : (side + 1) * seq_len], space], axis=1)
            for side in range(2)
        ]
        turned = skewed(jnp.concatenate(turned, axis=0), 0).astype(BF16)
        d_q_turned = join(masks, dot_nn(turned, rel_window))
        turned_wide = jnp.concatenate([turned[:height], turned[height:]], axis=1)
        d_rel_k = join(masks, dot_tn(turned_wide, q_turned))
        dek_ref[row_start : row_start + seq_len + height, cols] += scale * d_rel_k

        def turn_back(matrix, value):
            high = value.astype(BF16)
            rest = (value - high.astype(F32)).astype(BF16)
            both = dot_nn(matrix, jnp.concatenate([high, rest], axis=1))
            return both[:, :LANES] + both[:, LANES:]

        dq_ref[:, cols] = (scale * (d_q + turn_back(anti_rows, d_q_turned))).astype(BF16)
        backs = []
        for block in range(seq_len // LANES):
            start = seq_len - LANES - LANES * block + height * at
            rows = slice(block * LANES, (block + 1) * LANES)
            window = eq_ref[start : start + LANES + height, cols]
            tall = dot_nn(anti_keys, jnp.concatenate([side[rows] for side in d_scores_t], axis=1))
            space = jnp.zeros((LANES, LANES), F32)
            tall = [
                jnp.concatenate([tall[:, side * height : (side + 1) * height], space], axis=1)
                for side in range(2)
            ]
            tall = skewed(jnp.concatenate(tall, axis=0), 0).astype(BF16)
            backs.append(join(masks, dot_nn(tall, window)))
            k_turned = apart(masks, dot_nn(anti_keys, k_pair[rows]).astype(BF16))
            deq_ref[start : start + LANES + height, cols] += scale * dot_tn(tall, k_turned)
        for block, value in enumerate(backs):
            rows = slice(block * LANES, (block + 1) * LANES)
            dk_ref[rows, cols] += scale * (d_k[rows] + turn_back(anti_keys, value))
    if last:
        dk_low_ref, dv_low_ref = refs[5:]
        dk_low_ref[...] = dk_ref[...].astype(BF16)
        dv_low_ref[...] = dv_ref[...].astype(BF16)


def attend_back(line, at, height, last, d_ctx, q, k, v, eq, ek, att, carried):
    seq_len, cols = q.shape
    operands = [d_ctx, q, k, v, eq, ek, *att, *carried]
    outs = [
        sds((height, cols), BF16),
        sds((seq_len, cols), F32),
        sds((seq_len, cols), F32),
        sds((2 * seq_len, cols), F32),
        sds((2 * seq_len, cols), F32),
    ]
    if last:
        outs += [sds((seq_len, cols), BF16)] * 2
    base = 6 + len(att)
    return line.call(
        functools.partial(attend_back_kernel, at, height, len(att), not carried, last),
        f"attend_back_{at}", outs, operands,
        aliases={base + place: 1 + place for place in range(4)} if carried else {},
        flops=BACK_FLOPS,
    )


def feed_kernel(
    at, height, count, wout_ref, bout_ref, hidden_ref, gain_ref, shift_ref, win_ref, bin_ref,
    wdown_ref, *refs,
):
    own_refs, other_refs = refs[:count], refs[count : 2 * count]
    xhat_ref, rstd_ref, normed_ref, act_ref, slope_ref, low_ref = refs[2 * count :]
    own = jnp.concatenate([ref[...] for ref in own_refs], axis=0)
    other = jnp.concatenate([ref[...] for ref in other_refs], axis=0)
    first = lax.axis_index("head") == 0
    ctx = jnp.concatenate([jnp.where(first, own, other), jnp.where(first, other, own)], axis=1)
    ctx = ctx.astype(BF16)
    mixed = dot_nn(ctx, wout_ref[...])
    hidden = hidden_ref[at * height : (at + 1) * height].astype(F32)
    resid = mixed + bout_ref[...].astype(F32)[None, :] + hidden
    center = resid - jnp.mean(resid, axis=-1, keepdims=True)
    spread = jnp.mean(center * center, axis=-1, keepdims=True)
    rstd = lax.rsqrt(spread + EPSILON)
    xhat = center * rstd
    xhat_ref[...] = xhat
    rstd_ref[...] = rstd
    normed = xhat * gain_ref[...].astype(F32)[None, :] + shift_ref[...].astype(F32)[None, :]
    low = normed.astype(BF16)
    normed_ref[...] = low
    units = win_ref.shape[1]
    step = units // 3
    total = None
    bias = bin_ref[...].astype(F32)[None, :]
    for part in range(3):
        cols = slice(part * step, (part + 1) * step)
        inner = dot_nn(low, win_ref[:, cols]) + bias[:, cols]
        phi = 0.5 * (1.0 + lax.erf(inner * math.sqrt(0.5)))
        act = (inner * phi).astype(BF16)
        slope = phi + inner * (jnp.exp(-0.5 * inner * inner) * (1.0 / math.sqrt(2 * math.pi)))
        act_ref[:, cols] = act
        slope_ref[:, cols] = slope
        term = dot_nn(act, wdown_ref[cols, :])
        total = term if total is None else total + term
    low_ref[...] = total


def feed(line, at, height, own, other, wout, bout, hidden, gain, shift, win, b_in, wdown):
    width = hidden.shape[1]
    units = win.shape[1]
    outs = [
        sds((height, width), F32),
        sds((height, 1), F32),
        sds((height, width), BF16),
        sds((height, units), BF16),
        sds((height, units), F32),
        sds((height, width), F32),
    ]
    operands = (wout, bout, hidden, gain, shift, win, b_in, wdown, *own, *other)
    return line.call(
        functools.partial(feed_kernel, at, height, len(own)), f"feed_{at}", outs, operands,
        flops=BACK_FLOPS if at else 1024,
    )


def feed_back_kernel(
    at, height, count, low_own_ref, low_other_ref, xhat_one_ref, gain_one_ref, shift_one_ref, bdown_ref,
    gain_ref, shift_ref, cot_ref, slope_ref, win_ref, wdown_ref,
    *refs,
):
    before, refs = refs[:count], refs[count:]
    out_ref, d_two_ref, d_low_ref, d_inner_ref, vec_ref, bin_ref, *dn_refs = refs
    normed = xhat_one_ref[...] * gain_one_ref[...].astype(F32)[None, :]
    normed = normed + shift_one_ref[...].astype(F32)[None, :]
    resid = (low_own_ref[...] + low_other_ref[...]) + bdown_ref[...].astype(F32)[None, :] + normed
    center = resid - jnp.mean(resid, axis=-1, keepdims=True)
    spread = jnp.mean(center * center, axis=-1, keepdims=True)
    rstd = lax.rsqrt(spread + EPSILON)
    xhat = center * rstd
    gain = gain_ref[...].astype(F32)[None, :]
    value = (xhat * gain + shift_ref[...].astype(F32)[None, :]).astype(BF16)
    if out_ref.shape[0] == height:
        out_ref[...] = value
    else:
        for stream, ref in enumerate(before):
            out_ref[stream * height : (stream + 1) * height] = ref[...]
        out_ref[at * height : (at + 1) * height] = value
    err = cot_ref[at * height : (at + 1) * height].astype(F32)
    vec_ref[0:1, :] = jnp.sum(err * xhat, axis=0, keepdims=True)
    vec_ref[1:2, :] = jnp.sum(err, axis=0, keepdims=True)
    scaled = err * gain
    mean_a = jnp.mean(scaled, axis=-1, keepdims=True)
    mean_b = jnp.mean(scaled * xhat, axis=-1, keepdims=True)
    d_two = rstd * (scaled - mean_a - xhat * mean_b)
    d_two_ref[...] = d_two
    vec_ref[2:3, :] = jnp.sum(d_two, axis=0, keepdims=True)
    low = d_two.astype(BF16)
    d_low_ref[...] = low
    units = win_ref.shape[1]
    step = units // 3
    total = None
    for part in range(3):
        cols = slice(part * step, (part + 1) * step)
        d_act = dot_nt(low, wdown_ref[cols, :])
        d_inner = (d_act * slope_ref[:, cols]).astype(BF16)
        d_inner_ref[:, cols] = d_inner
        bin_ref[0:1, cols] = jnp.sum(d_inner.astype(F32), axis=0, keepdims=True)
        term = dot_nt(d_inner, win_ref[:, cols])
        total = term if total is None else total + term
    rows = dn_refs[0].shape[0]
    for piece, ref in enumerate(dn_refs):
        ref[...] = total[piece * rows : (piece + 1) * rows]


def feed_back(
    line, at, height, rows, before, low_own, low_other, xhat, gain_one, shift_one, bdown, gain,
    shift, cot, slope, win, wdown,
):
    width = cot.shape[1]
    units = win.shape[1]
    last = (at + 1) * height == cot.shape[0]
    before = before if last else []
    outs = [
        sds(cot.shape if last else (height, width), BF16),
        sds((height, width), F32),
        sds((height, width), BF16),
        sds((height, units), BF16),
        sds((8, width), F32),
        sds((8, units), F32),
    ]
    outs += [sds((rows, width), F32)] * (height // rows)
    operands = (
        low_own, low_other, xhat, gain_one, shift_one, bdown, gain, shift, cot, slope, win, wdown,
        *before,
    )
    return line.call(
        functools.partial(feed_back_kernel, at, height, len(before)), f"feed_back_{at}", outs,
        operands, direct=(0,) if last else (),
    )


def spread(order, me, total, kept_ref, sent_refs, cols):
    parts = 1 << len(order)
    height = total.shape[0] // parts
    for bit in (0, order[0]):

        @pl.when((me & order[0]) == bit)
        def _(bit=bit):
            for block in range(parts):
                origin = me ^ block
                place = 0
                for later in order[1:]:
                    place = 2 * place + ((origin >> (later.bit_length() - 1)) & 1)
                top = block * height
                if block & order[0] == bit:
                    kept_ref[place, :, cols] = total[top : top + height]
                else:
                    for ref in sent_refs:
                        ref[place, :, cols] = total[top : top + ref.shape[1]]
                        top += ref.shape[1]


def grad_kernel(order, groups, pieces, *refs):
    kept_ref, *sent_refs = refs[-1 - pieces :]
    me = lax.axis_index("dp")
    at, start = 0, 0
    for count in groups:
        terms = []
        for rights in count:
            terms.append((refs[at], refs[at + 1 : at + 1 + rights]))
            at += 1 + rights
        width = terms[0][1][0].shape[1]

        def part(index, terms=terms, start=start):
            total = None
            columns = pl.ds(pl.multiple_of(index * COLUMNS, COLUMNS), COLUMNS)
            for left_ref, right_refs in terms:
                right = jnp.concatenate([ref[:, columns] for ref in right_refs], axis=0)
                term = dot_tn(left_ref[...], right.astype(BF16))
                total = term if total is None else total + term
            target = pl.ds(pl.multiple_of(start + index * COLUMNS, COLUMNS), COLUMNS)
            spread(order, me, total, kept_ref, sent_refs, target)

        pl.loop(0, width // COLUMNS)(part)
        start += width


def halves(order, rows, cols, pieces):
    half, height = (1 << len(order)) // 2, rows >> len(order)
    return [sds((half, height, cols), F32)] + [sds((half, height // pieces, cols), F32)] * pieces


def grad_blocks(line, name, order, groups, pieces=1):
    width = groups[0][0][0].shape[1]
    cols = sum(group[0][1][0].shape[1] for group in groups)
    operands = [array for group in groups for left, right in group for array in (left, *right)]
    counts = [[len(right) for _, right in group] for group in groups]
    outs = halves(order, width, cols, pieces)
    return line.call(
        functools.partial(grad_kernel, order, counts, pieces), name, outs, operands,
        flops=GRAD_FLOPS,
    )


def rel_kernel(
    order, counts, table_rows, bucket_ref, deq_ref, dek_ref, wq_ref, wk_ref, dk_ref, dv_ref,
    *refs,
):
    groups = []
    for count in counts:
        groups.append(refs[:count])
        refs = refs[count:]
    dq_refs, one_refs, two_refs, unit_refs = groups
    relq_ref, relk_ref, kept_ref, *sent_refs, pack_ref = refs
    onehot = onehot_of(bucket_ref, table_rows)
    deq, dek = deq_ref[...], dek_ref[...]
    cols = deq.shape[1]
    d_rel = dot_nn(onehot, jnp.concatenate([deq, dek], axis=1).astype(BF16)).astype(BF16)
    relq_ref[...] = d_rel[:, :cols]
    relk_ref[...] = d_rel[:, cols:]
    total = dot_nt(d_rel, jnp.concatenate([wq_ref[...], wk_ref[...]], axis=1))
    width = total.shape[1]
    me = lax.axis_index("dp")
    spread(order, me, total, kept_ref, sent_refs, slice(0, width))

    def summed(value):
        return jnp.sum(value.astype(F32), axis=0, keepdims=True)

    def over(stream_refs):
        value = stream_refs[0][...]
        for ref in stream_refs[1:]:
            value = value + ref[...]
        return value

    one, two, unit = over(one_refs), over(two_refs), over(unit_refs)
    d_bias = summed(dq_refs[0][...])
    for ref in dq_refs[1:]:
        d_bias = d_bias + summed(ref[...])
    vectors = [
        d_bias + summed(deq),
        summed(dk_ref[...]) + summed(dek),
        summed(dv_ref[...]),
        one[2:3], one[0:1], one[1:2], unit[0:1], two[2:3], two[0:1], two[1:2],
    ]
    pack_ref[...] = jnp.zeros_like(pack_ref)
    row = 0
    for vector in vectors:
        for piece in range(vector.shape[1] // LANES):
            pack_ref[row : row + 1, :] = vector[:, piece * LANES : (piece + 1) * LANES]
            row += 1
    spread(order, me, pack_ref[...], kept_ref, sent_refs, slice(width, width + LANES))


def rel_grads(line, order, span, buckets, deq, dek, wq, wk, dk, dv, dq, one, two, unit):
    width, cols = wq.shape
    outs = [sds((span, cols), BF16)] * 2
    outs = outs + halves(order, span, width + LANES, REL_PIECES)
    operands = [buckets, deq, dek, wq, wk, dk, dv, *dq, *one, *two, *unit]
    return line.call(
        functools.partial(rel_kernel, order, [len(g) for g in (dq, one, two, unit)], span), "rel_grads", outs, operands,
        scratch=[pltpu.VMEM((span, LANES), F32)],
    )


def rel_split_kernel(own_ref, other_ref, table_ref, vector_ref):
    width = table_ref.shape[2]
    for at in range(2):
        total = own_ref[at] + other_ref[1 - at]
        table_ref[at] = total[:, :width]
        vector_ref[at] = total[:, width:]


def rel_split(own, other):
    count, rows, wide = own.shape
    outs = [sds((count, rows, wide - LANES), F32), sds((count, rows, LANES), F32)]
    return rel_split_kernel, "rel_split", outs, [own, other], ()


def rel_join_kernel(own_ref, other_ref, vector_ref, out_ref):
    width = own_ref.shape[2]
    out_ref[:, :, :width] = own_ref[...] + other_ref[...]
    out_ref[:, :, width:] = vector_ref[...]


def rel_join(own, other, vector):
    count, rows, width = own.shape
    outs = [sds((count, rows, width + vector.shape[2]), F32)]
    return rel_join_kernel, "rel_join", outs, [own, other, vector], ()


def hidden_join_kernel(own_ref, other_ref, *refs):
    out_ref = refs[-1]
    start = 0
    for ref in refs[:-1]:
        rows = slice(start, start + ref.shape[0])
        out_ref[rows] = ((own_ref[rows] + other_ref[rows]) + ref[...]).astype(BF16)
        start += ref.shape[0]


def hidden_join(own, other, d_one):
    outs = [sds(own.shape, BF16)]
    return hidden_join_kernel, "hidden_join", outs, [own, other, *d_one], (0,)


def unpack_kernel(origins, count, *refs):
    shared_refs, (table_ref, *vector_refs) = refs[:count], refs[count:]
    width = table_ref.shape[2]
    height = table_ref.shape[1]
    me = lax.axis_index("dp")
    places = [(ref, at) for ref in shared_refs for at in range(ref.shape[0])]
    rows = sum(ref.shape[0] for ref in vector_refs) // LANES
    lines = [
        (ref, piece) for ref in vector_refs for piece in range(ref.shape[0] // LANES)
    ]
    for (shared_ref, at), origin in zip(places, origins, strict=True):
        table_ref[me ^ origin] = shared_ref[at, :, :width]
        for block in range((rows + height - 1) // height):

            @pl.when(me ^ origin == block)
            def _(shared_ref=shared_ref, at=at, block=block):
                for row in range(block * height, min(rows, (block + 1) * height)):
                    ref, piece = lines[row]
                    inner = row % height
                    line = shared_ref[at, inner : inner + 1, width:]
                    ref[pl.ds(piece * LANES, LANES)] = line.reshape(LANES)


def unpack(origins, pieces, sizes):
    height, wide = pieces[0].shape[1:]
    outs = [sds((len(origins), height, wide - LANES), F32)] + [sds((size,), F32) for size in sizes]
    kernel = functools.partial(unpack_kernel, origins, len(pieces))
    return kernel, "unpack", outs, list(pieces), range(len(outs))


def hidden_kernel(dk_ref, dv_ref, wq_ref, wk_ref, wv_ref, *refs):
    out_ref = refs[-1]
    out_ref[...] = dot_nt(dk_ref[...], wk_ref[...]) + dot_nt(dv_ref[...], wv_ref[...])
    start = 0
    for ref in refs[:-1]:
        out_ref[start : start + ref.shape[0]] += dot_nt(ref[...], wq_ref[...])
        start += ref.shape[0]


def hidden_grad(line, dk, dv, wq, wk, wv, dq):
    out = sds((dk.shape[0], wq.shape[0]), F32)
    (total,) = line.call(
        hidden_kernel, "hidden_grad", [out], (dk, dv, wq, wk, wv, *dq)
    )
    return total


def bits_of(parts):
    return [1 << b for b in range(parts.bit_length() - 1)]


def swap_head(value):
    return lax.ppermute(value, "head", [(0, 1), (1, 0)])


def flip(value, parts, bit):
    return lax.ppermute(value, "dp", [(i, i ^ bit) for i in range(parts)])


def together(*values):
    return lax.optimization_barrier(values)


def step_kernel(kept_ref, *refs):
    *arrived_refs, kept_out, sent_out = refs
    half = kept_out.shape[0]
    top = 0
    for ref in arrived_refs:
        rows = slice(top, top + ref.shape[1])
        kept_out[:, rows] = kept_ref[:half, rows] + ref[:half]
        sent_out[:, rows] = kept_ref[half:, rows] + ref[half:]
        top += ref.shape[1]


class Scatter:
    def __init__(self, line, name, kept, *sent, order):
        self.line, self.name, self.order = line, name, list(order)
        self.parts = 1 << len(self.order)
        self.kept = kept
        self.send(sent)

    def send(self, sent):
        self.bit = self.order.pop(0)
        self.arrived = [flip(piece, self.parts, self.bit) for piece in sent]

    def step(self):
        shape = (self.kept.shape[0] // 2, *self.kept.shape[1:])
        self.kept, sent = yield (
            step_kernel, f"{self.name}_{self.bit}", [sds(shape, F32)] * 2,
            [self.kept, *self.arrived], (),
        )
        self.send([sent])

    def rest(self, left=0):
        while len(self.order) > left:
            self.line.group([self.step()])

    def exchange(self):
        def add(kept_ref, arrived_ref, out_ref):
            out_ref[...] = kept_ref[...] + arrived_ref[...]

        self.rest(1)
        outs = [sds(self.kept.shape, F32)]
        (self.both,) = yield add, f"{self.name}_{self.bit}", outs, [self.kept, *self.arrived], ()
        bit = self.order.pop(0)
        self.both_other, self.origins = flip(self.both, self.parts, bit), [0, bit]

    def finish(self, widths):
        def kernel(kept_ref, arrived_ref, *out_refs):
            start = 0
            for ref in out_refs:
                cols = slice(start, start + ref.shape[1])
                ref[...] = kept_ref[0, :, cols] + arrived_ref[0, :, cols]
                start += ref.shape[1]

        self.rest()
        outs = [sds((self.kept.shape[1], width), F32) for width in widths]
        operands = [self.kept, *self.arrived]
        self.sums = yield kernel, f"{self.name}_sum", outs, operands, range(len(outs))


def pack_kernel(*refs):
    start = 0
    for ref in refs[:-1]:
        refs[-1][start : start + ref.shape[0]] = ref[...]
        start += ref.shape[0]


class Gather:
    def __init__(self, line, value, origins, parts, order):
        self.line, self.parts, self.order = line, parts, list(order)
        self.pieces, self.origins = [value], origins
        self.send(value)

    def send(self, sent):
        bit = self.order.pop(0)
        self.pieces.append(flip(sent, self.parts, bit))
        self.origins = self.origins + [origin ^ bit for origin in self.origins]

    def step(self):
        shape = (len(self.origins), *self.pieces[0].shape[1:])
        name = f"pack_{len(self.origins)}"
        (sent,) = yield pack_kernel, name, [sds(shape, F32)], list(self.pieces), ()
        self.send(sent)

    def rest(self):
        while self.order:
            self.line.group([self.step()])


def words_of(text):
    words, open_word = [], None
    for letter in text:
        if letter == "(":
            open_word = ""
        elif letter == ")":
            words.append(open_word)
            open_word = None
        elif open_word is not None:
            open_word += letter
        else:
            words.append(letter)
    return words


def on_device(parts, *arguments):
    (
        hidden_in, lengths, cotangent, w_query, b_query, w_key, b_key, w_value, b_value,
        w_out, b_out, ln1_gain, ln1_bias, w_in, b_in, w_down, b_down, ln2_gain, ln2_bias,
        rel_table,
    ) = arguments
    seq_len, width = hidden_in.shape
    height = seq_len // STREAMS
    streams = range(STREAMS)
    bits = bits_of(parts)

    buckets = jnp.asarray(distance_buckets(seq_len)[None, :])
    line = Line()
    q, k, v, eq, ek, mine = project(
        line, buckets, hidden_in, w_query, b_query, w_key, b_key, w_value, b_value, rel_table,
        w_out,
    )
    fetched = swap_head(mine)
    contexts, attends = [], []
    for at in range(CONTEXTS * STREAMS):
        context, attended = attend(line, at, height // CONTEXTS, lengths, q, k, v, eq, ek)
        contexts.append(context)
        attends.append(attended)
    fetched, contexts[0] = together(fetched, contexts[0])
    quarters = [fetched, flip(fetched, parts, 1), flip(fetched, parts, 2)]
    quarters.append(flip(quarters[2], parts, 1))
    w_out_all = assemble(line, w_out, quarters)
    others = [swap_head(context) for context in contexts]
    of_stream = [slice(CONTEXTS * at, CONTEXTS * (at + 1)) for at in streams]
    fed = [
        feed(
            line, at, height, contexts[of_stream[at]], others[of_stream[at]],
            w_out_all, b_out, hidden_in, ln1_gain, ln1_bias, w_in, b_in, w_down,
        )
        for at in streams
    ]
    backs = []
    for at in streams:
        xhat, rstd, normed, act, slope, lowered = fed[at]
        backs.append(
            feed_back(
                line, at, height, height, [b[0] for b in backs], lowered, swap_head(lowered), xhat,
                ln1_gain, ln1_bias, b_down, ln2_gain, ln2_bias, cotangent, slope, w_in, w_down,
            )
        )
    output = backs[-1][0]
    crossed = bits[:1] + bits[2:] + bits[1:2]
    g_down = grad_blocks(
        line, "grad_down", bits, [[(backs[at][2], fed[at][3:4]) for at in streams]]
    )
    down = Scatter(line, "down", *g_down, order=bits)
    g_in = grad_blocks(
        line, "grad_in", crossed, [[(fed[at][2], backs[at][3:4]) for at in streams]]
    )
    inner = Scatter(line, "inner", *g_in, order=crossed)
    norms, dq = [], []
    carried = ()
    for at in streams:
        xhat, rstd = fed[at][:2]
        d_two, dn = backs[at][1], backs[at][6]
        norms.append(
            norm_back(line, at, 0, dn, swap_head(dn), d_two, xhat, rstd, ln1_gain, w_out)
        )
        if at == 0:
            line.group([down.step()])
            line.group([inner.step()])
        d_q, *carried = attend_back(
            line, at, height, at == streams[-1], norms[at][2], q, k, v, eq, ek,
            attends[of_stream[at]], carried,
        )
        dq.append(d_q)
    deq, dek, dk, dv = carried[2:]
    cols = q.shape[1]
    hidden_parts = [hidden_in[at * height : (at + 1) * height] for at in streams]
    chains = {"d": down, "i": inner}
    made = {}

    def start_rel():
        made["relq"], made["relk"], *blocks = rel_grads(
            line, bits, rel_table.shape[0], buckets, deq, dek, w_query, w_key, dk, dv, dq,
            [n[3] for n in norms], [b[4] for b in backs], [b[5] for b in backs],
        )
        chains["r"] = Scatter(line, "rel", *blocks, order=bits)

    def start_value_out():
        blocks = grad_blocks(
            line, "grad_value_out", bits,
            [
                [(hidden_in, [dv])],
                [(norms[at][1], contexts[of_stream[at]]) for at in streams],
            ],
            HEAD_PIECES,
        )
        chains["v"] = Scatter(line, "value_out", *blocks, order=bits)

    def start_query_key():
        blocks = grad_blocks(
            line, "grad_query_key", bits,
            [
                [*zip(hidden_parts, [[d] for d in dq], strict=True), (rel_table, [made["relq"]])],
                [(hidden_in, [dk]), (rel_table, [made["relk"]])],
            ],
            HEAD_PIECES,
        )
        chains["q"] = Scatter(line, "query_key", *blocks, order=bits)

    def start_hidden():
        made["hidden"] = hidden_grad(line, dk, dv, w_query, w_key, w_value, dq)
        made["hidden_other"] = swap_head(made["hidden"])

    def swap_rel():
        both, other = chains["r"].both, chains["r"].both_other
        made["own"], made["vectors"] = yield rel_split(both, other)
        made["own_other"] = swap_head(made["own"])

    def gather_rel():
        (joined,) = yield rel_join(made["own"], made["own_other"], made["vectors"])
        chains["p"] = Gather(line, joined, chains["r"].origins, parts, bits[-2::-1])

    def end_hidden():
        d_one = [n[0] for n in norms]
        made["grad_input"] = yield hidden_join(made["hidden"], made["hidden_other"], d_one)

    def end_rel():
        chains["p"].rest()
        sizes = [cols] * 3 + [width] * 3 + [w_in.shape[1]] + [width] * 3
        made["shared"] = yield unpack(chains["p"].origins, chains["p"].pieces, sizes)

    starters = {
        "L": start_rel, "G": start_value_out, "K": start_query_key, "Y": start_hidden,
    }
    steps = {
        "X": lambda: chains["r"].exchange(), "S": swap_rel, "J": gather_rel, "H": end_hidden,
        "U": end_rel,
    }
    widths = {"d": [w_in.shape[1]], "i": [w_in.shape[1]], "v": [cols, cols], "q": [cols, cols]}

    def work(letter):
        if letter in widths:
            return chains[letter].finish(widths[letter])
        return steps[letter]() if letter in steps else chains[letter.lower()].step()

    for word in words_of(TAIL):
        if word in starters:
            starters[word]()
        else:
            line.group([work(letter) for letter in word])
    (s_down,), (s_in,) = chains["d"].sums, chains["i"].sums
    (s_q, s_k), (s_v, s_out) = chains["q"].sums, chains["v"].sums
    (grad_input,) = made["grad_input"]
    table_blocks, *pieces = made["shared"]
    grad_rel_table = table_blocks.reshape(rel_table.shape)
    (
        grad_b_query, grad_b_key, grad_b_value, grad_b_out, grad_ln1_gain, grad_ln1_bias,
        grad_b_in, grad_b_down, grad_ln2_gain, grad_ln2_bias,
    ) = pieces
    return (
        output, grad_input, s_q, grad_b_query, s_k, grad_b_key, s_v, grad_b_value,
        s_out.T, grad_b_out, grad_ln1_gain, grad_ln1_bias, s_in, grad_b_in,
        s_down.T, grad_b_down, grad_ln2_gain, grad_ln2_bias, grad_rel_table,
    )


def solution(mesh):
    parts = mesh.shape["dp"]
    return jax.shard_map(
        functools.partial(on_device, parts),
        mesh=mesh,
        in_specs=(
            P("dp", None), P("dp"), P("dp", None),
            P(None, "head"), P("head"), P(None, "head"), P("head"), P(None, "head"), P("head"),
            P("head", None), P(), P(), P(),
            P(None, "head"), P("head"), P("head", None), P(), P(), P(), P(),
        ),
        out_specs=(
            P("dp", None), P("dp", None),
            P("dp", "head"), P("head"), P("dp", "head"), P("head"), P("dp", "head"), P("head"),
            P("head", "dp"), P(), P(), P(),
            P("dp", "head"), P("head"), P("head", "dp"), P(), P(), P(), P(),
        ),
        check_vma=False,
    )
```

```python
import functools
import itertools
import math

import jax
import jax.numpy as jnp
import numpy as np
from jax import lax
from jax.experimental import pallas as pl
from jax.experimental.pallas import tpu as pltpu
from jax.sharding import PartitionSpec as P

HEAD_DIM = 64
SPAN = 256
MAXPOS = 512
EPSILON = 1e-07
MASKED = -1000000000.0
LANES = 128
STREAMS = 2
CONTEXTS = 1
TAIL = "LYKGDIR(VQ)RDVXISQJiQqP(VH)dP(vU)"
REL_PIECES = 2
HEAD_PIECES = 1
QUARTERS = 4
COLUMNS = 384
BACK_FLOPS = 64 << 30
STEP_FLOPS = 1024
GRAD_FLOPS = 1024
VMEM_LIMIT = 8 * 1024 * 1024

BF16 = jnp.bfloat16
F32 = jnp.float32


def bucket_of(offsets, bucket_span, max_distance):
    middle = bucket_span // 2
    direction = np.sign(offsets)
    absolute = np.where((offsets < middle) & (offsets > -middle), middle - 1, np.abs(offsets))
    log_part = (
        np.ceil(np.log(absolute / middle) / np.log((max_distance - 1) / middle) * (middle - 1))
        + middle
    )
    bucket = np.where(absolute <= middle, offsets, log_part * direction).astype(np.int64)
    return np.clip(bucket + bucket_span, 0, 2 * bucket_span - 1).astype(np.int32)


def distance_buckets(seq_len):
    offsets = np.maximum(seq_len - 1 - np.arange(2 * seq_len), 1 - seq_len)
    return bucket_of(offsets, SPAN, MAXPOS)


def dot_nn(a, b):
    return lax.dot_general(a, b, (((1,), (0,)), ((), ())), preferred_element_type=F32)


def dot_nt(a, b):
    return lax.dot_general(a, b, (((1,), (1,)), ((), ())), preferred_element_type=F32)


def dot_tn(a, b):
    return lax.dot_general(a, b, (((0,), (0,)), ((), ())), preferred_element_type=F32)


def resume(work, results):
    try:
        yield work.send(results)
    except StopIteration:
        return


class Line:
    def __init__(self):
        self.last = ()

    def call(
        self, kernel, name, outs, operands, aliases=None, scalars=0, scratch=(), flops=1024,
        space=pltpu.VMEM, direct=(),
    ):
        in_specs = [pl.BlockSpec(memory_space=pltpu.SMEM)] * scalars
        in_specs += [pl.BlockSpec(memory_space=space)] * (len(operands) - scalars)
        in_specs += [pl.BlockSpec(memory_space=pl.ANY)] * len(self.last)
        count, skipped = len(operands), len(self.last)

        def body(*refs):
            kernel(*refs[:count], *refs[count + skipped :])

        results = pl.pallas_call(
            body,
            in_specs=in_specs,
            out_specs=[
                pl.BlockSpec() if at in direct else pl.BlockSpec(memory_space=pltpu.VMEM)
                for at in range(len(outs))
            ],
            out_shape=outs,
            scratch_shapes=list(scratch),
            input_output_aliases=aliases or {},
            compiler_params=pltpu.CompilerParams(vmem_limit_bytes=VMEM_LIMIT),
            cost_estimate=pl.CostEstimate(flops=flops, bytes_accessed=1024, transcendentals=0),
            name=name,
        )(*operands, *self.last)
        self.last = (min(results, key=lambda result: result.size * result.dtype.itemsize),)
        return results


    def group(self, works):
        calls = [next(work) for work in works]
        ins = [len(call[3]) for call in calls]
        sizes = [len(call[2]) for call in calls]

        def kernel(*refs):
            in_refs, out_refs = refs[: sum(ins)], refs[sum(ins) :]
            for call, count, size in zip(calls, ins, sizes, strict=True):
                call[0](*in_refs[:count], *out_refs[:size])
                in_refs, out_refs = in_refs[count:], out_refs[size:]

        outs, operands, direct = [], [], []
        for _, _, call_outs, call_operands, call_direct in calls:
            direct += [len(outs) + at for at in call_direct]
            outs += call_outs
            operands += call_operands
        name = "__".join(call[1] for call in calls)
        results = self.call(kernel, name, outs, operands, direct=direct, flops=STEP_FLOPS)
        for work, size in zip(works, sizes, strict=True):
            part, results = results[:size], results[size:]
            for _ in itertools.islice(resume(work, part), 1):
                raise ValueError("second call")


def sds(shape, dtype):
    return jax.ShapeDtypeStruct(shape, dtype)


def onehot_of(bucket_ref, span):
    buckets = bucket_ref[...]
    hot = buckets == lax.broadcasted_iota(jnp.int32, (span, buckets.shape[1]), 0)
    return jnp.where(hot, 1.0, 0.0).astype(BF16)


def project_kernel(
    bucket_hbm, hidden_hbm, wq_hbm, bq_hbm, wk_hbm, bk_hbm, wv_hbm, bv_hbm, table_hbm, wout_hbm,
    q_ref, k_ref, v_ref, eq_ref, ek_ref, mine_ref,
    bucket_ref, hidden_ref, weight_ref, bq_ref, bk_ref, bv_ref, table_ref, quarter_ref, sems,
):
    rows = quarter_ref.shape[0]
    first = pl.multiple_of(lax.rem(lax.axis_index("dp"), QUARTERS) * rows, rows)
    cols = q_ref.shape[1]
    weights = [weight_ref.at[:, at * cols : (at + 1) * cols] for at in range(3)]
    sources = (
        wout_hbm.at[pl.ds(first, rows)], hidden_hbm, wq_hbm, wk_hbm, wv_hbm, bq_hbm, bk_hbm, bv_hbm,
        table_hbm, bucket_hbm,
    )
    targets = (
        quarter_ref, hidden_ref, *weights, bq_ref, bk_ref, bv_ref, table_ref, bucket_ref,
    )
    copies = [
        pltpu.make_async_copy(source, target, sems.at[at])
        for at, (source, target) in enumerate(zip(sources, targets, strict=True))
    ]
    for copy in copies:
        copy.start()
    copies[0].wait()
    mine_ref[...] = quarter_ref[...].astype(F32)
    for copy in copies[1:8]:
        copy.wait()
    bias = jnp.concatenate([ref[...].astype(F32)[None, :] for ref in (bq_ref, bk_ref, bv_ref)], axis=1)
    rows = (dot_nn(hidden_ref[...], weight_ref[...]) + bias).astype(BF16)
    for at, ref in enumerate((q_ref, k_ref, v_ref)):
        ref[...] = rows[:, at * cols : (at + 1) * cols]
    for copy in copies[8:]:
        copy.wait()
    table = table_ref[...]
    onehot = onehot_of(bucket_ref, table.shape[0])
    both = (dot_nn(table, weight_ref[:, : 2 * cols]) + bias[:, : 2 * cols]).astype(BF16)
    spread_out = dot_tn(onehot, both).astype(BF16)
    eq_ref[...] = spread_out[:, :cols]
    ek_ref[...] = spread_out[:, cols:]


def project(line, buckets, hidden, wq, bq, wk, bk, wv, bv, table, wout):
    seq_len = hidden.shape[0]
    cols = wq.shape[1]
    rows = wout.shape[0] // QUARTERS
    outs = [sds((seq_len, cols), BF16)] * 3 + [sds((2 * seq_len, cols), BF16)] * 2
    outs += [sds((rows, wout.shape[1]), F32)]
    operands = (buckets, hidden, wq, bq, wk, bk, wv, bv, table, wout)
    shapes = [buckets, hidden, sds((wq.shape[0], 3 * cols), wq.dtype), bq, bk, bv, table]
    scratch = [pltpu.VMEM(array.shape, array.dtype) for array in shapes]
    scratch += [pltpu.VMEM((rows, wout.shape[1]), wout.dtype)]
    operands = [pltpu.with_memory_space_constraint(operand, pltpu.HBM) for operand in operands]
    scratch += [pltpu.SemaphoreType.DMA((len(operands),))]
    return line.call(
        project_kernel, "project", outs, operands, scratch=scratch, space=pltpu.HBM
    )


def assemble_kernel(own_ref, *refs):
    out_ref = refs[-1]
    side, me = lax.axis_index("head"), lax.rem(lax.axis_index("dp"), QUARTERS)
    out_ref[side] = own_ref[...]
    for origin, ref in enumerate(refs[:-1]):
        rows = ref.shape[0]
        first = pl.multiple_of((me ^ origin) * rows, rows)
        out_ref[1 - side, pl.ds(first, rows), :] = ref[...].astype(BF16)


def assemble(line, own, quarters):
    rows, width = own.shape
    out = sds((2, rows, width), BF16)
    (joined,) = line.call(assemble_kernel, "assemble", [out], (own, *quarters))
    return joined.reshape(2 * rows, width)


def half_masks():
    lane = lax.broadcasted_iota(jnp.int32, (1, LANES), 1)
    return [lane // HEAD_DIM == side for side in range(LANES // HEAD_DIM)]


def apart(masks, value):
    zero = jnp.zeros_like(value)
    return jnp.concatenate([jnp.where(mask, value, zero) for mask in masks], axis=0)


def join(masks, stacked):
    rows = stacked.shape[0] // 2
    return jnp.where(masks[0], stacked[:rows], stacked[rows:])


def skewed(stacked, shift):
    rows = stacked.shape[0] // 2
    parts = [
        pltpu.roll(part, shift, 1, stride=1, stride_axis=0)
        for part in (stacked[:rows], stacked[rows:])
    ]
    return jnp.concatenate(parts, axis=0)


def attend_kernel(at, height, len_ref, q_ref, k_ref, v_ref, eq_ref, ek_ref, ctx_ref, att_ref):
    seq_len = k_ref.shape[0]
    length = len_ref[0]
    scale = 1.0 / math.sqrt(3 * HEAD_DIM)
    masks = half_masks()
    key_valid = lax.broadcasted_iota(jnp.int32, (1, seq_len), 1) < length
    rows = at * height + lax.broadcasted_iota(jnp.int32, (height, 1), 0)
    rows = jnp.concatenate([rows, rows], axis=0)
    query_valid = rows < length
    row_start = seq_len - height - height * at
    @pl.loop(0, q_ref.shape[1] // LANES)
    def _(pair):
        cols = pl.ds(pl.multiple_of(pair * LANES, LANES), LANES)
        q_pair = q_ref[at * height : (at + 1) * height, cols]
        k_pair = k_ref[:, cols]
        v_pair = v_ref[:, cols]
        rel_window = ek_ref[row_start : row_start + seq_len + height, cols]
        q_two = apart(masks, q_pair)
        content = dot_nt(q_two, k_pair)
        picked = skewed(dot_nt(q_two, rel_window), seq_len + 1)[:, :seq_len]
        blocks = []
        for block in range(seq_len // LANES):
            start = seq_len - LANES - LANES * block + height * at
            window = eq_ref[start : start + LANES + height, cols]
            k_two = apart(masks, k_pair[block * LANES : (block + 1) * LANES])
            tall = skewed(dot_nt(k_two, window), height + 1)[:, :height]
            blocks.append(jnp.concatenate([tall[:LANES].T, tall[LANES:].T], axis=0))
        flipped = jnp.concatenate(blocks, axis=1)
        scores = jnp.where(key_valid, scale * (content + picked + flipped), MASKED)
        peak = jnp.max(scores, axis=-1, keepdims=True)
        weight = jnp.exp(scores - peak)
        total = jnp.sum(weight, axis=-1, keepdims=True)
        keep = jnp.where(query_valid, 1.0 / total, 0.0)
        attend = (weight * keep).astype(BF16)
        att_ref[2 * pair] = attend[:height]
        att_ref[2 * pair + 1] = attend[height:]
        ctx_ref[:, cols] = join(masks, dot_nn(attend, v_pair)).astype(BF16).astype(F32)


def attend(line, at, height, lengths, q, k, v, eq, ek):
    seq_len, cols = q.shape
    heads = cols // HEAD_DIM
    outs = [sds((height, cols), F32), sds((heads, height, seq_len), BF16)]
    return line.call(
        functools.partial(attend_kernel, at, height), f"attend_{at}", outs,
        (lengths, q, k, v, eq, ek), scalars=1,
    )


def norm_back_kernel(
    start, dn_own_ref, dn_other_ref, d_two_ref, xhat_ref, rstd_ref, gain_ref, wout_ref,
    d_one_ref, d_mixed_ref, d_ctx_ref, vec_ref,
):
    rows = slice(start, start + dn_own_ref.shape[0])
    d_normed = (dn_own_ref[...] + dn_other_ref[...]) + d_two_ref[rows]
    xhat = xhat_ref[rows]
    vec_ref[0:1, :] = jnp.sum(d_normed * xhat, axis=0, keepdims=True)
    vec_ref[1:2, :] = jnp.sum(d_normed, axis=0, keepdims=True)
    scaled = d_normed * gain_ref[...].astype(F32)[None, :]
    mean_a = jnp.mean(scaled, axis=-1, keepdims=True)
    mean_b = jnp.mean(scaled * xhat, axis=-1, keepdims=True)
    d_one = rstd_ref[rows] * (scaled - mean_a - xhat * mean_b)
    d_one_ref[...] = d_one
    vec_ref[2:3, :] = jnp.sum(d_one, axis=0, keepdims=True)
    d_mixed = d_one.astype(BF16)
    d_mixed_ref[...] = d_mixed
    d_ctx_ref[...] = dot_nt(d_mixed, wout_ref[...]).astype(BF16)


def norm_back(line, at, start, dn_own, dn_other, d_two, xhat, rstd, gain, wout):
    height, width = dn_own.shape
    outs = [
        sds((height, width), F32),
        sds((height, width), BF16),
        sds((height, wout.shape[0]), BF16),
        sds((8, width), F32),
    ]
    operands = (dn_own, dn_other, d_two, xhat, rstd, gain, wout)
    return line.call(
        functools.partial(norm_back_kernel, start), f"norm_back_{at}", outs, operands,
        flops=BACK_FLOPS,
    )


def attend_back_kernel(
    at, height, count, first, last, d_ctx_ref, q_ref, k_ref, v_ref, eq_ref, ek_ref, *refs
):
    att_refs, refs = refs[:count], refs[count:]
    if not first:
        refs = refs[4:]
    dq_ref, dk_ref, dv_ref, deq_ref, dek_ref = refs[:5]
    seq_len = k_ref.shape[0]
    scale = 1.0 / math.sqrt(3 * HEAD_DIM)
    masks = half_masks()

    def anti(size):
        row = lax.broadcasted_iota(jnp.int32, (size, size), 0)
        col = lax.broadcasted_iota(jnp.int32, (size, size), 1)
        return jnp.where(row + col == size - 1, 1.0, 0.0).astype(BF16)

    anti_rows = anti(height)
    anti_keys = anti(LANES)
    row_start = seq_len - height - height * at
    if first:
        dk_ref[...] = jnp.zeros_like(dk_ref)
        dv_ref[...] = jnp.zeros_like(dv_ref)
        deq_ref[...] = jnp.zeros_like(deq_ref)
        dek_ref[...] = jnp.zeros_like(dek_ref)

    @pl.loop(0, q_ref.shape[1] // LANES)
    def _(pair):
        cols = pl.ds(pl.multiple_of(pair * LANES, LANES), LANES)
        q_pair = q_ref[at * height : (at + 1) * height, cols]
        k_pair = k_ref[:, cols]
        v_pair = v_ref[:, cols]
        ctx_pair = d_ctx_ref[:, cols]
        rel_window = ek_ref[row_start : row_start + seq_len + height, cols]
        q_turned = dot_nn(anti_rows, q_pair).astype(BF16)
        weight = jnp.concatenate(
            [jnp.concatenate([ref[2 * pair + side] for ref in att_refs], axis=0) for side in range(2)],
            axis=0,
        )
        d_att = dot_nt(apart(masks, ctx_pair), v_pair)
        soft = weight.astype(F32)
        inner = jnp.sum(d_att * soft, axis=-1, keepdims=True)
        d_scores = (soft * (d_att - inner)).astype(BF16)
        sides = [d_scores[:height], d_scores[height:]]
        weight_wide = jnp.concatenate([weight[:height], weight[height:]], axis=1)
        dv_ref[:, cols] += join(masks, dot_tn(weight_wide, ctx_pair))
        d_q = join(masks, dot_nn(d_scores, k_pair))
        d_scores_t = [side.T for side in sides]
        d_k = join(masks, dot_nn(jnp.concatenate(d_scores_t, axis=0), q_pair))
        turned = dot_nn(anti_rows, jnp.concatenate(sides, axis=1))
        space = jnp.zeros((height, height), F32)
        turned = [
            jnp.concatenate([turned[:, side * seq_len : (side + 1) * seq_len], space], axis=1)
            for side in range(2)
        ]
        turned = skewed(jnp.concatenate(turned, axis=0), 0).astype(BF16)
        d_q_turned = join(masks, dot_nn(turned, rel_window))
        turned_wide = jnp.concatenate([turned[:height], turned[height:]], axis=1)
        d_rel_k = join(masks, dot_tn(turned_wide, q_turned))
        dek_ref[row_start : row_start + seq_len + height, cols] += scale * d_rel_k

        def turn_back(matrix, value):
            high = value.astype(BF16)
            rest = (value - high.astype(F32)).astype(BF16)
            both = dot_nn(matrix, jnp.concatenate([high, rest], axis=1))
            return both[:, :LANES] + both[:, LANES:]

        dq_ref[:, cols] = (scale * (d_q + turn_back(anti_rows, d_q_turned))).astype(BF16)
        backs = []
        for block in range(seq_len // LANES):
            start = seq_len - LANES - LANES * block + height * at
            rows = slice(block * LANES, (block + 1) * LANES)
            window = eq_ref[start : start + LANES + height, cols]
            tall = dot_nn(anti_keys, jnp.concatenate([side[rows] for side in d_scores_t], axis=1))
            space = jnp.zeros((LANES, LANES), F32)
            tall = [
                jnp.concatenate([tall[:, side * height : (side + 1) * height], space], axis=1)
                for side in range(2)
            ]
            tall = skewed(jnp.concatenate(tall, axis=0), 0).astype(BF16)
            backs.append(join(masks, dot_nn(tall, window)))
            k_turned = apart(masks, dot_nn(anti_keys, k_pair[rows]).astype(BF16))
            deq_ref[start : start + LANES + height, cols] += scale * dot_tn(tall, k_turned)
        for block, value in enumerate(backs):
            rows = slice(block * LANES, (block + 1) * LANES)
            dk_ref[rows, cols] += scale * (d_k[rows] + turn_back(anti_keys, value))
    if last:
        dk_low_ref, dv_low_ref = refs[5:]
        dk_low_ref[...] = dk_ref[...].astype(BF16)
        dv_low_ref[...] = dv_ref[...].astype(BF16)


def attend_back(line, at, height, last, d_ctx, q, k, v, eq, ek, att, carried):
    seq_len, cols = q.shape
    operands = [d_ctx, q, k, v, eq, ek, *att, *carried]
    outs = [
        sds((height, cols), BF16),
        sds((seq_len, cols), F32),
        sds((seq_len, cols), F32),
        sds((2 * seq_len, cols), F32),
        sds((2 * seq_len, cols), F32),
    ]
    if last:
        outs += [sds((seq_len, cols), BF16)] * 2
    base = 6 + len(att)
    return line.call(
        functools.partial(attend_back_kernel, at, height, len(att), not carried, last),
        f"attend_back_{at}", outs, operands,
        aliases={base + place: 1 + place for place in range(4)} if carried else {},
        flops=BACK_FLOPS,
    )


def feed_kernel(
    at, height, count, wout_ref, bout_ref, hidden_ref, gain_ref, shift_ref, win_ref, bin_ref,
    wdown_ref, *refs,
):
    own_refs, other_refs = refs[:count], refs[count : 2 * count]
    xhat_ref, rstd_ref, normed_ref, act_ref, slope_ref, low_ref, bias_ref = refs[2 * count :]
    own = jnp.concatenate([ref[...] for ref in own_refs], axis=0)
    other = jnp.concatenate([ref[...] for ref in other_refs], axis=0)
    first = lax.axis_index("head") == 0
    ctx = jnp.concatenate([jnp.where(first, own, other), jnp.where(first, other, own)], axis=1)
    ctx = ctx.astype(BF16)
    mixed = dot_nn(ctx, wout_ref[...])
    hidden = hidden_ref[at * height : (at + 1) * height].astype(F32)
    resid = mixed + bout_ref[...].astype(F32)[None, :] + hidden
    center = resid - jnp.mean(resid, axis=-1, keepdims=True)
    spread = jnp.mean(center * center, axis=-1, keepdims=True)
    rstd = lax.rsqrt(spread + EPSILON)
    xhat = center * rstd
    xhat_ref[...] = xhat
    rstd_ref[...] = rstd
    normed = xhat * gain_ref[...].astype(F32)[None, :] + shift_ref[...].astype(F32)[None, :]
    low = normed.astype(BF16)
    normed_ref[...] = low
    units = win_ref.shape[1]
    step = units // 3
    bias_ref[...] = bin_ref[...].astype(F32)[None, :]
    low_ref[...] = jnp.zeros_like(low_ref)

    @pl.loop(0, 3)
    def _(part):
        cols = pl.ds(pl.multiple_of(part * step, step), step)
        inner = dot_nn(low, win_ref[:, cols]) + bias_ref[:, cols]
        phi = 0.5 * (1.0 + lax.erf(inner * math.sqrt(0.5)))
        act = (inner * phi).astype(BF16)
        slope = phi + inner * (jnp.exp(-0.5 * inner * inner) * (1.0 / math.sqrt(2 * math.pi)))
        act_ref[:, cols] = act
        slope_ref[:, cols] = slope
        low_ref[...] += dot_nn(act, wdown_ref[cols, :])


def feed(line, at, height, own, other, wout, bout, hidden, gain, shift, win, b_in, wdown):
    width = hidden.shape[1]
    units = win.shape[1]
    outs = [
        sds((height, width), F32),
        sds((height, 1), F32),
        sds((height, width), BF16),
        sds((height, units), BF16),
        sds((height, units), F32),
        sds((height, width), F32),
    ]
    operands = (wout, bout, hidden, gain, shift, win, b_in, wdown, *own, *other)
    return line.call(
        functools.partial(feed_kernel, at, height, len(own)), f"feed_{at}", outs, operands,
        scratch=[pltpu.VMEM((1, units), F32)], flops=BACK_FLOPS if at else 1024,
    )


def feed_back_kernel(
    at, height, count, low_own_ref, low_other_ref, xhat_one_ref, gain_one_ref, shift_one_ref, bdown_ref,
    gain_ref, shift_ref, cot_ref, slope_ref, win_ref, wdown_ref,
    *refs,
):
    before, refs = refs[:count], refs[count:]
    out_ref, d_two_ref, d_low_ref, d_inner_ref, vec_ref, bin_ref, dn_ref = refs
    normed = xhat_one_ref[...] * gain_one_ref[...].astype(F32)[None, :]
    normed = normed + shift_one_ref[...].astype(F32)[None, :]
    resid = (low_own_ref[...] + low_other_ref[...]) + bdown_ref[...].astype(F32)[None, :] + normed
    center = resid - jnp.mean(resid, axis=-1, keepdims=True)
    spread = jnp.mean(center * center, axis=-1, keepdims=True)
    rstd = lax.rsqrt(spread + EPSILON)
    xhat = center * rstd
    gain = gain_ref[...].astype(F32)[None, :]
    value = (xhat * gain + shift_ref[...].astype(F32)[None, :]).astype(BF16)
    if out_ref.shape[0] == height:
        out_ref[...] = value
    else:
        for stream, ref in enumerate(before):
            out_ref[stream * height : (stream + 1) * height] = ref[...]
        out_ref[at * height : (at + 1) * height] = value
    err = cot_ref[at * height : (at + 1) * height].astype(F32)
    vec_ref[0:1, :] = jnp.sum(err * xhat, axis=0, keepdims=True)
    vec_ref[1:2, :] = jnp.sum(err, axis=0, keepdims=True)
    scaled = err * gain
    mean_a = jnp.mean(scaled, axis=-1, keepdims=True)
    mean_b = jnp.mean(scaled * xhat, axis=-1, keepdims=True)
    d_two = rstd * (scaled - mean_a - xhat * mean_b)
    d_two_ref[...] = d_two
    vec_ref[2:3, :] = jnp.sum(d_two, axis=0, keepdims=True)
    low = d_two.astype(BF16)
    d_low_ref[...] = low
    units = win_ref.shape[1]
    step = units // 3
    dn_ref[...] = jnp.zeros_like(dn_ref)

    @pl.loop(0, 3)
    def _(part):
        cols = pl.ds(pl.multiple_of(part * step, step), step)
        d_act = dot_nt(low, wdown_ref[cols, :])
        d_inner = (d_act * slope_ref[:, cols]).astype(BF16)
        d_inner_ref[:, cols] = d_inner
        bin_ref[0:1, cols] = jnp.sum(d_inner.astype(F32), axis=0, keepdims=True)
        dn_ref[...] += dot_nt(d_inner, win_ref[:, cols])


def feed_back(
    line, at, height, rows, before, low_own, low_other, xhat, gain_one, shift_one, bdown, gain,
    shift, cot, slope, win, wdown,
):
    width = cot.shape[1]
    units = win.shape[1]
    last = (at + 1) * height == cot.shape[0]
    before = before if last else []
    outs = [
        sds(cot.shape if last else (height, width), BF16),
        sds((height, width), F32),
        sds((height, width), BF16),
        sds((height, units), BF16),
        sds((8, width), F32),
        sds((8, units), F32),
    ]
    outs += [sds((rows, width), F32)] * (height // rows)
    operands = (
        low_own, low_other, xhat, gain_one, shift_one, bdown, gain, shift, cot, slope, win, wdown,
        *before,
    )
    return line.call(
        functools.partial(feed_back_kernel, at, height, len(before)), f"feed_back_{at}", outs,
        operands, direct=(0,) if last else (),
    )


def spread(order, me, total, kept_ref, sent_refs, cols):
    parts = 1 << len(order)
    height = total.shape[0] // parts
    for bit in (0, order[0]):

        @pl.when((me & order[0]) == bit)
        def _(bit=bit):
            for block in range(parts):
                origin = me ^ block
                place = 0
                for later in order[1:]:
                    place = 2 * place + ((origin >> (later.bit_length() - 1)) & 1)
                top = block * height
                if block & order[0] == bit:
                    kept_ref[place, :, cols] = total[top : top + height]
                else:
                    for ref in sent_refs:
                        ref[place, :, cols] = total[top : top + ref.shape[1]]
                        top += ref.shape[1]


def grad_kernel(order, groups, pieces, *refs):
    kept_ref, *sent_refs = refs[-1 - pieces :]
    me = lax.axis_index("dp")
    at, start = 0, 0
    for count in groups:
        terms = []
        for rights in count:
            terms.append((refs[at], refs[at + 1 : at + 1 + rights]))
            at += 1 + rights
        width = terms[0][1][0].shape[1]

        def part(index, terms=terms, start=start):
            total = None
            columns = pl.ds(pl.multiple_of(index * COLUMNS, COLUMNS), COLUMNS)
            for left_ref, right_refs in terms:
                right = jnp.concatenate([ref[:, columns] for ref in right_refs], axis=0)
                term = dot_tn(left_ref[...], right.astype(BF16))
                total = term if total is None else total + term
            target = pl.ds(pl.multiple_of(start + index * COLUMNS, COLUMNS), COLUMNS)
            spread(order, me, total, kept_ref, sent_refs, target)

        pl.loop(0, width // COLUMNS)(part)
        start += width


def halves(order, rows, cols, pieces):
    half, height = (1 << len(order)) // 2, rows >> len(order)
    return [sds((half, height, cols), F32)] + [sds((half, height // pieces, cols), F32)] * pieces


def grad_blocks(line, name, order, groups, pieces=1):
    width = groups[0][0][0].shape[1]
    cols = sum(group[0][1][0].shape[1] for group in groups)
    operands = [array for group in groups for left, right in group for array in (left, *right)]
    counts = [[len(right) for _, right in group] for group in groups]
    outs = halves(order, width, cols, pieces)
    return line.call(
        functools.partial(grad_kernel, order, counts, pieces), name, outs, operands,
        flops=GRAD_FLOPS,
    )


def rel_kernel(
    order, counts, table_rows, bucket_ref, deq_ref, dek_ref, wq_ref, wk_ref, dk_ref, dv_ref,
    *refs,
):
    groups = []
    for count in counts:
        groups.append(refs[:count])
        refs = refs[count:]
    dq_refs, one_refs, two_refs, unit_refs = groups
    relq_ref, relk_ref, kept_ref, *sent_refs, pack_ref = refs
    onehot = onehot_of(bucket_ref, table_rows)
    deq, dek = deq_ref[...], dek_ref[...]
    cols = deq.shape[1]
    d_rel = dot_nn(onehot, jnp.concatenate([deq, dek], axis=1).astype(BF16)).astype(BF16)
    relq_ref[...] = d_rel[:, :cols]
    relk_ref[...] = d_rel[:, cols:]
    total = dot_nt(d_rel, jnp.concatenate([wq_ref[...], wk_ref[...]], axis=1))
    width = total.shape[1]
    me = lax.axis_index("dp")
    spread(order, me, total, kept_ref, sent_refs, slice(0, width))

    def summed(value):
        return jnp.sum(value.astype(F32), axis=0, keepdims=True)

    def over(stream_refs):
        value = stream_refs[0][...]
        for ref in stream_refs[1:]:
            value = value + ref[...]
        return value

    one, two, unit = over(one_refs), over(two_refs), over(unit_refs)
    d_bias = summed(dq_refs[0][...])
    for ref in dq_refs[1:]:
        d_bias = d_bias + summed(ref[...])
    vectors = [
        d_bias + summed(deq),
        summed(dk_ref[...]) + summed(dek),
        summed(dv_ref[...]),
        one[2:3], one[0:1], one[1:2], unit[0:1], two[2:3], two[0:1], two[1:2],
    ]
    pack_ref[...] = jnp.zeros_like(pack_ref)
    row = 0
    for vector in vectors:
        for piece in range(vector.shape[1] // LANES):
            pack_ref[row : row + 1, :] = vector[:, piece * LANES : (piece + 1) * LANES]
            row += 1
    spread(order, me, pack_ref[...], kept_ref, sent_refs, slice(width, width + LANES))


def rel_grads(line, order, span, buckets, deq, dek, wq, wk, dk, dv, dq, one, two, unit):
    width, cols = wq.shape
    outs = [sds((span, cols), BF16)] * 2
    outs = outs + halves(order, span, width + LANES, REL_PIECES)
    operands = [buckets, deq, dek, wq, wk, dk, dv, *dq, *one, *two, *unit]
    return line.call(
        functools.partial(rel_kernel, order, [len(g) for g in (dq, one, two, unit)], span), "rel_grads", outs, operands,
        scratch=[pltpu.VMEM((span, LANES), F32)],
    )


def rel_split_kernel(own_ref, other_ref, table_ref, vector_ref):
    width = table_ref.shape[2]
    for at in range(2):
        total = own_ref[at] + other_ref[1 - at]
        table_ref[at] = total[:, :width]
        vector_ref[at] = total[:, width:]


def rel_split(own, other):
    count, rows, wide = own.shape
    outs = [sds((count, rows, wide - LANES), F32), sds((count, rows, LANES), F32)]
    return rel_split_kernel, "rel_split", outs, [own, other], ()


def rel_join_kernel(own_ref, other_ref, vector_ref, out_ref):
    width = own_ref.shape[2]
    out_ref[:, :, :width] = own_ref[...] + other_ref[...]
    out_ref[:, :, width:] = vector_ref[...]


def rel_join(own, other, vector):
    count, rows, width = own.shape
    outs = [sds((count, rows, width + vector.shape[2]), F32)]
    return rel_join_kernel, "rel_join", outs, [own, other, vector], ()


def hidden_join_kernel(own_ref, other_ref, *refs):
    out_ref = refs[-1]
    start = 0
    for ref in refs[:-1]:
        rows = slice(start, start + ref.shape[0])
        out_ref[rows] = ((own_ref[rows] + other_ref[rows]) + ref[...]).astype(BF16)
        start += ref.shape[0]


def hidden_join(own, other, d_one):
    outs = [sds(own.shape, BF16)]
    return hidden_join_kernel, "hidden_join", outs, [own, other, *d_one], (0,)


def unpack_kernel(origins, count, *refs):
    shared_refs, (table_ref, *vector_refs) = refs[:count], refs[count:]
    width = table_ref.shape[2]
    height = table_ref.shape[1]
    me = lax.axis_index("dp")
    places = [(ref, at) for ref in shared_refs for at in range(ref.shape[0])]
    rows = sum(ref.shape[0] for ref in vector_refs) // LANES
    lines = [
        (ref, piece) for ref in vector_refs for piece in range(ref.shape[0] // LANES)
    ]
    for (shared_ref, at), origin in zip(places, origins, strict=True):
        table_ref[me ^ origin] = shared_ref[at, :, :width]
        for block in range((rows + height - 1) // height):

            @pl.when(me ^ origin == block)
            def _(shared_ref=shared_ref, at=at, block=block):
                for row in range(block * height, min(rows, (block + 1) * height)):
                    ref, piece = lines[row]
                    inner = row % height
                    line = shared_ref[at, inner : inner + 1, width:]
                    ref[pl.ds(piece * LANES, LANES)] = line.reshape(LANES)


def unpack(origins, pieces, sizes):
    height, wide = pieces[0].shape[1:]
    outs = [sds((len(origins), height, wide - LANES), F32)] + [sds((size,), F32) for size in sizes]
    kernel = functools.partial(unpack_kernel, origins, len(pieces))
    return kernel, "unpack", outs, list(pieces), range(len(outs))


def hidden_kernel(dk_ref, dv_ref, wq_ref, wk_ref, wv_ref, *refs):
    out_ref = refs[-1]
    out_ref[...] = dot_nt(dk_ref[...], wk_ref[...]) + dot_nt(dv_ref[...], wv_ref[...])
    start = 0
    for ref in refs[:-1]:
        out_ref[start : start + ref.shape[0]] += dot_nt(ref[...], wq_ref[...])
        start += ref.shape[0]


def hidden_grad(line, dk, dv, wq, wk, wv, dq):
    out = sds((dk.shape[0], wq.shape[0]), F32)
    (total,) = line.call(
        hidden_kernel, "hidden_grad", [out], (dk, dv, wq, wk, wv, *dq)
    )
    return total


def bits_of(parts):
    return [1 << b for b in range(parts.bit_length() - 1)]


def swap_head(value):
    return lax.ppermute(value, "head", [(0, 1), (1, 0)])


def flip(value, parts, bit):
    return lax.ppermute(value, "dp", [(i, i ^ bit) for i in range(parts)])


def together(*values):
    return lax.optimization_barrier(values)


def step_kernel(kept_ref, *refs):
    *arrived_refs, kept_out, sent_out = refs
    half = kept_out.shape[0]
    top = 0
    for ref in arrived_refs:
        rows = slice(top, top + ref.shape[1])
        kept_out[:, rows] = kept_ref[:half, rows] + ref[:half]
        sent_out[:, rows] = kept_ref[half:, rows] + ref[half:]
        top += ref.shape[1]


class Scatter:
    def __init__(self, line, name, kept, *sent, order):
        self.line, self.name, self.order = line, name, list(order)
        self.parts = 1 << len(self.order)
        self.kept = kept
        self.send(sent)

    def send(self, sent):
        self.bit = self.order.pop(0)
        self.arrived = [flip(piece, self.parts, self.bit) for piece in sent]

    def step(self):
        shape = (self.kept.shape[0] // 2, *self.kept.shape[1:])
        self.kept, sent = yield (
            step_kernel, f"{self.name}_{self.bit}", [sds(shape, F32)] * 2,
            [self.kept, *self.arrived], (),
        )
        self.send([sent])

    def rest(self, left=0):
        while len(self.order) > left:
            self.line.group([self.step()])

    def exchange(self):
        def add(kept_ref, arrived_ref, out_ref):
            out_ref[...] = kept_ref[...] + arrived_ref[...]

        self.rest(1)
        outs = [sds(self.kept.shape, F32)]
        (self.both,) = yield add, f"{self.name}_{self.bit}", outs, [self.kept, *self.arrived], ()
        bit = self.order.pop(0)
        self.both_other, self.origins = flip(self.both, self.parts, bit), [0, bit]

    def finish(self, widths):
        def kernel(kept_ref, arrived_ref, *out_refs):
            start = 0
            for ref in out_refs:
                cols = slice(start, start + ref.shape[1])
                ref[...] = kept_ref[0, :, cols] + arrived_ref[0, :, cols]
                start += ref.shape[1]

        self.rest()
        outs = [sds((self.kept.shape[1], width), F32) for width in widths]
        operands = [self.kept, *self.arrived]
        self.sums = yield kernel, f"{self.name}_sum", outs, operands, range(len(outs))


def pack_kernel(*refs):
    start = 0
    for ref in refs[:-1]:
        refs[-1][start : start + ref.shape[0]] = ref[...]
        start += ref.shape[0]


class Gather:
    def __init__(self, line, value, origins, parts, order):
        self.line, self.parts, self.order = line, parts, list(order)
        self.pieces, self.origins = [value], origins
        self.send(value)

    def send(self, sent):
        bit = self.order.pop(0)
        self.pieces.append(flip(sent, self.parts, bit))
        self.origins = self.origins + [origin ^ bit for origin in self.origins]

    def step(self):
        shape = (len(self.origins), *self.pieces[0].shape[1:])
        name = f"pack_{len(self.origins)}"
        (sent,) = yield pack_kernel, name, [sds(shape, F32)], list(self.pieces), ()
        self.send(sent)

    def rest(self):
        while self.order:
            self.line.group([self.step()])


def words_of(text):
    words, open_word = [], None
    for letter in text:
        if letter == "(":
            open_word = ""
        elif letter == ")":
            words.append(open_word)
            open_word = None
        elif open_word is not None:
            open_word += letter
        else:
            words.append(letter)
    return words


def on_device(parts, *arguments):
    (
        hidden_in, lengths, cotangent, w_query, b_query, w_key, b_key, w_value, b_value,
        w_out, b_out, ln1_gain, ln1_bias, w_in, b_in, w_down, b_down, ln2_gain, ln2_bias,
        rel_table,
    ) = arguments
    seq_len, width = hidden_in.shape
    height = seq_len // STREAMS
    streams = range(STREAMS)
    bits = bits_of(parts)

    buckets = jnp.asarray(distance_buckets(seq_len)[None, :])
    line = Line()
    q, k, v, eq, ek, mine = project(
        line, buckets, hidden_in, w_query, b_query, w_key, b_key, w_value, b_value, rel_table,
        w_out,
    )
    fetched = swap_head(mine)
    contexts, attends = [], []
    for at in range(CONTEXTS * STREAMS):
        context, attended = attend(line, at, height // CONTEXTS, lengths, q, k, v, eq, ek)
        contexts.append(context)
        attends.append(attended)
    fetched, contexts[0] = together(fetched, contexts[0])
    quarters = [fetched, flip(fetched, parts, 1), flip(fetched, parts, 2)]
    quarters.append(flip(quarters[2], parts, 1))
    w_out_all = assemble(line, w_out, quarters)
    others = [swap_head(context) for context in contexts]
    of_stream = [slice(CONTEXTS * at, CONTEXTS * (at + 1)) for at in streams]
    fed = [
        feed(
            line, at, height, contexts[of_stream[at]], others[of_stream[at]],
            w_out_all, b_out, hidden_in, ln1_gain, ln1_bias, w_in, b_in, w_down,
        )
        for at in streams
    ]
    backs = []
    for at in streams:
        xhat, rstd, normed, act, slope, lowered = fed[at]
        backs.append(
            feed_back(
                line, at, height, height, [b[0] for b in backs], lowered, swap_head(lowered), xhat,
                ln1_gain, ln1_bias, b_down, ln2_gain, ln2_bias, cotangent, slope, w_in, w_down,
            )
        )
    output = backs[-1][0]
    crossed = bits[:1] + bits[2:] + bits[1:2]
    g_down = grad_blocks(
        line, "grad_down", bits, [[(backs[at][2], fed[at][3:4]) for at in streams]]
    )
    down = Scatter(line, "down", *g_down, order=bits)
    g_in = grad_blocks(
        line, "grad_in", crossed, [[(fed[at][2], backs[at][3:4]) for at in streams]]
    )
    inner = Scatter(line, "inner", *g_in, order=crossed)
    norms, dq = [], []
    carried = ()
    for at in streams:
        xhat, rstd = fed[at][:2]
        d_two, dn = backs[at][1], backs[at][6]
        norms.append(
            norm_back(line, at, 0, dn, swap_head(dn), d_two, xhat, rstd, ln1_gain, w_out)
        )
        if at == 0:
            line.group([down.step()])
            line.group([inner.step()])
        d_q, *carried = attend_back(
            line, at, height, at == streams[-1], norms[at][2], q, k, v, eq, ek,
            attends[of_stream[at]], carried,
        )
        dq.append(d_q)
    deq, dek, dk, dv = carried[2:]
    cols = q.shape[1]
    hidden_parts = [hidden_in[at * height : (at + 1) * height] for at in streams]
    chains = {"d": down, "i": inner}
    made = {}

    def start_rel():
        made["relq"], made["relk"], *blocks = rel_grads(
            line, bits, rel_table.shape[0], buckets, deq, dek, w_query, w_key, dk, dv, dq,
            [n[3] for n in norms], [b[4] for b in backs], [b[5] for b in backs],
        )
        chains["r"] = Scatter(line, "rel", *blocks, order=bits)

    def start_value_out():
        blocks = grad_blocks(
            line, "grad_value_out", bits,
            [
                [(hidden_in, [dv])],
                [(norms[at][1], contexts[of_stream[at]]) for at in streams],
            ],
            HEAD_PIECES,
        )
        chains["v"] = Scatter(line, "value_out", *blocks, order=bits)

    def start_query_key():
        blocks = grad_blocks(
            line, "grad_query_key", bits,
            [
                [*zip(hidden_parts, [[d] for d in dq], strict=True), (rel_table, [made["relq"]])],
                [(hidden_in, [dk]), (rel_table, [made["relk"]])],
            ],
            HEAD_PIECES,
        )
        chains["q"] = Scatter(line, "query_key", *blocks, order=bits)

    def start_hidden():
        made["hidden"] = hidden_grad(line, dk, dv, w_query, w_key, w_value, dq)
        made["hidden_other"] = swap_head(made["hidden"])

    def swap_rel():
        both, other = chains["r"].both, chains["r"].both_other
        made["own"], made["vectors"] = yield rel_split(both, other)
        made["own_other"] = swap_head(made["own"])

    def gather_rel():
        (joined,) = yield rel_join(made["own"], made["own_other"], made["vectors"])
        chains["p"] = Gather(line, joined, chains["r"].origins, parts, bits[-2::-1])

    def end_hidden():
        d_one = [n[0] for n in norms]
        made["grad_input"] = yield hidden_join(made["hidden"], made["hidden_other"], d_one)

    def end_rel():
        chains["p"].rest()
        sizes = [cols] * 3 + [width] * 3 + [w_in.shape[1]] + [width] * 3
        made["shared"] = yield unpack(chains["p"].origins, chains["p"].pieces, sizes)

    starters = {
        "L": start_rel, "G": start_value_out, "K": start_query_key, "Y": start_hidden,
    }
    steps = {
        "X": lambda: chains["r"].exchange(), "S": swap_rel, "J": gather_rel, "H": end_hidden,
        "U": end_rel,
    }
    widths = {"d": [w_in.shape[1]], "i": [w_in.shape[1]], "v": [cols, cols], "q": [cols, cols]}

    def work(letter):
        if letter in widths:
            return chains[letter].finish(widths[letter])
        return steps[letter]() if letter in steps else chains[letter.lower()].step()

    for word in words_of(TAIL):
        if word in starters:
            starters[word]()
        else:
            line.group([work(letter) for letter in word])
    (s_down,), (s_in,) = chains["d"].sums, chains["i"].sums
    (s_q, s_k), (s_v, s_out) = chains["q"].sums, chains["v"].sums
    (grad_input,) = made["grad_input"]
    table_blocks, *pieces = made["shared"]
    grad_rel_table = table_blocks.reshape(rel_table.shape)
    (
        grad_b_query, grad_b_key, grad_b_value, grad_b_out, grad_ln1_gain, grad_ln1_bias,
        grad_b_in, grad_b_down, grad_ln2_gain, grad_ln2_bias,
    ) = pieces
    return (
        output, grad_input, s_q, grad_b_query, s_k, grad_b_key, s_v, grad_b_value,
        s_out.T, grad_b_out, grad_ln1_gain, grad_ln1_bias, s_in, grad_b_in,
        s_down.T, grad_b_down, grad_ln2_gain, grad_ln2_bias, grad_rel_table,
    )


def solution(mesh):
    parts = mesh.shape["dp"]
    return jax.shard_map(
        functools.partial(on_device, parts),
        mesh=mesh,
        in_specs=(
            P("dp", None), P("dp"), P("dp", None),
            P(None, "head"), P("head"), P(None, "head"), P("head"), P(None, "head"), P("head"),
            P("head", None), P(), P(), P(),
            P(None, "head"), P("head"), P("head", None), P(), P(), P(), P(),
        ),
        out_specs=(
            P("dp", None), P("dp", None),
            P("dp", "head"), P("head"), P("dp", "head"), P("head"), P("dp", "head"), P("head"),
            P("head", "dp"), P(), P(), P(),
            P("dp", "head"), P("head"), P("head", "dp"), P(), P(), P(), P(),
        ),
        check_vma=False,
    )
```

```python
import functools
import itertools
import math

import jax
import jax.numpy as jnp
import numpy as np
from jax import lax
from jax.experimental import pallas as pl
from jax.experimental.pallas import tpu as pltpu
from jax.sharding import PartitionSpec as P

HEAD_DIM = 64
SPAN = 256
MAXPOS = 512
EPSILON = 1e-07
MASKED = -1000000000.0
LANES = 128
STREAMS = 2
CONTEXTS = 1
TAIL = "LYKGDIR(VQ)RDVXI(SQ)JiQqP(VH)dP(vU)"
REL_PIECES = 2
HEAD_PIECES = 1
QUARTERS = 4
COLUMNS = 384
BACK_FLOPS = 64 << 30
STEP_FLOPS = 1024
GRAD_FLOPS = 1024
VMEM_LIMIT = 8 * 1024 * 1024

BF16 = jnp.bfloat16
F32 = jnp.float32


def bucket_of(offsets, bucket_span, max_distance):
    middle = bucket_span // 2
    direction = np.sign(offsets)
    absolute = np.where((offsets < middle) & (offsets > -middle), middle - 1, np.abs(offsets))
    log_part = (
        np.ceil(np.log(absolute / middle) / np.log((max_distance - 1) / middle) * (middle - 1))
        + middle
    )
    bucket = np.where(absolute <= middle, offsets, log_part * direction).astype(np.int64)
    return np.clip(bucket + bucket_span, 0, 2 * bucket_span - 1).astype(np.int32)


def distance_buckets(seq_len):
    offsets = np.maximum(seq_len - 1 - np.arange(2 * seq_len), 1 - seq_len)
    return bucket_of(offsets, SPAN, MAXPOS)


def dot_nn(a, b):
    return lax.dot_general(a, b, (((1,), (0,)), ((), ())), preferred_element_type=F32)


def dot_nt(a, b):
    return lax.dot_general(a, b, (((1,), (1,)), ((), ())), preferred_element_type=F32)


def dot_tn(a, b):
    return lax.dot_general(a, b, (((0,), (0,)), ((), ())), preferred_element_type=F32)


def resume(work, results):
    try:
        yield work.send(results)
    except StopIteration:
        return


class Line:
    def __init__(self):
        self.last = ()

    def call(
        self, kernel, name, outs, operands, aliases=None, scalars=0, scratch=(), flops=1024,
        space=pltpu.VMEM, direct=(),
    ):
        in_specs = [pl.BlockSpec(memory_space=pltpu.SMEM)] * scalars
        in_specs += [pl.BlockSpec(memory_space=space)] * (len(operands) - scalars)
        in_specs += [pl.BlockSpec(memory_space=pl.ANY)] * len(self.last)
        count, skipped = len(operands), len(self.last)

        def body(*refs):
            kernel(*refs[:count], *refs[count + skipped :])

        results = pl.pallas_call(
            body,
            in_specs=in_specs,
            out_specs=[
                pl.BlockSpec() if at in direct else pl.BlockSpec(memory_space=pltpu.VMEM)
                for at in range(len(outs))
            ],
            out_shape=outs,
            scratch_shapes=list(scratch),
            input_output_aliases=aliases or {},
            compiler_params=pltpu.CompilerParams(vmem_limit_bytes=VMEM_LIMIT),
            cost_estimate=pl.CostEstimate(flops=flops, bytes_accessed=1024, transcendentals=0),
            name=name,
        )(*operands, *self.last)
        self.last = (min(results, key=lambda result: result.size * result.dtype.itemsize),)
        return results


    def group(self, works):
        calls = [next(work) for work in works]
        ins = [len(call[3]) for call in calls]
        sizes = [len(call[2]) for call in calls]

        def kernel(*refs):
            in_refs, out_refs = refs[: sum(ins)], refs[sum(ins) :]
            for call, count, size in zip(calls, ins, sizes, strict=True):
                call[0](*in_refs[:count], *out_refs[:size])
                in_refs, out_refs = in_refs[count:], out_refs[size:]

        outs, operands, direct = [], [], []
        for _, _, call_outs, call_operands, call_direct in calls:
            direct += [len(outs) + at for at in call_direct]
            outs += call_outs
            operands += call_operands
        name = "__".join(call[1] for call in calls)
        results = self.call(kernel, name, outs, operands, direct=direct, flops=STEP_FLOPS)
        for work, size in zip(works, sizes, strict=True):
            part, results = results[:size], results[size:]
            for _ in itertools.islice(resume(work, part), 1):
                raise ValueError("second call")


def sds(shape, dtype):
    return jax.ShapeDtypeStruct(shape, dtype)


def onehot_of(bucket_ref, span):
    buckets = bucket_ref[...]
    hot = buckets == lax.broadcasted_iota(jnp.int32, (span, buckets.shape[1]), 0)
    return jnp.where(hot, 1.0, 0.0).astype(BF16)


def project_kernel(
    bucket_hbm, hidden_hbm, wq_hbm, bq_hbm, wk_hbm, bk_hbm, wv_hbm, bv_hbm, table_hbm, wout_hbm,
    q_ref, k_ref, v_ref, eq_ref, ek_ref, mine_ref,
    bucket_ref, hidden_ref, weight_ref, bq_ref, bk_ref, bv_ref, table_ref, quarter_ref, sems,
):
    rows = quarter_ref.shape[0]
    first = pl.multiple_of(lax.rem(lax.axis_index("dp"), QUARTERS) * rows, rows)
    cols = q_ref.shape[1]
    weights = [weight_ref.at[:, at * cols : (at + 1) * cols] for at in range(3)]
    sources = (
        wout_hbm.at[pl.ds(first, rows)], hidden_hbm, wq_hbm, wk_hbm, wv_hbm, bq_hbm, bk_hbm, bv_hbm,
        table_hbm, bucket_hbm,
    )
    targets = (
        quarter_ref, hidden_ref, *weights, bq_ref, bk_ref, bv_ref, table_ref, bucket_ref,
    )
    copies = [
        pltpu.make_async_copy(source, target, sems.at[at])
        for at, (source, target) in enumerate(zip(sources, targets, strict=True))
    ]
    for copy in copies:
        copy.start()
    copies[0].wait()
    mine_ref[...] = quarter_ref[...].astype(F32)
    for copy in copies[1:8]:
        copy.wait()
    bias = jnp.concatenate([ref[...].astype(F32)[None, :] for ref in (bq_ref, bk_ref, bv_ref)], axis=1)
    rows = (dot_nn(hidden_ref[...], weight_ref[...]) + bias).astype(BF16)
    for at, ref in enumerate((q_ref, k_ref, v_ref)):
        ref[...] = rows[:, at * cols : (at + 1) * cols]
    for copy in copies[8:]:
        copy.wait()
    table = table_ref[...]
    onehot = onehot_of(bucket_ref, table.shape[0])
    both = (dot_nn(table, weight_ref[:, : 2 * cols]) + bias[:, : 2 * cols]).astype(BF16)
    spread_out = dot_tn(onehot, both).astype(BF16)
    eq_ref[...] = spread_out[:, :cols]
    ek_ref[...] = spread_out[:, cols:]


def project(line, buckets, hidden, wq, bq, wk, bk, wv, bv, table, wout):
    seq_len = hidden.shape[0]
    cols = wq.shape[1]
    rows = wout.shape[0] // QUARTERS
    outs = [sds((seq_len, cols), BF16)] * 3 + [sds((2 * seq_len, cols), BF16)] * 2
    outs += [sds((rows, wout.shape[1]), F32)]
    operands = (buckets, hidden, wq, bq, wk, bk, wv, bv, table, wout)
    shapes = [buckets, hidden, sds((wq.shape[0], 3 * cols), wq.dtype), bq, bk, bv, table]
    scratch = [pltpu.VMEM(array.shape, array.dtype) for array in shapes]
    scratch += [pltpu.VMEM((rows, wout.shape[1]), wout.dtype)]
    operands = [pltpu.with_memory_space_constraint(operand, pltpu.HBM) for operand in operands]
    scratch += [pltpu.SemaphoreType.DMA((len(operands),))]
    return line.call(
        project_kernel, "project", outs, operands, scratch=scratch, space=pltpu.HBM
    )


def assemble_kernel(own_ref, *refs):
    out_ref = refs[-1]
    side, me = lax.axis_index("head"), lax.rem(lax.axis_index("dp"), QUARTERS)
    out_ref[side] = own_ref[...]
    for origin, ref in enumerate(refs[:-1]):
        rows = ref.shape[0]
        first = pl.multiple_of((me ^ origin) * rows, rows)
        out_ref[1 - side, pl.ds(first, rows), :] = ref[...].astype(BF16)


def assemble(line, own, quarters):
    rows, width = own.shape
    out = sds((2, rows, width), BF16)
    (joined,) = line.call(assemble_kernel, "assemble", [out], (own, *quarters))
    return joined.reshape(2 * rows, width)


def half_masks():
    lane = lax.broadcasted_iota(jnp.int32, (1, LANES), 1)
    return [lane // HEAD_DIM == side for side in range(LANES // HEAD_DIM)]


def apart(masks, value):
    zero = jnp.zeros_like(value)
    return jnp.concatenate([jnp.where(mask, value, zero) for mask in masks], axis=0)


def join(masks, stacked):
    rows = stacked.shape[0] // 2
    return jnp.where(masks[0], stacked[:rows], stacked[rows:])


def skewed(stacked, shift):
    rows = stacked.shape[0] // 2
    parts = [
        pltpu.roll(part, shift, 1, stride=1, stride_axis=0)
        for part in (stacked[:rows], stacked[rows:])
    ]
    return jnp.concatenate(parts, axis=0)


def attend_kernel(at, height, len_ref, q_ref, k_ref, v_ref, eq_ref, ek_ref, ctx_ref, att_ref):
    seq_len = k_ref.shape[0]
    length = len_ref[0]
    scale = 1.0 / math.sqrt(3 * HEAD_DIM)
    masks = half_masks()
    key_valid = lax.broadcasted_iota(jnp.int32, (1, seq_len), 1) < length
    rows = at * height + lax.broadcasted_iota(jnp.int32, (height, 1), 0)
    rows = jnp.concatenate([rows, rows], axis=0)
    query_valid = rows < length
    row_start = seq_len - height - height * at
    @pl.loop(0, q_ref.shape[1] // LANES)
    def _(pair):
        cols = pl.ds(pl.multiple_of(pair * LANES, LANES), LANES)
        q_pair = q_ref[at * height : (at + 1) * height, cols]
        k_pair = k_ref[:, cols]
        v_pair = v_ref[:, cols]
        rel_window = ek_ref[row_start : row_start + seq_len + height, cols]
        q_two = apart(masks, q_pair)
        content = dot_nt(q_two, k_pair)
        picked = skewed(dot_nt(q_two, rel_window), seq_len + 1)[:, :seq_len]
        blocks = []
        for block in range(seq_len // LANES):
            start = seq_len - LANES - LANES * block + height * at
            window = eq_ref[start : start + LANES + height, cols]
            k_two = apart(masks, k_pair[block * LANES : (block + 1) * LANES])
            tall = skewed(dot_nt(k_two, window), height + 1)[:, :height]
            blocks.append(jnp.concatenate([tall[:LANES].T, tall[LANES:].T], axis=0))
        flipped = jnp.concatenate(blocks, axis=1)
        scores = jnp.where(key_valid, scale * (content + picked + flipped), MASKED)
        peak = jnp.max(scores, axis=-1, keepdims=True)
        weight = jnp.exp(scores - peak)
        total = jnp.sum(weight, axis=-1, keepdims=True)
        keep = jnp.where(query_valid, 1.0 / total, 0.0)
        attend = (weight * keep).astype(BF16)
        att_ref[2 * pair] = attend[:height]
        att_ref[2 * pair + 1] = attend[height:]
        ctx_ref[:, cols] = join(masks, dot_nn(attend, v_pair)).astype(BF16).astype(F32)


def attend(line, at, height, lengths, q, k, v, eq, ek):
    seq_len, cols = q.shape
    heads = cols // HEAD_DIM
    outs = [sds((height, cols), F32), sds((heads, height, seq_len), BF16)]
    return line.call(
        functools.partial(attend_kernel, at, height), f"attend_{at}", outs,
        (lengths, q, k, v, eq, ek), scalars=1,
    )


def norm_back_kernel(
    start, dn_own_ref, dn_other_ref, d_two_ref, xhat_ref, rstd_ref, gain_ref, wout_ref,
    d_one_ref, d_mixed_ref, d_ctx_ref, vec_ref,
):
    rows = slice(start, start + dn_own_ref.shape[0])
    d_normed = (dn_own_ref[...] + dn_other_ref[...]) + d_two_ref[rows]
    xhat = xhat_ref[rows]
    vec_ref[0:1, :] = jnp.sum(d_normed * xhat, axis=0, keepdims=True)
    vec_ref[1:2, :] = jnp.sum(d_normed, axis=0, keepdims=True)
    scaled = d_normed * gain_ref[...].astype(F32)[None, :]
    mean_a = jnp.mean(scaled, axis=-1, keepdims=True)
    mean_b = jnp.mean(scaled * xhat, axis=-1, keepdims=True)
    d_one = rstd_ref[rows] * (scaled - mean_a - xhat * mean_b)
    d_one_ref[...] = d_one
    vec_ref[2:3, :] = jnp.sum(d_one, axis=0, keepdims=True)
    d_mixed = d_one.astype(BF16)
    d_mixed_ref[...] = d_mixed
    d_ctx_ref[...] = dot_nt(d_mixed, wout_ref[...]).astype(BF16)


def norm_back(line, at, start, dn_own, dn_other, d_two, xhat, rstd, gain, wout):
    height, width = dn_own.shape
    outs = [
        sds((height, width), F32),
        sds((height, width), BF16),
        sds((height, wout.shape[0]), BF16),
        sds((8, width), F32),
    ]
    operands = (dn_own, dn_other, d_two, xhat, rstd, gain, wout)
    return line.call(
        functools.partial(norm_back_kernel, start), f"norm_back_{at}", outs, operands,
        flops=BACK_FLOPS,
    )


def attend_back_kernel(
    at, height, count, first, last, d_ctx_ref, q_ref, k_ref, v_ref, eq_ref, ek_ref, *refs
):
    att_refs, refs = refs[:count], refs[count:]
    if not first:
        refs = refs[4:]
    dq_ref, dk_ref, dv_ref, deq_ref, dek_ref = refs[:5]
    seq_len = k_ref.shape[0]
    scale = 1.0 / math.sqrt(3 * HEAD_DIM)
    masks = half_masks()

    def anti(size):
        row = lax.broadcasted_iota(jnp.int32, (size, size), 0)
        col = lax.broadcasted_iota(jnp.int32, (size, size), 1)
        return jnp.where(row + col == size - 1, 1.0, 0.0).astype(BF16)

    anti_rows = anti(height)
    anti_keys = anti(LANES)
    row_start = seq_len - height - height * at
    if first:
        dk_ref[...] = jnp.zeros_like(dk_ref)
        dv_ref[...] = jnp.zeros_like(dv_ref)
        deq_ref[...] = jnp.zeros_like(deq_ref)
        dek_ref[...] = jnp.zeros_like(dek_ref)

    @pl.loop(0, q_ref.shape[1] // LANES)
    def _(pair):
        cols = pl.ds(pl.multiple_of(pair * LANES, LANES), LANES)
        q_pair = q_ref[at * height : (at + 1) * height, cols]
        k_pair = k_ref[:, cols]
        v_pair = v_ref[:, cols]
        ctx_pair = d_ctx_ref[:, cols]
        rel_window = ek_ref[row_start : row_start + seq_len + height, cols]
        q_turned = dot_nn(anti_rows, q_pair).astype(BF16)
        weight = jnp.concatenate(
            [jnp.concatenate([ref[2 * pair + side] for ref in att_refs], axis=0) for side in range(2)],
            axis=0,
        )
        d_att = dot_nt(apart(masks, ctx_pair), v_pair)
        soft = weight.astype(F32)
        inner = jnp.sum(d_att * soft, axis=-1, keepdims=True)
        d_scores = (soft * (d_att - inner)).astype(BF16)
        sides = [d_scores[:height], d_scores[height:]]
        weight_wide = jnp.concatenate([weight[:height], weight[height:]], axis=1)
        dv_ref[:, cols] += join(masks, dot_tn(weight_wide, ctx_pair))
        d_q = join(masks, dot_nn(d_scores, k_pair))
        d_scores_t = [side.T for side in sides]
        d_k = join(masks, dot_nn(jnp.concatenate(d_scores_t, axis=0), q_pair))
        turned = dot_nn(anti_rows, jnp.concatenate(sides, axis=1))
        space = jnp.zeros((height, height), F32)
        turned = [
            jnp.concatenate([turned[:, side * seq_len : (side + 1) * seq_len], space], axis=1)
            for side in range(2)
        ]
        turned = skewed(jnp.concatenate(turned, axis=0), 0).astype(BF16)
        d_q_turned = join(masks, dot_nn(turned, rel_window))
        turned_wide = jnp.concatenate([turned[:height], turned[height:]], axis=1)
        d_rel_k = join(masks, dot_tn(turned_wide, q_turned))
        dek_ref[row_start : row_start + seq_len + height, cols] += scale * d_rel_k

        def turn_back(matrix, value):
            high = value.astype(BF16)
            rest = (value - high.astype(F32)).astype(BF16)
            both = dot_nn(matrix, jnp.concatenate([high, rest], axis=1))
            return both[:, :LANES] + both[:, LANES:]

        dq_ref[:, cols] = (scale * (d_q + turn_back(anti_rows, d_q_turned))).astype(BF16)
        backs = []
        for block in range(seq_len // LANES):
            start = seq_len - LANES - LANES * block + height * at
            rows = slice(block * LANES, (block + 1) * LANES)
            window = eq_ref[start : start + LANES + height, cols]
            tall = dot_nn(anti_keys, jnp.concatenate([side[rows] for side in d_scores_t], axis=1))
            space = jnp.zeros((LANES, LANES), F32)
            tall = [
                jnp.concatenate([tall[:, side * height : (side + 1) * height], space], axis=1)
                for side in range(2)
            ]
            tall = skewed(jnp.concatenate(tall, axis=0), 0).astype(BF16)
            backs.append(join(masks, dot_nn(tall, window)))
            k_turned = apart(masks, dot_nn(anti_keys, k_pair[rows]).astype(BF16))
            deq_ref[start : start + LANES + height, cols] += scale * dot_tn(tall, k_turned)
        for block, value in enumerate(backs):
            rows = slice(block * LANES, (block + 1) * LANES)
            dk_ref[rows, cols] += scale * (d_k[rows] + turn_back(anti_keys, value))
    if last:
        dk_low_ref, dv_low_ref = refs[5:]
        dk_low_ref[...] = dk_ref[...].astype(BF16)
        dv_low_ref[...] = dv_ref[...].astype(BF16)


def attend_back(line, at, height, last, d_ctx, q, k, v, eq, ek, att, carried):
    seq_len, cols = q.shape
    operands = [d_ctx, q, k, v, eq, ek, *att, *carried]
    outs = [
        sds((height, cols), BF16),
        sds((seq_len, cols), F32),
        sds((seq_len, cols), F32),
        sds((2 * seq_len, cols), F32),
        sds((2 * seq_len, cols), F32),
    ]
    if last:
        outs += [sds((seq_len, cols), BF16)] * 2
    base = 6 + len(att)
    return line.call(
        functools.partial(attend_back_kernel, at, height, len(att), not carried, last),
        f"attend_back_{at}", outs, operands,
        aliases={base + place: 1 + place for place in range(4)} if carried else {},
        flops=BACK_FLOPS,
    )


def feed_kernel(
    at, height, count, wout_ref, bout_ref, hidden_ref, gain_ref, shift_ref, win_ref, bin_ref,
    wdown_ref, *refs,
):
    own_refs, other_refs = refs[:count], refs[count : 2 * count]
    xhat_ref, rstd_ref, normed_ref, act_ref, slope_ref, low_ref, bias_ref = refs[2 * count :]
    own = jnp.concatenate([ref[...] for ref in own_refs], axis=0)
    other = jnp.concatenate([ref[...] for ref in other_refs], axis=0)
    first = lax.axis_index("head") == 0
    ctx = jnp.concatenate([jnp.where(first, own, other), jnp.where(first, other, own)], axis=1)
    ctx = ctx.astype(BF16)
    mixed = dot_nn(ctx, wout_ref[...])
    hidden = hidden_ref[at * height : (at + 1) * height].astype(F32)
    resid = mixed + bout_ref[...].astype(F32)[None, :] + hidden
    center = resid - jnp.mean(resid, axis=-1, keepdims=True)
    spread = jnp.mean(center * center, axis=-1, keepdims=True)
    rstd = lax.rsqrt(spread + EPSILON)
    xhat = center * rstd
    xhat_ref[...] = xhat
    rstd_ref[...] = rstd
    normed = xhat * gain_ref[...].astype(F32)[None, :] + shift_ref[...].astype(F32)[None, :]
    low = normed.astype(BF16)
    normed_ref[...] = low
    units = win_ref.shape[1]
    step = units // 3
    bias_ref[...] = bin_ref[...].astype(F32)[None, :]
    low_ref[...] = jnp.zeros_like(low_ref)

    @pl.loop(0, 3)
    def _(part):
        cols = pl.ds(pl.multiple_of(part * step, step), step)
        inner = dot_nn(low, win_ref[:, cols]) + bias_ref[:, cols]
        phi = 0.5 * (1.0 + lax.erf(inner * math.sqrt(0.5)))
        act = (inner * phi).astype(BF16)
        slope = phi + inner * (jnp.exp(-0.5 * inner * inner) * (1.0 / math.sqrt(2 * math.pi)))
        act_ref[:, cols] = act
        slope_ref[:, cols] = slope
        low_ref[...] += dot_nn(act, wdown_ref[cols, :])


def feed(line, at, height, own, other, wout, bout, hidden, gain, shift, win, b_in, wdown):
    width = hidden.shape[1]
    units = win.shape[1]
    outs = [
        sds((height, width), F32),
        sds((height, 1), F32),
        sds((height, width), BF16),
        sds((height, units), BF16),
        sds((height, units), F32),
        sds((height, width), F32),
    ]
    operands = (wout, bout, hidden, gain, shift, win, b_in, wdown, *own, *other)
    return line.call(
        functools.partial(feed_kernel, at, height, len(own)), f"feed_{at}", outs, operands,
        scratch=[pltpu.VMEM((1, units), F32)], flops=BACK_FLOPS if at else 1024,
    )


def feed_back_kernel(
    at, height, count, low_own_ref, low_other_ref, xhat_one_ref, gain_one_ref, shift_one_ref, bdown_ref,
    gain_ref, shift_ref, cot_ref, slope_ref, win_ref, wdown_ref,
    *refs,
):
    before, refs = refs[:count], refs[count:]
    out_ref, d_two_ref, d_low_ref, d_inner_ref, vec_ref, bin_ref, dn_ref = refs
    normed = xhat_one_ref[...] * gain_one_ref[...].astype(F32)[None, :]
    normed = normed + shift_one_ref[...].astype(F32)[None, :]
    resid = (low_own_ref[...] + low_other_ref[...]) + bdown_ref[...].astype(F32)[None, :] + normed
    center = resid - jnp.mean(resid, axis=-1, keepdims=True)
    spread = jnp.mean(center * center, axis=-1, keepdims=True)
    rstd = lax.rsqrt(spread + EPSILON)
    xhat = center * rstd
    gain = gain_ref[...].astype(F32)[None, :]
    value = (xhat * gain + shift_ref[...].astype(F32)[None, :]).astype(BF16)
    if out_ref.shape[0] == height:
        out_ref[...] = value
    else:
        for stream, ref in enumerate(before):
            out_ref[stream * height : (stream + 1) * height] = ref[...]
        out_ref[at * height : (at + 1) * height] = value
    err = cot_ref[at * height : (at + 1) * height].astype(F32)
    vec_ref[0:1, :] = jnp.sum(err * xhat, axis=0, keepdims=True)
    vec_ref[1:2, :] = jnp.sum(err, axis=0, keepdims=True)
    scaled = err * gain
    mean_a = jnp.mean(scaled, axis=-1, keepdims=True)
    mean_b = jnp.mean(scaled * xhat, axis=-1, keepdims=True)
    d_two = rstd * (scaled - mean_a - xhat * mean_b)
    d_two_ref[...] = d_two
    vec_ref[2:3, :] = jnp.sum(d_two, axis=0, keepdims=True)
    low = d_two.astype(BF16)
    d_low_ref[...] = low
    units = win_ref.shape[1]
    step = units // 3
    dn_ref[...] = jnp.zeros_like(dn_ref)

    @pl.loop(0, 3)
    def _(part):
        cols = pl.ds(pl.multiple_of(part * step, step), step)
        d_act = dot_nt(low, wdown_ref[cols, :])
        d_inner = (d_act * slope_ref[:, cols]).astype(BF16)
        d_inner_ref[:, cols] = d_inner
        bin_ref[0:1, cols] = jnp.sum(d_inner.astype(F32), axis=0, keepdims=True)
        dn_ref[...] += dot_nt(d_inner, win_ref[:, cols])


def feed_back(
    line, at, height, rows, before, low_own, low_other, xhat, gain_one, shift_one, bdown, gain,
    shift, cot, slope, win, wdown,
):
    width = cot.shape[1]
    units = win.shape[1]
    last = (at + 1) * height == cot.shape[0]
    before = before if last else []
    outs = [
        sds(cot.shape if last else (height, width), BF16),
        sds((height, width), F32),
        sds((height, width), BF16),
        sds((height, units), BF16),
        sds((8, width), F32),
        sds((8, units), F32),
    ]
    outs += [sds((rows, width), F32)] * (height // rows)
    operands = (
        low_own, low_other, xhat, gain_one, shift_one, bdown, gain, shift, cot, slope, win, wdown,
        *before,
    )
    return line.call(
        functools.partial(feed_back_kernel, at, height, len(before)), f"feed_back_{at}", outs,
        operands, direct=(0,) if last else (),
    )


def spread(order, me, total, kept_ref, sent_refs, cols):
    parts = 1 << len(order)
    height = total.shape[0] // parts
    for bit in (0, order[0]):

        @pl.when((me & order[0]) == bit)
        def _(bit=bit):
            for block in range(parts):
                origin = me ^ block
                place = 0
                for later in order[1:]:
                    place = 2 * place + ((origin >> (later.bit_length() - 1)) & 1)
                top = block * height
                if block & order[0] == bit:
                    kept_ref[place, :, cols] = total[top : top + height]
                else:
                    for ref in sent_refs:
                        ref[place, :, cols] = total[top : top + ref.shape[1]]
                        top += ref.shape[1]


def grad_kernel(order, groups, pieces, *refs):
    kept_ref, *sent_refs = refs[-1 - pieces :]
    me = lax.axis_index("dp")
    at, start = 0, 0
    for count in groups:
        terms = []
        for rights in count:
            terms.append((refs[at], refs[at + 1 : at + 1 + rights]))
            at += 1 + rights
        width = terms[0][1][0].shape[1]

        def part(index, terms=terms, start=start):
            total = None
            columns = pl.ds(pl.multiple_of(index * COLUMNS, COLUMNS), COLUMNS)
            for left_ref, right_refs in terms:
                right = jnp.concatenate([ref[:, columns] for ref in right_refs], axis=0)
                term = dot_tn(left_ref[...], right.astype(BF16))
                total = term if total is None else total + term
            target = pl.ds(pl.multiple_of(start + index * COLUMNS, COLUMNS), COLUMNS)
            spread(order, me, total, kept_ref, sent_refs, target)

        pl.loop(0, width // COLUMNS)(part)
        start += width


def halves(order, rows, cols, pieces):
    half, height = (1 << len(order)) // 2, rows >> len(order)
    return [sds((half, height, cols), F32)] + [sds((half, height // pieces, cols), F32)] * pieces


def grad_blocks(line, name, order, groups, pieces=1):
    width = groups[0][0][0].shape[1]
    cols = sum(group[0][1][0].shape[1] for group in groups)
    operands = [array for group in groups for left, right in group for array in (left, *right)]
    counts = [[len(right) for _, right in group] for group in groups]
    outs = halves(order, width, cols, pieces)
    return line.call(
        functools.partial(grad_kernel, order, counts, pieces), name, outs, operands,
        flops=GRAD_FLOPS,
    )


def rel_kernel(
    order, counts, table_rows, bucket_ref, deq_ref, dek_ref, wq_ref, wk_ref, dk_ref, dv_ref,
    *refs,
):
    groups = []
    for count in counts:
        groups.append(refs[:count])
        refs = refs[count:]
    dq_refs, one_refs, two_refs, unit_refs = groups
    relq_ref, relk_ref, kept_ref, *sent_refs, pack_ref = refs
    onehot = onehot_of(bucket_ref, table_rows)
    deq, dek = deq_ref[...], dek_ref[...]
    cols = deq.shape[1]
    d_rel = dot_nn(onehot, jnp.concatenate([deq, dek], axis=1).astype(BF16)).astype(BF16)
    relq_ref[...] = d_rel[:, :cols]
    relk_ref[...] = d_rel[:, cols:]
    total = dot_nt(d_rel, jnp.concatenate([wq_ref[...], wk_ref[...]], axis=1))
    width = total.shape[1]
    me = lax.axis_index("dp")
    spread(order, me, total, kept_ref, sent_refs, slice(0, width))

    def summed(value):
        return jnp.sum(value.astype(F32), axis=0, keepdims=True)

    def over(stream_refs):
        value = stream_refs[0][...]
        for ref in stream_refs[1:]:
            value = value + ref[...]
        return value

    one, two, unit = over(one_refs), over(two_refs), over(unit_refs)
    d_bias = summed(dq_refs[0][...])
    for ref in dq_refs[1:]:
        d_bias = d_bias + summed(ref[...])
    vectors = [
        d_bias + summed(deq),
        summed(dk_ref[...]) + summed(dek),
        summed(dv_ref[...]),
        one[2:3], one[0:1], one[1:2], unit[0:1], two[2:3], two[0:1], two[1:2],
    ]
    pack_ref[...] = jnp.zeros_like(pack_ref)
    row = 0
    for vector in vectors:
        for piece in range(vector.shape[1] // LANES):
            pack_ref[row : row + 1, :] = vector[:, piece * LANES : (piece + 1) * LANES]
            row += 1
    spread(order, me, pack_ref[...], kept_ref, sent_refs, slice(width, width + LANES))


def rel_grads(line, order, span, buckets, deq, dek, wq, wk, dk, dv, dq, one, two, unit):
    width, cols = wq.shape
    outs = [sds((span, cols), BF16)] * 2
    outs = outs + halves(order, span, width + LANES, REL_PIECES)
    operands = [buckets, deq, dek, wq, wk, dk, dv, *dq, *one, *two, *unit]
    return line.call(
        functools.partial(rel_kernel, order, [len(g) for g in (dq, one, two, unit)], span), "rel_grads", outs, operands,
        scratch=[pltpu.VMEM((span, LANES), F32)],
    )


def rel_split_kernel(own_ref, other_ref, table_ref, vector_ref):
    width = table_ref.shape[2]
    for at in range(2):
        total = own_ref[at] + other_ref[1 - at]
        table_ref[at] = total[:, :width]
        vector_ref[at] = total[:, width:]


def rel_split(own, other):
    count, rows, wide = own.shape
    outs = [sds((count, rows, wide - LANES), F32), sds((count, rows, LANES), F32)]
    return rel_split_kernel, "rel_split", outs, [own, other], ()


def rel_join_kernel(own_ref, other_ref, vector_ref, out_ref):
    width = own_ref.shape[2]
    out_ref[:, :, :width] = own_ref[...] + other_ref[...]
    out_ref[:, :, width:] = vector_ref[...]


def rel_join(own, other, vector):
    count, rows, width = own.shape
    outs = [sds((count, rows, width + vector.shape[2]), F32)]
    return rel_join_kernel, "rel_join", outs, [own, other, vector], ()


def hidden_join_kernel(own_ref, other_ref, *refs):
    out_ref = refs[-1]
    start = 0
    for ref in refs[:-1]:
        rows = slice(start, start + ref.shape[0])
        out_ref[rows] = ((own_ref[rows] + other_ref[rows]) + ref[...]).astype(BF16)
        start += ref.shape[0]


def hidden_join(own, other, d_one):
    outs = [sds(own.shape, BF16)]
    return hidden_join_kernel, "hidden_join", outs, [own, other, *d_one], (0,)


def unpack_kernel(origins, count, *refs):
    shared_refs, (table_ref, *vector_refs) = refs[:count], refs[count:]
    width = table_ref.shape[2]
    height = table_ref.shape[1]
    me = lax.axis_index("dp")
    places = [(ref, at) for ref in shared_refs for at in range(ref.shape[0])]
    rows = sum(ref.shape[0] for ref in vector_refs) // LANES
    lines = [
        (ref, piece) for ref in vector_refs for piece in range(ref.shape[0] // LANES)
    ]
    for (shared_ref, at), origin in zip(places, origins, strict=True):
        table_ref[me ^ origin] = shared_ref[at, :, :width]
        for block in range((rows + height - 1) // height):

            @pl.when(me ^ origin == block)
            def _(shared_ref=shared_ref, at=at, block=block):
                for row in range(block * height, min(rows, (block + 1) * height)):
                    ref, piece = lines[row]
                    inner = row % height
                    line = shared_ref[at, inner : inner + 1, width:]
                    ref[pl.ds(piece * LANES, LANES)] = line.reshape(LANES)


def unpack(origins, pieces, sizes):
    height, wide = pieces[0].shape[1:]
    outs = [sds((len(origins), height, wide - LANES), F32)] + [sds((size,), F32) for size in sizes]
    kernel = functools.partial(unpack_kernel, origins, len(pieces))
    return kernel, "unpack", outs, list(pieces), range(len(outs))


def hidden_kernel(dk_ref, dv_ref, wq_ref, wk_ref, wv_ref, *refs):
    out_ref = refs[-1]
    out_ref[...] = dot_nt(dk_ref[...], wk_ref[...]) + dot_nt(dv_ref[...], wv_ref[...])
    start = 0
    for ref in refs[:-1]:
        out_ref[start : start + ref.shape[0]] += dot_nt(ref[...], wq_ref[...])
        start += ref.shape[0]


def hidden_grad(line, dk, dv, wq, wk, wv, dq):
    out = sds((dk.shape[0], wq.shape[0]), F32)
    (total,) = line.call(
        hidden_kernel, "hidden_grad", [out], (dk, dv, wq, wk, wv, *dq)
    )
    return total


def bits_of(parts):
    return [1 << b for b in range(parts.bit_length() - 1)]


def swap_head(value):
    return lax.ppermute(value, "head", [(0, 1), (1, 0)])


def flip(value, parts, bit):
    return lax.ppermute(value, "dp", [(i, i ^ bit) for i in range(parts)])


def together(*values):
    return lax.optimization_barrier(values)


def step_kernel(kept_ref, *refs):
    *arrived_refs, kept_out, sent_out = refs
    half = kept_out.shape[0]
    top = 0
    for ref in arrived_refs:
        rows = slice(top, top + ref.shape[1])
        kept_out[:, rows] = kept_ref[:half, rows] + ref[:half]
        sent_out[:, rows] = kept_ref[half:, rows] + ref[half:]
        top += ref.shape[1]


class Scatter:
    def __init__(self, line, name, kept, *sent, order):
        self.line, self.name, self.order = line, name, list(order)
        self.parts = 1 << len(self.order)
        self.kept = kept
        self.send(sent)

    def send(self, sent):
        self.bit = self.order.pop(0)
        self.arrived = [flip(piece, self.parts, self.bit) for piece in sent]

    def step(self):
        shape = (self.kept.shape[0] // 2, *self.kept.shape[1:])
        self.kept, sent = yield (
            step_kernel, f"{self.name}_{self.bit}", [sds(shape, F32)] * 2,
            [self.kept, *self.arrived], (),
        )
        self.send([sent])

    def rest(self, left=0):
        while len(self.order) > left:
            self.line.group([self.step()])

    def exchange(self):
        def add(kept_ref, arrived_ref, out_ref):
            out_ref[...] = kept_ref[...] + arrived_ref[...]

        self.rest(1)
        outs = [sds(self.kept.shape, F32)]
        (self.both,) = yield add, f"{self.name}_{self.bit}", outs, [self.kept, *self.arrived], ()
        bit = self.order.pop(0)
        self.both_other, self.origins = flip(self.both, self.parts, bit), [0, bit]

    def finish(self, widths):
        def kernel(kept_ref, arrived_ref, *out_refs):
            start = 0
            for ref in out_refs:
                cols = slice(start, start + ref.shape[1])
                ref[...] = kept_ref[0, :, cols] + arrived_ref[0, :, cols]
                start += ref.shape[1]

        self.rest()
        outs = [sds((self.kept.shape[1], width), F32) for width in widths]
        operands = [self.kept, *self.arrived]
        self.sums = yield kernel, f"{self.name}_sum", outs, operands, range(len(outs))


def pack_kernel(*refs):
    start = 0
    for ref in refs[:-1]:
        refs[-1][start : start + ref.shape[0]] = ref[...]
        start += ref.shape[0]


class Gather:
    def __init__(self, line, value, origins, parts, order):
        self.line, self.parts, self.order = line, parts, list(order)
        self.pieces, self.origins = [value], origins
        self.send(value)

    def send(self, sent):
        bit = self.order.pop(0)
        self.pieces.append(flip(sent, self.parts, bit))
        self.origins = self.origins + [origin ^ bit for origin in self.origins]

    def step(self):
        shape = (len(self.origins), *self.pieces[0].shape[1:])
        name = f"pack_{len(self.origins)}"
        (sent,) = yield pack_kernel, name, [sds(shape, F32)], list(self.pieces), ()
        self.send(sent)

    def rest(self):
        while self.order:
            self.line.group([self.step()])


def words_of(text):
    words, open_word = [], None
    for letter in text:
        if letter == "(":
            open_word = ""
        elif letter == ")":
            words.append(open_word)
            open_word = None
        elif open_word is not None:
            open_word += letter
        else:
            words.append(letter)
    return words


def on_device(parts, *arguments):
    (
        hidden_in, lengths, cotangent, w_query, b_query, w_key, b_key, w_value, b_value,
        w_out, b_out, ln1_gain, ln1_bias, w_in, b_in, w_down, b_down, ln2_gain, ln2_bias,
        rel_table,
    ) = arguments
    seq_len, width = hidden_in.shape
    height = seq_len // STREAMS
    streams = range(STREAMS)
    bits = bits_of(parts)

    buckets = jnp.asarray(distance_buckets(seq_len)[None, :])
    line = Line()
    q, k, v, eq, ek, mine = project(
        line, buckets, hidden_in, w_query, b_query, w_key, b_key, w_value, b_value, rel_table,
        w_out,
    )
    fetched = swap_head(mine)
    contexts, attends = [], []
    for at in range(CONTEXTS * STREAMS):
        context, attended = attend(line, at, height // CONTEXTS, lengths, q, k, v, eq, ek)
        contexts.append(context)
        attends.append(attended)
    fetched, contexts[0] = together(fetched, contexts[0])
    quarters = [fetched, flip(fetched, parts, 1), flip(fetched, parts, 2)]
    quarters.append(flip(quarters[2], parts, 1))
    w_out_all = assemble(line, w_out, quarters)
    others = [swap_head(context) for context in contexts]
    of_stream = [slice(CONTEXTS * at, CONTEXTS * (at + 1)) for at in streams]
    fed = [
        feed(
            line, at, height, contexts[of_stream[at]], others[of_stream[at]],
            w_out_all, b_out, hidden_in, ln1_gain, ln1_bias, w_in, b_in, w_down,
        )
        for at in streams
    ]
    backs = []
    for at in streams:
        xhat, rstd, normed, act, slope, lowered = fed[at]
        backs.append(
            feed_back(
                line, at, height, height, [b[0] for b in backs], lowered, swap_head(lowered), xhat,
                ln1_gain, ln1_bias, b_down, ln2_gain, ln2_bias, cotangent, slope, w_in, w_down,
            )
        )
    output = backs[-1][0]
    crossed = bits[:1] + bits[2:] + bits[1:2]
    g_down = grad_blocks(
        line, "grad_down", bits, [[(backs[at][2], fed[at][3:4]) for at in streams]]
    )
    down = Scatter(line, "down", *g_down, order=bits)
    g_in = grad_blocks(
        line, "grad_in", crossed, [[(fed[at][2], backs[at][3:4]) for at in streams]]
    )
    inner = Scatter(line, "inner", *g_in, order=crossed)
    norms, dq = [], []
    carried = ()
    for at in streams:
        xhat, rstd = fed[at][:2]
        d_two, dn = backs[at][1], backs[at][6]
        norms.append(
            norm_back(line, at, 0, dn, swap_head(dn), d_two, xhat, rstd, ln1_gain, w_out)
        )
        if at == 0:
            line.group([down.step()])
            line.group([inner.step()])
        d_q, *carried = attend_back(
            line, at, height, at == streams[-1], norms[at][2], q, k, v, eq, ek,
            attends[of_stream[at]], carried,
        )
        dq.append(d_q)
    deq, dek, dk, dv = carried[2:]
    cols = q.shape[1]
    hidden_parts = [hidden_in[at * height : (at + 1) * height] for at in streams]
    chains = {"d": down, "i": inner}
    made = {}

    def start_rel():
        made["relq"], made["relk"], *blocks = rel_grads(
            line, bits, rel_table.shape[0], buckets, deq, dek, w_query, w_key, dk, dv, dq,
            [n[3] for n in norms], [b[4] for b in backs], [b[5] for b in backs],
        )
        chains["r"] = Scatter(line, "rel", *blocks, order=bits)

    def start_value_out():
        blocks = grad_blocks(
            line, "grad_value_out", bits,
            [
                [(hidden_in, [dv])],
                [(norms[at][1], contexts[of_stream[at]]) for at in streams],
            ],
            HEAD_PIECES,
        )
        chains["v"] = Scatter(line, "value_out", *blocks, order=bits)

    def start_query_key():
        blocks = grad_blocks(
            line, "grad_query_key", bits,
            [
                [*zip(hidden_parts, [[d] for d in dq], strict=True), (rel_table, [made["relq"]])],
                [(hidden_in, [dk]), (rel_table, [made["relk"]])],
            ],
            HEAD_PIECES,
        )
        chains["q"] = Scatter(line, "query_key", *blocks, order=bits)

    def start_hidden():
        made["hidden"] = hidden_grad(line, dk, dv, w_query, w_key, w_value, dq)
        made["hidden_other"] = swap_head(made["hidden"])

    def swap_rel():
        both, other = chains["r"].both, chains["r"].both_other
        made["own"], made["vectors"] = yield rel_split(both, other)
        made["own_other"] = swap_head(made["own"])

    def gather_rel():
        (joined,) = yield rel_join(made["own"], made["own_other"], made["vectors"])
        chains["p"] = Gather(line, joined, chains["r"].origins, parts, bits[-2::-1])

    def end_hidden():
        d_one = [n[0] for n in norms]
        made["grad_input"] = yield hidden_join(made["hidden"], made["hidden_other"], d_one)

    def end_rel():
        chains["p"].rest()
        sizes = [cols] * 3 + [width] * 3 + [w_in.shape[1]] + [width] * 3
        made["shared"] = yield unpack(chains["p"].origins, chains["p"].pieces, sizes)

    starters = {
        "L": start_rel, "G": start_value_out, "K": start_query_key, "Y": start_hidden,
    }
    steps = {
        "X": lambda: chains["r"].exchange(), "S": swap_rel, "J": gather_rel, "H": end_hidden,
        "U": end_rel,
    }
    widths = {"d": [w_in.shape[1]], "i": [w_in.shape[1]], "v": [cols, cols], "q": [cols, cols]}

    def work(letter):
        if letter in widths:
            return chains[letter].finish(widths[letter])
        return steps[letter]() if letter in steps else chains[letter.lower()].step()

    for word in words_of(TAIL):
        if word in starters:
            starters[word]()
        else:
            line.group([work(letter) for letter in word])
    (s_down,), (s_in,) = chains["d"].sums, chains["i"].sums
    (s_q, s_k), (s_v, s_out) = chains["q"].sums, chains["v"].sums
    (grad_input,) = made["grad_input"]
    table_blocks, *pieces = made["shared"]
    grad_rel_table = table_blocks.reshape(rel_table.shape)
    (
        grad_b_query, grad_b_key, grad_b_value, grad_b_out, grad_ln1_gain, grad_ln1_bias,
        grad_b_in, grad_b_down, grad_ln2_gain, grad_ln2_bias,
    ) = pieces
    return (
        output, grad_input, s_q, grad_b_query, s_k, grad_b_key, s_v, grad_b_value,
        s_out.T, grad_b_out, grad_ln1_gain, grad_ln1_bias, s_in, grad_b_in,
        s_down.T, grad_b_down, grad_ln2_gain, grad_ln2_bias, grad_rel_table,
    )


def solution(mesh):
    parts = mesh.shape["dp"]
    return jax.shard_map(
        functools.partial(on_device, parts),
        mesh=mesh,
        in_specs=(
            P("dp", None), P("dp"), P("dp", None),
            P(None, "head"), P("head"), P(None, "head"), P("head"), P(None, "head"), P("head"),
            P("head", None), P(), P(), P(),
            P(None, "head"), P("head"), P("head", None), P(), P(), P(), P(),
        ),
        out_specs=(
            P("dp", None), P("dp", None),
            P("dp", "head"), P("head"), P("dp", "head"), P("head"), P("dp", "head"), P("head"),
            P("head", "dp"), P(), P(), P(),
            P("dp", "head"), P("head"), P("head", "dp"), P(), P(), P(), P(),
        ),
        check_vma=False,
    )
```
